32 devices in a mesh: dp: 8 (over y, x, core), seq: 4 (over z).
Axes of the slice: x: 2, y: 2, z: 4, core: 2. Of those that a mesh axis runs over, the one named last changes fastest.
Arguments:
- tokens: bfloat16 [16, 512, 2048], P('dp', 'seq'), may hold values from -6 to 6
- cotangent: bfloat16 [16, 512, 2048], P('dp', 'seq'), may hold values from -6 to 6
- attention_base: bfloat16 [4, 2048, 2048], P(None, ('dp', 'seq')), may hold values from -0.125 to 0.125
- expand_base: bfloat16 [2, 2048, 5632], P(None, ('dp', 'seq')), may hold values from -0.125 to 0.125
- contract_base: bfloat16 [5632, 2048], P(None, ('dp', 'seq')), may hold values from -0.078125 to 0.078125
- attention_down: float32 [4, 2048, 16], replicated, may hold values from -0.125 to 0.125
- attention_up: float32 [4, 16, 2048], replicated, may hold values from -0.15 to 0.15
- attention_magnitude: float32 [4, 2048], replicated, may hold values from 0.5 to 24
- expand_down: float32 [2, 2048, 16], replicated, may hold values from -0.125 to 0.125
- expand_up: float32 [2, 16, 5632], replicated, may hold values from -0.15 to 0.15
- expand_magnitude: float32 [2, 5632], replicated, may hold values from 0.5 to 1.5
- contract_down: float32 [5632, 16], replicated, may hold values from -0.078125 to 0.078125
- contract_up: float32 [16, 2048], replicated, may hold values from -0.15 to 0.15
- contract_magnitude: float32 [2048], replicated, may hold values from 0.5 to 1.5
- prompt_length: int32 [16], P('dp'), may hold values from 64 to 256, as said below
- response_length: int32 [16], P('dp'), may hold values from 128 to 256
Outputs:
- layer_output: bfloat16 [16, 512, 2048], P('dp', 'seq')
- tokens_grad: float32 [16, 512, 2048], P('dp', 'seq')
- attention_down_grad: float32 [4, 2048, 16], replicated
- attention_up_grad: float32 [4, 16, 2048], replicated
- attention_magnitude_grad: float32 [4, 2048], replicated
- expand_down_grad: float32 [2, 2048, 16], replicated
- expand_up_grad: float32 [2, 16, 5632], replicated
- expand_magnitude_grad: float32 [2, 5632], replicated
- contract_down_grad: float32 [5632, 16], replicated
- contract_up_grad: float32 [16, 2048], replicated
- contract_magnitude_grad: float32 [2048], replicated
The draws below stay inside these ranges and needn't reach their ends.
Inputs may be any that keep to these rules, and one draw needn't show every extreme that they name: `prompt_length`: rows 2i and 2i+1 form a pair with the same prompt length.
All inputs are finite; a program needn't handle non-finite values.
Results may differ from the reference program's by a relative error of at most 0.025.
Values may be sent and summed in bfloat16 or wider, within the bound.
No kernel may reach another device: no remote copies, remote signals or barrier semaphores. Data moves between devices by JAX's collectives and lax.ppermute only.
A program may use at most 320 MiB of HBM per device.

```python
import jax
import jax.numpy as jnp
from jax import lax

D = 2048
HEADS = 16
HEAD_DIM = 128
FF = 5632
RANK = 16
ROWS = 16
LENGTH = 512


def forced_ends(key, count, smallest, largest):
    drawn = jax.random.randint(jax.random.fold_in(key, 11), (count,), smallest, largest + 1)
    shuffled = jax.random.permutation(jax.random.fold_in(key, 12), count)
    return jnp.where(shuffled == 0, largest, jnp.where(shuffled == 1, smallest, drawn)).astype(jnp.int32)


def draw_prompt_length(key, part):
    return jnp.repeat(forced_ends(key, ROWS // 2, LENGTH // 8, LENGTH // 2), 2).astype(jnp.int32)


def draw_response_length(key, part):
    return forced_ends(key, ROWS, LENGTH // 4, LENGTH // 2)


def draw_attention_magnitude(key, part):
    inner = jax.random.uniform(jax.random.fold_in(key, 21), (3, D), jnp.float32, 0.5, 1.5)
    outer = jax.random.uniform(jax.random.fold_in(key, 22), (1, D), jnp.float32, 8.0, 24.0)
    return jnp.concatenate([inner, outer], axis=0)


def block_scale(rng, shape, cuts, low, high):
    def one(position, blocks):
        heights = jax.random.uniform(jax.random.fold_in(jax.random.fold_in(rng, 6), position), (blocks,), jnp.float32, low / len(cuts), high / len(cuts))
        return jnp.repeat(jnp.exp(heights), shape[position] // blocks).reshape((-1,) + (1,) * (len(shape) - position - 1))

    factor_of = one(*cuts[0])
    for cut in cuts[1:]:
        factor_of = factor_of * one(*cut)
    return factor_of


def scatter_about(stream_key, shape, deviation, most, shards=(), held_as=jnp.bfloat16):
    values = deviation * jax.random.normal(stream_key, shape, jnp.float32)
    if shards:
        values = values * block_scale(stream_key, shape, shards, -0.22, 0.18)
    return jnp.clip(values, -most, most).astype(held_as)


def setup_inputs(seed: int = 0) -> dict:
    streams_of = jax.random.split(jax.random.key(seed), 17)
    return {
        "tokens": scatter_about(streams_of[0], (ROWS, LENGTH, D), 1.0, 6.0, ((0, 8), (1, 4))),
        "cotangent": scatter_about(streams_of[1], (ROWS, LENGTH, D), 1.0, 6.0, ((0, 8), (1, 4))),
        "attention_base": scatter_about(streams_of[2], (4, D, D), D ** -0.5, 0.125, ((1, 32),)),
        "expand_base": scatter_about(streams_of[3], (2, D, FF), D ** -0.5, 0.125, ((1, 32),)),
        "contract_base": scatter_about(streams_of[4], (FF, D), FF ** -0.5, 0.078125, ((1, 32),)),
        "attention_down": scatter_about(streams_of[5], (4, D, RANK), D ** -0.5, 0.125, (), jnp.float32),
        "attention_up": scatter_about(streams_of[6], (4, RANK, D), 0.025, 0.15, (), jnp.float32),
        "attention_magnitude": draw_attention_magnitude(jax.random.fold_in(streams_of[16], 71), 0),
        "expand_down": scatter_about(streams_of[8], (2, D, RANK), D ** -0.5, 0.125, (), jnp.float32),
        "expand_up": scatter_about(streams_of[9], (2, RANK, FF), 0.025, 0.15, (), jnp.float32),
        "expand_magnitude": jnp.clip(jax.random.uniform(streams_of[10], (2, FF), jnp.float32, 0.5, 1.5), 0.5, 1.5),
        "contract_down": scatter_about(streams_of[11], (FF, RANK), FF ** -0.5, 0.078125, (), jnp.float32),
        "contract_up": scatter_about(streams_of[12], (RANK, D), 0.025, 0.15, (), jnp.float32),
        "contract_magnitude": jnp.clip(jax.random.uniform(streams_of[13], (D,), jnp.float32, 0.5, 1.5), 0.5, 1.5),
        "prompt_length": draw_prompt_length(jax.random.fold_in(streams_of[16], 71), 0),
        "response_length": draw_response_length(jax.random.fold_in(streams_of[16], 71), 0),
    }


@jax.custom_vjp
def low(v):
    return lax.optimization_barrier(v.astype(jnp.bfloat16)).astype(jnp.float32)

@jax.custom_vjp
def low_back(v):
    return v

def low_keep(v):
    return (low(v), None)

def low_pass(kept, grad):
    return (grad,)

def back_keep(v):
    return (v, None)

def back_low(kept, grad):
    return (low(grad),)
low.defvjp(low_keep, low_pass)
low_back.defvjp(back_keep, back_low)
adapter_scale = 2.0
highest_precision = lax.Precision.HIGHEST

def rms_norm(values):
    return values * lax.rsqrt(lax.optimization_barrier(jnp.mean(values * values, axis=-1, keepdims=True)) + 1e-05)

def rotary(values, positions):
    head_half = HEAD_DIM // 2
    frequency = 10000.0 ** (-jnp.arange(head_half).astype(jnp.float32) / head_half)
    angles = positions[:, None] * frequency[None, :]
    cosine = jnp.cos(angles)[None, :, None, :]
    sine = jnp.sin(angles)[None, :, None, :]
    shaped = values.reshape(values.shape[0], values.shape[1], HEADS, 2, head_half)
    former = shaped[:, :, :, 0]
    latter = shaped[:, :, :, 1]
    turned = jnp.stack([former * cosine - latter * sine, latter * cosine + former * sine], axis=3)
    return turned.reshape(values.shape)

def weight_decomposed_adapter(input_rows, frozen_weight, adapter_down_weight, adapter_up_weight, magnitude_vector):
    merged_weight = frozen_weight + adapter_scale * jnp.dot(adapter_down_weight, adapter_up_weight, precision=highest_precision)
    per_column_norm = jnp.sqrt(lax.optimization_barrier(jnp.sum(merged_weight * merged_weight, axis=0)))
    frozen_product = low_back(jnp.dot(input_rows, frozen_weight, precision=highest_precision))
    adapter_product = jnp.dot(jnp.dot(input_rows, adapter_down_weight, precision=highest_precision), adapter_up_weight, precision=highest_precision)
    return (frozen_product + adapter_scale * adapter_product) * (magnitude_vector / per_column_norm)

def attend_row(row_data):
    queries, key_rows, value_rows, row_total = row_data
    block_rows = min(512, LENGTH)
    query_heads = queries.reshape(LENGTH, HEADS, HEAD_DIM)
    key_heads = key_rows.reshape(LENGTH, HEADS, HEAD_DIM)
    value_heads = value_rows.reshape(LENGTH, HEADS, HEAD_DIM)
    key_place = jnp.arange(LENGTH).astype(jnp.int32)

    def score_block(block_start):
        query_block = lax.dynamic_slice_in_dim(query_heads, block_start, block_rows, 0)
        raw_scores = jnp.einsum('qhd,khd->hqk', query_block, key_heads, precision=highest_precision)
        query_place = block_start + jnp.arange(block_rows).astype(jnp.int32)
        allowed = (key_place[None, :] <= query_place[:, None]) & (key_place[None, :] < row_total)
        scores = jnp.where(allowed[None], low_back(raw_scores) * HEAD_DIM ** (-0.5), -1e+30)
        row_peak = lax.optimization_barrier(jnp.max(scores, axis=-1, keepdims=True))
        weights = jnp.exp(scores - row_peak)
        shares = weights / lax.optimization_barrier(jnp.sum(weights, axis=-1, keepdims=True))
        mixed_rows = jnp.einsum('hqk,khd->qhd', low(shares), value_heads, precision=highest_precision)
        return mixed_rows.reshape(block_rows, HEADS * HEAD_DIM)
    starts = (jnp.arange(LENGTH // block_rows) * block_rows).astype(jnp.int32)
    return lax.map(jax.checkpoint(score_block), starts).reshape(LENGTH, HEADS * HEAD_DIM)

def reference(tokens, cotangent, attention_base, expand_base, contract_base, attention_down, attention_up, attention_magnitude, expand_down, expand_up, expand_magnitude, contract_down, contract_up, contract_magnitude, prompt_length, response_length):
    totals = (prompt_length + response_length).astype(jnp.int32)
    positions = jnp.arange(LENGTH).astype(jnp.float32)
    attention_float = attention_base.astype(jnp.float32)
    expand_float = expand_base.astype(jnp.float32)
    contract_float = contract_base.astype(jnp.float32)

    def forward(flat_tokens, adapters):
        normed = low(rms_norm(flat_tokens))
        projected = [weight_decomposed_adapter(normed, attention_float[member], adapters[0][member], adapters[1][member], adapters[2][member]) for member in range(3)]
        queries = low(rotary(projected[0].reshape(ROWS, LENGTH, D), positions))
        key_rows = low(rotary(projected[1].reshape(ROWS, LENGTH, D), positions))
        value_rows = low(projected[2].reshape(ROWS, LENGTH, D))
        attended = lax.map(attend_row, (queries, key_rows, value_rows, totals))
        gathered = low(low_back(attended.reshape(ROWS * LENGTH, D)))
        middle = flat_tokens + weight_decomposed_adapter(gathered, attention_float[3], adapters[0][3], adapters[1][3], adapters[2][3])
        second = low(rms_norm(middle))
        gate_value = weight_decomposed_adapter(second, expand_float[0], adapters[3][0], adapters[4][0], adapters[5][0])
        up_value = weight_decomposed_adapter(second, expand_float[1], adapters[3][1], adapters[4][1], adapters[5][1])
        hidden = low(gate_value / (1.0 + jnp.exp(-gate_value)) * up_value)
        return middle + weight_decomposed_adapter(hidden, contract_float, adapters[6], adapters[7], adapters[8])
    flat_tokens = tokens.reshape(ROWS * LENGTH, D).astype(jnp.float32)
    adapters = (attention_down, attention_up, attention_magnitude, expand_down, expand_up, expand_magnitude, contract_down, contract_up, contract_magnitude)
    result, pullback = jax.vjp(forward, flat_tokens, adapters)
    grad_flat, grad_adapters = pullback(cotangent.reshape(ROWS * LENGTH, D).astype(jnp.float32))
    return (result.reshape(ROWS, LENGTH, D).astype(jnp.bfloat16), grad_flat.reshape(ROWS, LENGTH, D), grad_adapters[0], grad_adapters[1], grad_adapters[2], grad_adapters[3], grad_adapters[4], grad_adapters[5], grad_adapters[6], grad_adapters[7], grad_adapters[8])
```

```python
import functools

import jax
import jax.numpy as jnp
from jax import lax
from jax.experimental import pallas as pl
from jax.experimental.pallas import tpu as pltpu
from jax.sharding import Mesh
from jax.sharding import PartitionSpec as P

HEAD_DIM = 128
SCALE = 2.0
BF = jnp.bfloat16
F32 = jnp.float32
ALL = ("yy", "xx", "core", "seq")
WORD = 512


def mm(a, b, dims=((1,), (0,))):
    return lax.dot_general(a, b, (dims, ((), ())), preferred_element_type=F32)


def nt(a, b):
    return mm(a, b, ((1,), (1,)))


def tn(a, b):
    return mm(a, b, ((0,), (0,)))


def take(a, index, axis):
    return lax.dynamic_index_in_dim(a, index, axis, keepdims=False)


def swap(a, name):
    return lax.ppermute(a, name, [(0, 1), (1, 0)])


def shift(a, name, step):
    size = lax.axis_size(name)
    return lax.ppermute(a, name, [(i, (i + step) % size) for i in range(size)])


def pair(mine, other, index, axis=0):
    first = jnp.where(index == 0, mine, other)
    second = jnp.where(index == 0, other, mine)
    return jnp.stack([first, second], axis=axis)


def put(buffer, block, index, axis):
    return lax.dynamic_update_slice_in_dim(buffer, jnp.expand_dims(block, axis), index, axis)


def rms(v):
    return v * lax.rsqrt(jnp.mean(v * v, axis=-1, keepdims=True) + 1e-05)


def rms_back(v, grad):
    inverse = lax.rsqrt(jnp.mean(v * v, axis=-1, keepdims=True) + 1e-05)
    inner = jnp.mean(v * grad, axis=-1, keepdims=True)
    return grad * inverse - v * (inner * inverse * inverse * inverse)


def merged(base, down, up):
    product = lax.dot_general(
        down, up, (((down.ndim - 1,), (up.ndim - 2,)), (tuple(range(down.ndim - 2)),) * 2),
        precision=lax.Precision.HIGHEST, preferred_element_type=F32,
    )
    return (base.astype(F32) + SCALE * product).astype(BF)


class Box:
    def __init__(self, arrays):
        self.arrays = list(arrays)


class Links:
    def __init__(self, depth):
        self.depth = depth
        self.sent = {}

    def hold(self, link, arrays):
        history = self.sent.setdefault(link, [])
        if len(history) >= self.depth:
            old = history[-self.depth]
            both = lax.optimization_barrier((list(arrays), old.arrays))
            arrays, old.arrays = both[0], both[1]
        return arrays

    def send(self, link, box, move):
        box.arrays = list(self.hold(link, box.arrays))
        result = Box([move(a) for a in box.arrays])
        self.sent[link].append(result)
        return result


class Gathered:
    def __init__(self, over_x):
        self.over_x = over_x
        self.blocks = []

    def add(self, box, turn, far, step):
        self.blocks.append((box, turn, far, step))

    def build(self, index):
        y, x, z = lax.axis_index("yy"), lax.axis_index("xx"), lax.axis_index("seq")
        ny, count = lax.axis_size("yy"), lax.axis_size("seq")
        piece = self.blocks[0][0].arrays[index]
        lead = piece.ndim - 2
        shape = (ny,) + ((2,) if self.over_x else ()) + piece.shape[:lead] + (count,) + piece.shape[lead:]
        buffer = jnp.zeros(shape, piece.dtype)
        for box, turn, far, step in self.blocks:
            block = jnp.expand_dims(box.arrays[index], lead)[None]
            start = [(y - turn) % ny]
            if self.over_x:
                block = block[None]
                start.append(1 - x if far else x)
            start += [0] * lead + [(z - step) % count, 0, 0]
            buffer = lax.dynamic_update_slice(buffer, block, [jnp.int32(s) for s in start])
        return buffer


def turned(v, cosine, sine):
    return v * cosine + pltpu.roll(v, HEAD_DIM // 2, 1) * sine


def qkv_kernel(rotated, h_ref, v_ref, m_ref, cos_ref, sin_ref, t_ref, p_ref, n_ref):
    block = v_ref[...]
    t = jnp.dot(h_ref[...], block, preferred_element_type=F32)
    wide = block.astype(F32)
    norm = jnp.sqrt(jnp.sum(wide * wide, axis=0, keepdims=True))
    n_ref[...] = norm
    t_ref[...] = t.astype(BF)
    scaled = t * (m_ref[...] / norm)

    @pl.when(pl.program_id(0) < rotated)
    def _():
        for part in range(t.shape[1] // HEAD_DIM):
            columns = slice(part * HEAD_DIM, (part + 1) * HEAD_DIM)
            p_ref[:, columns] = turned(scaled[:, columns], cos_ref[...], sin_ref[...]).astype(BF)

    @pl.when(pl.program_id(0) >= rotated)
    def _():
        p_ref[...] = scaled.astype(BF)


def qkv_forward(h, weight, magnitude, cosine, sine):
    rows, depth = h.shape
    columns = weight.shape[1]
    width = 2 * HEAD_DIM
    rotated = columns * 2 // 3 // width
    whole = lambda j: (0, 0)
    strip = lambda j: (0, j)
    return pl.pallas_call(
        functools.partial(qkv_kernel, rotated),
        grid=(columns // width,),
        in_specs=[
            pl.BlockSpec((rows, depth), whole),
            pl.BlockSpec((depth, width), strip),
            pl.BlockSpec((1, width), strip),
            pl.BlockSpec((rows, HEAD_DIM), whole),
            pl.BlockSpec((rows, HEAD_DIM), whole),
        ],
        out_specs=[
            pl.BlockSpec((rows, width), strip),
            pl.BlockSpec((rows, width), strip),
            pl.BlockSpec((1, width), strip),
        ],
        out_shape=[
            jax.ShapeDtypeStruct((rows, columns), BF),
            jax.ShapeDtypeStruct((rows, columns), BF),
            jax.ShapeDtypeStruct((1, columns), F32),
        ],
        compiler_params=pltpu.CompilerParams(vmem_limit_bytes=32 << 20),
        cost_estimate=pl.CostEstimate(
            flops=2 * rows * depth * columns, bytes_accessed=2 * depth * columns + 6 * rows * columns,
            transcendentals=columns,
        ),
        name="qkv_forward",
    )(h, weight, magnitude, cosine, sine)


def softmax_block(q, k, bias):
    scores = nt(q, k) * HEAD_DIM ** (-0.5) + bias
    weights = jnp.exp(scores - jnp.max(scores, axis=-1, keepdims=True))
    return weights / jnp.sum(weights, axis=-1, keepdims=True)


def attend_kernel(q_ref, k_ref, v_ref, bias_ref, o_ref):
    probs = softmax_block(q_ref[...], k_ref[...], bias_ref[...])
    o_ref[...] = mm(probs.astype(BF), v_ref[...]).astype(BF)


def attend_back_kernel(q_ref, k_ref, v_ref, g_ref, bias_ref, dq_ref, dk_ref, dv_ref):
    q, k, g = q_ref[...], k_ref[...], g_ref[...]
    probs = softmax_block(q, k, bias_ref[...])
    grad = nt(g, v_ref[...])
    inner = jnp.sum(probs * grad, axis=-1, keepdims=True)
    raw = (probs * (grad - inner) * HEAD_DIM ** (-0.5)).astype(BF)
    dq_ref[...] = mm(raw, k)
    dk_ref[...] = tn(raw, q)
    dv_ref[...] = tn(probs.astype(BF), g)


def attention_call(kernel, name, heads, q, kv, offsets, extra, bias, outs):
    rows, keys = bias.shape
    head = lambda base: lambda j: (0, base + j)
    specs = [
        pl.BlockSpec((rows, HEAD_DIM), head(0)),
        pl.BlockSpec((keys, HEAD_DIM), head(offsets[0])),
        pl.BlockSpec((keys, HEAD_DIM), head(offsets[1])),
    ]
    specs += [pl.BlockSpec((rows, HEAD_DIM), head(0)) for _ in extra]
    specs.append(pl.BlockSpec((rows, keys), lambda j: (0, 0)))
    return pl.pallas_call(
        kernel,
        grid=(heads,),
        in_specs=specs,
        out_specs=[pl.BlockSpec((length, HEAD_DIM), head(0)) for length, _ in outs],
        out_shape=[jax.ShapeDtypeStruct((length, heads * HEAD_DIM), kind) for length, kind in outs],
        compiler_params=pltpu.CompilerParams(vmem_limit_bytes=48 << 20),
        cost_estimate=pl.CostEstimate(
            flops=4 * len(outs) * rows * keys * HEAD_DIM * heads,
            bytes_accessed=8 * rows * HEAD_DIM * heads, transcendentals=rows * keys * heads,
        ),
        name=name,
    )(q, kv, kv, *extra, bias)


def attend_back_turn_kernel(
    q_ref, k_ref, v_ref, g_ref, bias_ref, tq_ref, tk_ref, tv_ref, s_ref, r_ref, cos_ref, sin_ref, dt_ref, dm_ref
):
    q, k, g = q_ref[...], k_ref[...], g_ref[...]
    probs = softmax_block(q, k, bias_ref[...])
    grad = nt(g, v_ref[...])
    inner = jnp.sum(probs * grad, axis=-1, keepdims=True)
    raw = (probs * (grad - inner) * HEAD_DIM ** (-0.5)).astype(BF)
    cosine, sine = cos_ref[...], -sin_ref[...]
    plain = (turned(mm(raw, k), cosine, sine), turned(tn(raw, q), cosine, sine), tn(probs.astype(BF), g))
    for member, t_ref in enumerate((tq_ref, tk_ref, tv_ref)):
        dt_ref[member] = (plain[member] * s_ref[member]).astype(BF)
        dm_ref[member] = jnp.sum(plain[member] * t_ref[...].astype(F32), axis=0, keepdims=True) * r_ref[member]


def attend_back_turn(heads, qkv, grad, bias, t, factor, inverse, cosine, sine):
    rows = bias.shape[0]
    head = lambda base: lambda j: (0, base + j)
    whole = lambda j: (0, 0)
    block = lambda base: pl.BlockSpec((rows, HEAD_DIM), head(base))
    member = lambda j: (0, 0, j)
    return pl.pallas_call(
        attend_back_turn_kernel,
        grid=(heads,),
        in_specs=[
            block(0), block(heads), block(2 * heads), block(0),
            pl.BlockSpec((rows, rows), whole),
            block(0), block(heads), block(2 * heads),
            pl.BlockSpec((3, 1, HEAD_DIM), member),
            pl.BlockSpec((3, 1, HEAD_DIM), member),
            pl.BlockSpec((rows, HEAD_DIM), whole),
            pl.BlockSpec((rows, HEAD_DIM), whole),
        ],
        out_specs=[pl.BlockSpec((3, rows, HEAD_DIM), member), pl.BlockSpec((3, 1, HEAD_DIM), member)],
        out_shape=[
            jax.ShapeDtypeStruct((3, rows, heads * HEAD_DIM), BF),
            jax.ShapeDtypeStruct((3, 1, heads * HEAD_DIM), F32),
        ],
        compiler_params=pltpu.CompilerParams(vmem_limit_bytes=48 << 20),
        cost_estimate=pl.CostEstimate(
            flops=10 * rows * rows * HEAD_DIM * heads, bytes_accessed=20 * rows * HEAD_DIM * heads,
            transcendentals=rows * rows * heads,
        ),
        name="attend_back_turn",
    )(qkv, qkv, qkv, grad, bias, t, t, t, factor, inverse, cosine, sine)


def words_out(ref, start, value):
    rows, columns = value.shape
    for chunk in range(-(-columns // WORD)):
        left = chunk * WORD
        used = min(WORD, columns - left)
        ref[chunk, start : start + rows, :used] = value[:, left : left + used]
        if used < WORD:
            ref[chunk, start : start + rows, used:] = jnp.zeros((rows, WORD - used), F32)


def row_of(row, rows=8):
    return jnp.concatenate([row, jnp.zeros((rows - row.shape[0], row.shape[1]), F32)], axis=0)


def qkv_back_kernel(
    dt_ref, v_ref, h_ref, low_ref, up_ref, cross_ref, s_ref, n_ref, dm_ref, out_ref, shared_ref, core_ref, acc_ref
):
    member = pl.program_id(0)
    dt, weight = dt_ref[0], v_ref[...]
    update = nt(dt, weight)

    @pl.when(member == 0)
    def _():
        acc_ref[...] = update

    @pl.when(member > 0)
    def _():
        acc_ref[...] += update

    @pl.when(member == pl.num_programs(0) - 1)
    def _():
        out_ref[...] = acc_ref[...].astype(BF)

    up = up_ref[0]
    pull = -s_ref[0] * dm_ref[0] / n_ref[0]
    low_grad = nt(dt, up.astype(BF)).astype(BF)
    words_out(shared_ref, 0, SCALE * (tn(low_grad, h_ref[...]) + nt((up * pull).astype(BF), weight)))
    words_out(core_ref, 0, SCALE * (mm(low_ref[0], dt) + cross_ref[0] * pull))


def qkv_back(dt, weight, h, low, up, cross, factor, norm, dm):
    members, rows, columns = dt.shape
    width = h.shape[1]
    rank = up.shape[1]
    step = lambda j: (j, 0, 0)
    small = pl.BlockSpec((1, 1, columns), step)
    return pl.pallas_call(
        qkv_back_kernel,
        grid=(members,),
        in_specs=[
            pl.BlockSpec((1, rows, columns), step),
            pl.BlockSpec((width, columns), lambda j: (0, j)),
            pl.BlockSpec((rows, width), lambda j: (0, 0)),
            pl.BlockSpec((1, rank, rows), step),
            pl.BlockSpec((1, rank, columns), step),
            pl.BlockSpec((1, rank, columns), step),
            small, small, small,
        ],
        out_specs=[
            pl.BlockSpec((rows, width), lambda j: (0, 0)),
            pl.BlockSpec((width // WORD, rank, WORD), lambda j: (0, j, 0)),
            pl.BlockSpec((columns // WORD, rank, WORD), lambda j: (0, j, 0)),
        ],
        out_shape=[
            jax.ShapeDtypeStruct((rows, width), BF),
            jax.ShapeDtypeStruct((width // WORD, members * rank, WORD), F32),
            jax.ShapeDtypeStruct((columns // WORD, members * rank, WORD), F32),
        ],
        scratch_shapes=[pltpu.VMEM((rows, width), F32)],
        compiler_params=pltpu.CompilerParams(vmem_limit_bytes=48 << 20),
        cost_estimate=pl.CostEstimate(
            flops=2 * members * rows * columns * width, bytes_accessed=2 * members * width * columns,
            transcendentals=0,
        ),
        name="qkv_back",
    )(dt, weight, h, low, up, cross, factor, norm, dm)


def out_adapter_kernel(dt_ref, v_ref, u_ref, down_ref, up_ref, s_ref, n_ref, dm_ref, own_ref, shared_ref, core_ref):
    dt, weight, u = dt_ref[...], v_ref[...], u_ref[...]
    down, up = down_ref[...], up_ref[...]
    rank = up.shape[0]
    pull = -s_ref[...] * dm_ref[...] / n_ref[...]
    low_grad = nt(dt, up.astype(BF)).astype(BF)
    low = nt(down, u).astype(BF)
    words_out(core_ref, 0, SCALE * (tn(low_grad, u) + nt((up * pull).astype(BF), weight)))
    words_out(shared_ref, 0, SCALE * (mm(low, dt) + mm(down, weight) * pull))
    words_out(shared_ref, rank, row_of(own_ref[...]))


def out_adapter(dt, weight, u, down, up, factor, norm, dm_pair, dm_own):
    rank, width = up.shape
    inside = u.shape[1]
    return pl.pallas_call(
        out_adapter_kernel,
        out_shape=[
            jax.ShapeDtypeStruct((width // WORD, rank + 8, WORD), F32),
            jax.ShapeDtypeStruct((inside // WORD, rank, WORD), F32),
        ],
        compiler_params=pltpu.CompilerParams(vmem_limit_bytes=48 << 20),
        cost_estimate=pl.CostEstimate(
            flops=2 * width * inside * 256, bytes_accessed=2 * width * inside, transcendentals=0
        ),
        name="out_adapter",
    )(dt, weight, u, down, up, factor, norm, dm_pair, dm_own)


def chunks_of(columns, width):
    return [(left, min(left + width, columns)) for left in range(0, columns, width)]


def feed_kernel(
    h_ref, g_ref, expand_ref, contract_ref, s_ref, back_ref, out_ref, dt_ref, hidden_ref, dm_ref
):
    h, g = h_ref[...], g_ref[...]
    quarter = hidden_ref.shape[1]

    @pl.when(pl.program_id(0) == 0)
    def _():
        dm_ref[...] = jnp.zeros_like(dm_ref)

    for left, right in chunks_of(quarter, 512):
        near, far = slice(left, right), slice(quarter + left, quarter + right)
        gate_t = mm(h, expand_ref[:, near])
        up_t = mm(h, expand_ref[:, far])
        grad = mm(g, contract_ref[:, near])
        gate = gate_t * s_ref[:, near]
        up = up_t * s_ref[:, far]
        sigmoid = 1.0 / (1.0 + jnp.exp(-gate))
        silu = gate * sigmoid
        hidden_ref[:, near] = (silu * up).astype(BF)
        up_grad = grad * silu
        gate_grad = grad * up * (sigmoid + silu * (1.0 - sigmoid))
        dm_ref[:, near] += jnp.sum(gate_grad * gate_t, axis=0, keepdims=True)
        dm_ref[:, far] += jnp.sum(up_grad * up_t, axis=0, keepdims=True)
        dt_ref[:, near] = (gate_grad * s_ref[:, near]).astype(BF)
        dt_ref[:, far] = (up_grad * s_ref[:, far]).astype(BF)
    back_ref[...] = nt(dt_ref[...], expand_ref[...]).astype(BF)
    out_ref[...] = nt(hidden_ref[...], contract_ref[...]).astype(BF)


def feed_forward_back(h, g, expand, contract, factor):
    rows, width = h.shape
    double = expand.shape[1]
    quarter = double // 2
    block = rows // 2
    row = lambda i: (i, 0)
    whole = lambda i: (0, 0)
    once = pl.Buffered(1)
    return pl.pallas_call(
        feed_kernel,
        grid=(rows // block,),
        in_specs=[
            pl.BlockSpec((block, width), row),
            pl.BlockSpec((block, width), row),
            pl.BlockSpec((width, double), whole, pipeline_mode=once),
            pl.BlockSpec((width, quarter), whole, pipeline_mode=once),
            pl.BlockSpec((1, double), whole),
        ],
        out_specs=[
            pl.BlockSpec((block, width), row),
            pl.BlockSpec((block, width), row),
            pl.BlockSpec((block, double), row),
            pl.BlockSpec((block, quarter), row),
            pl.BlockSpec((1, double), whole),
        ],
        out_shape=[
            jax.ShapeDtypeStruct((rows, width), BF),
            jax.ShapeDtypeStruct((rows, width), BF),
            jax.ShapeDtypeStruct((rows, double), BF),
            jax.ShapeDtypeStruct((rows, quarter), BF),
            jax.ShapeDtypeStruct((1, double), F32),
        ],
        compiler_params=pltpu.CompilerParams(vmem_limit_bytes=56 << 20),
        cost_estimate=pl.CostEstimate(
            flops=12 * rows * width * quarter, bytes_accessed=6 * width * quarter + 18 * rows * quarter,
            transcendentals=rows * quarter,
        ),
        name="feed_forward_back",
    )(h, g, expand, contract, factor)


def feed_adapter_kernel(h_ref, g_ref, dt_ref, hidden_ref, down_ref, up_ref, cdown_ref, cup_ref, *refs):
    shared_ref, quad_ref = refs[-2:]
    rank = cup_ref.shape[0]
    h, g, dt, hidden = h_ref[...], g_ref[...], dt_ref[...], hidden_ref[...]
    quarter = hidden.shape[1]
    down, up, cdown, cup = down_ref[...], up_ref[...], cdown_ref[...], cup_ref[...]
    halves = (slice(0, quarter), slice(quarter, 2 * quarter))
    shared, quads = [], []
    low = nt(down, h).astype(BF)
    for member, part in enumerate(halves):
        place = slice(member * rank, (member + 1) * rank)
        low_grad = nt(dt[:, part], up[member].astype(BF)).astype(BF)
        shared.append(tn(low_grad, h))
        quads.append(mm(low[place], dt[:, part]))
    low_grad = nt(g, cup.astype(BF)).astype(BF)
    quads.append(tn(low_grad, hidden))
    shared.append(mm(nt(cdown, hidden).astype(BF), g))
    if len(refs) == 2:
        for member in range(3):
            rows = slice(member * rank, (member + 1) * rank)
            shared_ref[rows] = shared[member]
            quad_ref[rows] = quads[member]
        return
    shared_in, quad_in, expand_ref, contract_ref, pull_ref, dm_ref, cpull_ref, cdm_ref = refs[:-2]
    for member, part in enumerate(halves):
        rows = slice(member * rank, (member + 1) * rank)
        pull = pull_ref[:, part]
        weight = expand_ref[:, part]
        total = shared[member] + shared_in[rows] + nt((up[member] * pull).astype(BF), weight)
        words_out(shared_ref, member * rank, SCALE * total)
        total = quads[member] + quad_in[rows] + mm(down[rows], weight) * pull
        words_out(quad_ref, member * rank, SCALE * total)
    rows = slice(2 * rank, 3 * rank)
    total = quads[2] + quad_in[rows] + mm((cup * cpull_ref[...]).astype(BF), contract_ref[...])
    words_out(quad_ref, 2 * rank, SCALE * total)
    total = shared[2] + shared_in[rows] + nt(cdown, contract_ref[...]) * cpull_ref[...]
    words_out(shared_ref, 2 * rank, SCALE * total)
    words_out(shared_ref, 3 * rank, row_of(cdm_ref[...]))
    both = jnp.concatenate([dm_ref[:, part] for part in halves], axis=0)
    words_out(quad_ref, 3 * rank, row_of(both))


def feed_adapter(h, g, dt, hidden, down, up, cdown, cup, last=None):
    rank, width = cup.shape
    quarter = hidden.shape[1]
    if last is None:
        shapes = [(3 * rank, width), (3 * rank, quarter)]
    else:
        shapes = [(width // WORD, 3 * rank + 8, WORD), (-(-quarter // WORD), 3 * rank + 8, WORD)]
    return pl.pallas_call(
        feed_adapter_kernel,
        out_shape=[jax.ShapeDtypeStruct(shape, F32) for shape in shapes],
        compiler_params=pltpu.CompilerParams(vmem_limit_bytes=56 << 20),
        cost_estimate=pl.CostEstimate(
            flops=8 * h.shape[0] * width * 512, bytes_accessed=8 * h.shape[0] * width, transcendentals=0
        ),
        name="feed_adapter",
    )(h, g, dt, hidden, down, up, cdown, cup, *(last or ()))


def turn_back_kernel(rotated, g_ref, t_ref, s_ref, r_ref, cos_ref, sin_ref, dt_ref, dm_ref):
    grad = g_ref[...]

    def finish(plain):
        dt_ref[0] = (plain * s_ref[...]).astype(BF)
        dm_ref[...] = jnp.sum(plain * t_ref[...].astype(F32), axis=0, keepdims=True) * r_ref[...]

    @pl.when(pl.program_id(0) < rotated)
    def _():
        finish(turned(grad, cos_ref[...], -sin_ref[...]))

    @pl.when(pl.program_id(0) >= rotated)
    def _():
        finish(grad)


def turn_back(grads, t, factor, inverse, cosine, sine):
    rows, columns = t.shape
    whole = lambda j: (0, 0)
    strip = lambda j: (0, j)
    heads = columns // HEAD_DIM
    each = heads // 3
    return pl.pallas_call(
        functools.partial(turn_back_kernel, 2 * each),
        grid=(heads,),
        in_specs=[
            pl.BlockSpec((rows, HEAD_DIM), strip),
            pl.BlockSpec((rows, HEAD_DIM), strip),
            pl.BlockSpec((1, HEAD_DIM), strip),
            pl.BlockSpec((1, HEAD_DIM), strip),
            pl.BlockSpec((rows, HEAD_DIM), whole),
            pl.BlockSpec((rows, HEAD_DIM), whole),
        ],
        out_specs=[
            pl.BlockSpec((1, rows, HEAD_DIM), lambda j: (j // each, 0, j % each)),
            pl.BlockSpec((1, HEAD_DIM), strip),
        ],
        out_shape=[
            jax.ShapeDtypeStruct((3, rows, columns // 3), BF),
            jax.ShapeDtypeStruct((1, columns), F32),
        ],
        name="turn_back",
    )(grads, t, factor, inverse, cosine, sine)


def unpacked(words, columns):
    return jnp.concatenate([words[i] for i in range(words.shape[0])], axis=1)[:, :columns]


def pad_rows(a, multiple):
    short = -a.shape[0] % multiple
    return jnp.pad(a, ((0, short), (0, 0))) if short else a


def halve(a, name, index):
    parts = a.reshape(2, a.shape[0] // 2, a.shape[1])
    return take(parts, index, 0) + swap(take(parts, 1 - index, 0), name)


def join(a, name, index):
    return pair(a, swap(a, name), index).reshape(2 * a.shape[0], a.shape[1])


def spread(a, name):
    size, place = lax.axis_size(name), lax.axis_index(name)
    parts = a.reshape(size, a.shape[0] // size, a.shape[1])
    total = take(parts, place, 0)
    for step in range(1, size):
        total = total + shift(take(parts, (place + step) % size, 0), name, step)
    return total


def collect(a, name):
    size, place = lax.axis_size(name), lax.axis_index(name)
    buffer = jnp.zeros((size,) + a.shape, a.dtype)
    buffer = put(buffer, a, place, 0)
    for step in range(1, size):
        buffer = put(buffer, shift(a, name, step), (place - step) % size, 0)
    return buffer.reshape(size * a.shape[0], a.shape[1])


def reduce_all(shared, by_core, by_quad):
    c, x = lax.axis_index("core"), lax.axis_index("xx")
    unit = lax.axis_size("yy") * lax.axis_size("seq")
    half = halve(pad_rows(shared, 16), "core", c)
    stack = half if by_core is None else jnp.concatenate([half, by_core], axis=0)
    quarter = halve(pad_rows(stack, 16), "xx", x)
    last = quarter if by_quad is None else jnp.concatenate([quarter, by_quad], axis=0)
    last = pad_rows(last, 8 * unit)
    last = collect(collect(spread(spread(last, "yy"), "seq"), "seq"), "yy")
    joined = join(last[: quarter.shape[0]], "xx", x)
    everywhere = join(joined[: half.shape[0]], "core", c)
    cores = None
    if by_core is not None:
        mine = joined[half.shape[0] : half.shape[0] + by_core.shape[0]]
        cores = pair(mine, swap(mine, "core"), c)
    quads = None
    if by_quad is not None:
        mine = last[quarter.shape[0] : quarter.shape[0] + by_quad.shape[0]]
        both = pair(mine, swap(mine, "xx"), x)
        quads = pair(both, swap(both, "core"), c, axis=1)
    return everywhere, cores, quads


def body(
    tokens,
    cotangent,
    attention_base,
    expand_base,
    contract_base,
    attention_down,
    attention_up,
    attention_magnitude,
    expand_down,
    expand_up,
    expand_magnitude,
    contract_down,
    contract_up,
    contract_magnitude,
    prompt_length,
    response_length,
):
    y, x = lax.axis_index("yy"), lax.axis_index("xx")
    c, z = lax.axis_index("core"), lax.axis_index("seq")
    ny, count = lax.axis_size("yy"), lax.axis_size("seq")
    own_rows, local, width = tokens.shape
    rows = 2 * own_rows
    split = count // rows
    piece = local // (2 * split)
    half = count * piece
    blocks = ny * 2
    rank = attention_down.shape[-1]
    unit = attention_base.shape[1]
    hidden_size = expand_base.shape[-1]
    quarter = hidden_size // 4
    place = ((y * 2 + x) * 2 + c) * count + z
    sub = z % split

    def by_core(a):
        shaped = a.reshape(a.shape[:-1] + (blocks, 2, a.shape[-1] // blocks // 2))
        axis = a.ndim
        flat = a.shape[:-1] + (a.shape[-1] // 2,)
        return take(shaped, c, axis).reshape(flat), take(shaped, 1 - c, axis).reshape(flat)

    def by_quarter(a):
        shaped = a.reshape(a.shape[:-1] + (4, quarter))
        return take(shaped, 2 * x + c, a.ndim - 1)

    down_rows = lax.dynamic_slice_in_dim(attention_down, place * unit, unit, 1)
    attention = merged(attention_base, down_rows, attention_up)
    mine, other = by_core(attention[:3])
    mine = mine.transpose(1, 0, 2).reshape(unit, -1)
    other = other.transpose(1, 0, 2).reshape(unit, -1)
    qkv_piece = pair(mine, swap(other, "core"), c)

    def relayout_start(a):
        shaped = a.reshape(own_rows, split, 2, piece, width)
        kept, sent = take(shaped, c, 2), take(shaped, 1 - c, 2)
        return Box([pair(kept, swap(sent, "core"), c).reshape(count, piece, width)])

    def exchange(a):
        return lax.all_to_all(a, "seq", 0, 0, tiled=True)

    def ring(box):
        return links.send("seq", box, lambda a: shift(a, "seq", 1))

    def across(box, turn):
        return links.send("yy", box, lambda a: shift(a, "yy", turn)) if turn else box

    links = Links(2)
    out_piece = attention[3]
    attention_boxes = [Box([qkv_piece, out_piece])]
    attention_far = [links.send("xx", attention_boxes[0], lambda a: swap(a, "xx"))]

    expand_rows = lax.dynamic_slice_in_dim(expand_down, place * unit, unit, 1)
    expand = merged(expand_base, expand_rows, expand_up)
    contract_columns = lax.dynamic_slice_in_dim(contract_up, place * unit, unit, 1)
    contract = merged(contract_base.T, contract_columns.T, contract_down.T)
    feed = jnp.stack([expand[0], expand[1], contract], axis=1).reshape(unit, 3, 2, 2, quarter)
    by_x = pair(take(feed, c, 3), swap(take(feed, 1 - c, 3), "core"), c)
    far = links.send("xx", Box([take(by_x, 1 - x, 3)]), lambda a: swap(a, "xx"))
    feed_piece = pair(take(by_x, x, 3), far.arrays[0], x)
    expand_piece = feed_piece[:, :, :, :2].reshape(2, 2, unit, 2 * quarter)

    for step in range(1, count):
        attention_boxes.append(ring(attention_boxes[-1]))
    tokens_moved = links.send("seq", relayout_start(tokens), exchange)
    expand_boxes, contract_boxes = [Box([expand_piece])], [Box([feed_piece[:, :, :, 2]])]
    for step in range(1, count):
        expand_boxes.append(ring(expand_boxes[-1]))
        contract_boxes.append(ring(contract_boxes[-1]))
        if step == 1:
            cotangent_moved = links.send("seq", relayout_start(cotangent), exchange)

    attention_all, expand_all, contract_all = Gathered(True), Gathered(False), Gathered(False)

    def feed_step(step):
        for boxes, gathered in ((expand_boxes, expand_all), (contract_boxes, contract_all)):
            for turn in range(ny):
                gathered.add(across(boxes[step], turn), turn, False, step)

    def attention_step(step):
        for turn in range(ny):
            near = across(attention_boxes[step], turn)
            if step == 0 and turn == 0:
                other = attention_far[0]
            else:
                other = links.send("xx", near, lambda a: swap(a, "xx"))
            attention_all.add(near, turn, False, step)
            attention_all.add(other, turn, True, step)

    for step in range(count):
        if step >= 2:
            feed_step(step - 2)
        attention_step(step)
    for step in range(max(count - 2, 0), count):
        feed_step(step)

    tokens_own = tokens_moved.arrays[0].reshape(half, width)
    tokens_both = jnp.concatenate([tokens_own, swap(tokens_own, "core")], axis=0)
    qkv_weight = attention_all.build(0).reshape(width, -1)
    out_weight = attention_all.build(1).reshape(width // 2, width)
    expand_weight = expand_all.build(0).reshape(width, 2 * quarter)
    contract_weight = contract_all.build(0).reshape(width, quarter)

    def positions_of(sub_place, core_place):
        source = jnp.arange(count, dtype=jnp.int32)[:, None] * local
        inner = sub_place * 2 * piece + core_place * piece + jnp.arange(piece, dtype=jnp.int32)[None]
        return (source + inner).reshape(half)

    query_place = jnp.concatenate([positions_of(sub, c), positions_of(sub, 1 - c)])
    key_place = jnp.concatenate(
        [positions_of((sub - step) % split, side) for step in range(split) for side in (c, 1 - c)]
    )
    totals = (prompt_length + response_length).astype(F32)
    total = take(pair(totals, swap(totals, "core"), c).reshape(rows), z // split, 0).astype(jnp.int32)
    allowed = (key_place[None] <= query_place[:, None]) & (key_place[None] < total)
    bias = jnp.where(allowed, 0.0, -1e30).astype(F32)
    frequency = 10000.0 ** (-jnp.arange(HEAD_DIM // 2).astype(F32) / (HEAD_DIM // 2))
    angles = query_place.astype(F32)[:, None] * frequency[None]
    cosine = jnp.concatenate([jnp.cos(angles)] * 2, axis=1)
    sine = jnp.concatenate([-jnp.sin(angles), jnp.sin(angles)], axis=1)

    heads = width // 2 // HEAD_DIM
    rows_both = tokens_both.astype(F32)
    first = rms(rows_both).astype(BF)
    magnitude = by_core(attention_magnitude[:3])[0].reshape(1, -1)
    qkv_t, qkv_p, qkv_norm = qkv_forward(first, qkv_weight, magnitude, cosine, sine)

    def share(a, step):
        perm = [(i, (i // split) * split + (i % split + step) % split) for i in range(count)]
        return lax.ppermute(a, "seq", perm)

    if split == 1:
        kv, offsets = qkv_p, (heads, 2 * heads)
    else:
        own_kv = qkv_p[:, heads * HEAD_DIM :]
        kv = jnp.concatenate([own_kv] + [share(own_kv, step) for step in range(1, split)], axis=0)
        offsets = (0, heads)
    (mixed,) = attention_call(
        attend_kernel, "attend", heads, qkv_p, kv, offsets, [], bias, [(2 * half, BF)]
    )

    def core_scatter(partial):
        return partial[:half].astype(F32) + swap(partial[half:].astype(BF), "core").astype(F32)

    def core_join(own):
        return jnp.concatenate([own, swap(own, "core")], axis=0)

    out_square = jnp.sum(out_weight.astype(F32) ** 2, axis=0, keepdims=True)
    out_norm = jnp.sqrt(out_square + swap(out_square, "core"))
    out_scale = attention_magnitude[3:] / out_norm
    out_t = core_scatter(mm(mixed, out_weight))
    rows_own = tokens_own.astype(F32)
    middle = rows_own + out_t * out_scale
    second_own = rms(middle).astype(BF)
    second_near = core_join(second_own)
    second_own_far = swap(second_own, "xx")
    second_far = core_join(second_own_far)

    cotangent_own = cotangent_moved.arrays[0].reshape(half, width)
    grad_own = cotangent_own.astype(F32)
    contract_square = jnp.sum(contract_weight.astype(F32) ** 2, axis=1)[None]
    contract_square = contract_square + swap(contract_square, "core")
    contract_norm = jnp.sqrt(contract_square + swap(contract_square, "xx"))
    contract_scale = contract_magnitude[None] / contract_norm
    scaled = (grad_own * contract_scale).astype(BF)
    scaled_near = core_join(scaled)
    scaled_far = core_join(swap(scaled, "xx"))
    expand_norm = jnp.sqrt(jnp.sum(expand_weight.astype(F32) ** 2, axis=0, keepdims=True))
    expand_scale = by_quarter(expand_magnitude).reshape(1, -1) / expand_norm
    back_far, out_far, dt_far, hidden_far, dm_far = feed_forward_back(
        second_far, scaled_far, expand_weight, contract_weight, expand_scale
    )
    back_near, out_near, dt_near, hidden_near, dm_near = feed_forward_back(
        second_near, scaled_near, expand_weight, contract_weight, expand_scale
    )

    def quad_scatter(near, far):
        far_sum = core_scatter(far).astype(BF)
        return core_scatter(near) + swap(far_sum, "xx").astype(F32)

    second_grad = quad_scatter(back_near, back_far)
    middle_grad = grad_own + rms_back(middle, second_grad)
    contract_t = quad_scatter(out_near, out_far)
    output_own = (middle + contract_t * contract_scale).astype(BF)

    out_dm = jnp.sum(middle_grad * out_t, axis=0, keepdims=True) / out_norm
    out_dt = core_join((middle_grad * out_scale).astype(BF))
    mixed_grad = nt(out_dt, out_weight).astype(BF)
    keys = 2 * half * split
    members = lambda a: a.reshape(3, 1, width // 2)
    qkv_scale = magnitude / qkv_norm

    def reunite(a):
        parts = a.reshape(split, 2 * half, -1)
        total = parts[0]
        for step in range(1, split):
            total = total + share(parts[step].astype(BF), -step).astype(F32)
        return total

    if split > 1:
        dq, dk, dv = attention_call(
            attend_back_kernel, "attend_back", heads, qkv_p, kv, offsets, [mixed_grad], bias,
            [(2 * half, F32), (keys, F32), (keys, F32)],
        )
        grads = jnp.concatenate([dq, reunite(dk), reunite(dv)], axis=1)
        qkv_dt, qkv_dm = turn_back(grads, qkv_t, qkv_scale, 1.0 / qkv_norm, cosine, sine)
        qkv_dm = members(qkv_dm)
    else:
        qkv_dt, qkv_dm = attend_back_turn(
            heads, qkv_p, mixed_grad, bias, qkv_t, members(qkv_scale), members(1.0 / qkv_norm), cosine, sine
        )
    core_up = by_core(attention_up[:3])[0]
    downs = attention_down[:3].transpose(0, 2, 1).reshape(3 * rank, width).astype(BF)
    low = nt(downs, first).astype(BF).reshape(3, rank, 2 * half)
    cross = mm(downs, qkv_weight)
    cross = jnp.stack(
        [cross[i * rank : (i + 1) * rank, i * width // 2 : (i + 1) * width // 2] for i in range(3)]
    )
    first_part, qkv_shared, qkv_core = qkv_back(
        qkv_dt, qkv_weight, first, low, core_up, cross, members(qkv_scale), members(qkv_norm), qkv_dm
    )
    first_grad = core_scatter(first_part)
    tokens_grad_own = middle_grad + rms_back(rows_own, first_grad)

    gate_up = jnp.stack([by_quarter(expand_up[i]) for i in range(2)])
    feed_downs = expand_down.transpose(0, 2, 1).reshape(2 * rank, width).astype(BF)
    contract_rows = take(contract_down.T.reshape(rank, 4, quarter), 2 * x + c, 1).astype(BF)
    expand_dm = (dm_near + dm_far) / expand_norm
    contract_dm = jnp.sum(grad_own * contract_t, axis=0, keepdims=True) / contract_norm
    contract_sum = contract_dm + swap(contract_dm, "core")
    contract_sum = contract_sum + swap(contract_sum, "xx")
    part = feed_adapter(
        second_far, scaled_far, dt_far, hidden_far, feed_downs, gate_up, contract_rows, contract_up
    )
    pulls = (-expand_scale * expand_dm / expand_norm, -contract_scale * contract_sum / contract_norm)
    feed_words, feed_quad_words = feed_adapter(
        second_near, scaled_near, dt_near, hidden_near, feed_downs, gate_up, contract_rows, contract_up,
        (*part, expand_weight, contract_weight, pulls[0], expand_dm, pulls[1], contract_dm),
    )
    flat = lambda a: a.reshape(-1, WORD)
    feed_shared, _, feed_quads = reduce_all(flat(feed_words), None, flat(feed_quad_words))

    out_rows = by_core(attention_down[3].T)[0].astype(BF)
    out_words, out_core_words = out_adapter(
        out_dt, out_weight, mixed, out_rows, attention_up[3], out_scale, out_norm, out_dm + swap(out_dm, "core"),
        out_dm,
    )
    dm_words = jnp.pad(qkv_dm[:, 0], ((0, 5), (0, 0)))
    dm_words = jnp.stack([dm_words[:, i : i + WORD] for i in range(0, width // 2, WORD)])
    shared = jnp.concatenate([flat(qkv_shared), flat(out_words)])
    cores = jnp.concatenate([flat(qkv_core), flat(dm_words), flat(out_core_words)])
    attention_shared, attention_cores, _ = reduce_all(shared, cores, None)

    def interleave(parts):
        shaped = [p.reshape(p.shape[0], blocks, 1, -1) for p in parts]
        return jnp.concatenate(shaped, axis=2).reshape(parts[0].shape[0], -1)

    used = flat(qkv_shared).shape[0]
    qkv_down_all = unpacked(attention_shared[:used].reshape(qkv_shared.shape), width)
    out_all = unpacked(attention_shared[used : used + flat(out_words).shape[0]].reshape(out_words.shape), width)
    core_parts = []
    for side in range(2):
        start, parts = 0, []
        for words in (qkv_core, dm_words, out_core_words):
            used = flat(words).shape[0]
            parts.append(unpacked(attention_cores[side, start : start + used].reshape(words.shape), width // 2))
            start += used
        core_parts.append(parts)
    qkv_up_all, qkv_dm_all, out_down_all = (interleave([core_parts[0][i], core_parts[1][i]]) for i in range(3))
    attention_down_grad = (
        jnp.concatenate([qkv_down_all, out_down_all]).reshape(4, rank, width).transpose(0, 2, 1)
    )
    attention_up_grad = jnp.concatenate([qkv_up_all, out_all[:rank]]).reshape(4, rank, width)
    attention_magnitude_grad = jnp.concatenate([qkv_dm_all[:3], out_all[rank : rank + 1]])

    feed_all = unpacked(feed_shared[: flat(feed_words).shape[0]].reshape(feed_words.shape), width)
    quad_all = jnp.concatenate(
        [unpacked(feed_quads[i, j].reshape(feed_quad_words.shape), quarter) for i in range(2) for j in range(2)],
        axis=1,
    )

    def restore(own):
        joined = own.reshape(count, piece, width)
        joined = lax.all_to_all(joined, "seq", 0, 0, tiled=True)
        shaped = joined.reshape(2, own_rows, split, piece, width)
        kept, sent = take(shaped, c, 0), take(shaped, 1 - c, 0)
        return pair(kept, swap(sent, "core"), c, axis=2).reshape(own_rows, local, width)

    layer_output = restore(output_own)
    tokens_grad = restore(tokens_grad_own.astype(BF)).astype(F32)
    return (
        layer_output,
        tokens_grad,
        attention_down_grad,
        attention_up_grad,
        attention_magnitude_grad,
        feed_all[: 2 * rank].reshape(2, rank, width).transpose(0, 2, 1),
        quad_all[: 2 * rank].reshape(2, rank, hidden_size),
        quad_all[3 * rank : 3 * rank + 2],
        quad_all[2 * rank : 3 * rank].T,
        feed_all[2 * rank : 3 * rank],
        feed_all[3 * rank],
    )


def solution(mesh):
    devices = mesh.devices
    chips = devices.shape[0] // 2
    fine = Mesh(devices.reshape(chips // 2, 2, 2, devices.shape[1]), ALL)
    dp = ("yy", "xx", "core")
    every = ("yy", "xx", "core", "seq")
    placed = (
        P(dp, "seq", None),
        P(dp, "seq", None),
        P(None, every, None),
        P(None, every, None),
        P(None, every),
        P(),
        P(),
        P(),
        P(),
        P(),
        P(),
        P(),
        P(),
        P(),
        P(dp),
        P(dp),
    )
    return jax.shard_map(
        body,
        mesh=fine,
        in_specs=placed,
        out_specs=(P(dp, "seq", None), P(dp, "seq", None)) + (P(),) * 9,
        check_vma=False,
    )
```

```python
import functools

import jax
import jax.numpy as jnp
from jax import lax
from jax.experimental import pallas as pl
from jax.experimental.pallas import tpu as pltpu
from jax.sharding import Mesh
from jax.sharding import PartitionSpec as P

HEAD_DIM = 128
SCALE = 2.0
BF = jnp.bfloat16
F32 = jnp.float32
ALL = ("yy", "xx", "core", "seq")
WORD = 512


def mm(a, b, dims=((1,), (0,))):
    return lax.dot_general(a, b, (dims, ((), ())), preferred_element_type=F32)


def nt(a, b):
    return mm(a, b, ((1,), (1,)))


def tn(a, b):
    return mm(a, b, ((0,), (0,)))


def take(a, index, axis):
    return lax.dynamic_index_in_dim(a, index, axis, keepdims=False)


def swap(a, name):
    return lax.ppermute(a, name, [(0, 1), (1, 0)])


def shift(a, name, step):
    size = lax.axis_size(name)
    return lax.ppermute(a, name, [(i, (i + step) % size) for i in range(size)])


def pair(mine, other, index, axis=0):
    first = jnp.where(index == 0, mine, other)
    second = jnp.where(index == 0, other, mine)
    return jnp.stack([first, second], axis=axis)


def put(buffer, block, index, axis):
    return lax.dynamic_update_slice_in_dim(buffer, jnp.expand_dims(block, axis), index, axis)


def rms(v):
    return v * lax.rsqrt(jnp.mean(v * v, axis=-1, keepdims=True) + 1e-05)


def rms_back(v, grad):
    inverse = lax.rsqrt(jnp.mean(v * v, axis=-1, keepdims=True) + 1e-05)
    inner = jnp.mean(v * grad, axis=-1, keepdims=True)
    return grad * inverse - v * (inner * inverse * inverse * inverse)


def merged(base, down, up):
    product = lax.dot_general(
        down.astype(BF), up.astype(BF), (((down.ndim - 1,), (up.ndim - 2,)), (tuple(range(down.ndim - 2)),) * 2),
        preferred_element_type=F32,
    )
    return (base.astype(F32) + SCALE * product).astype(BF)


class Box:
    def __init__(self, array):
        self.array = array


class Links:
    def __init__(self, depth, boxes, buffers):
        self.depth = depth
        self.boxes = boxes
        self.buffers = buffers
        self.rounds = []
        self.placed = 0

    def run(self, queues):
        boxes = self.boxes
        while any(queues):
            ready = set(boxes)
            self.place(len(self.rounds) - self.depth)
            self.rounds.append([])
            for queue in queues:
                for place, (source, result, move) in enumerate(queue):
                    if source in ready:
                        queue.pop(place)
                        self.send(boxes, source, result, move)
                        break

    def place(self, until):
        while self.placed < until:
            for name, box in self.rounds[self.placed]:
                for buffer in self.buffers.values():
                    buffer.put(name, box.array)
            self.placed += 1

    def send(self, boxes, source, result, move):
        box = boxes[source]
        if len(self.rounds) > self.depth:
            old = [b for name, b in self.rounds[-1 - self.depth] if b is not box and "_" not in name]
            held = [b for b in self.buffers.values() if b.pending()]
            both = lax.optimization_barrier((box.array, [b.array for b in old], [b.array for b in held]))
            box.array = both[0]
            for b, array in zip(old + held, both[1] + both[2]):
                b.array = array
        boxes[result] = Box(move(box.array))
        self.rounds[-1].append((result, boxes[result]))


class Buffer:
    def __init__(self, shape, free, blocks):
        self.array = unwritten(shape, BF)
        self.free = free
        self.blocks = blocks

    def pending(self):
        return len(self.blocks) > self.free

    def put(self, name, block):
        if name in self.blocks:
            part, start = self.blocks.pop(name)(block)
            self.array = lax.dynamic_update_slice(self.array, part, [jnp.int32(v) for v in start])


def unwritten(shape, kind):
    return pl.pallas_call(
        lambda ref: None, out_shape=jax.ShapeDtypeStruct(shape, kind),
        out_specs=pl.BlockSpec(memory_space=pl.ANY), name="unwritten",
    )()


def turned(v, cosine, sine):
    return v * cosine + pltpu.roll(v, HEAD_DIM // 2, 1) * sine


def qkv_kernel(rotated, h_ref, v_ref, down_ref, m_ref, cos_ref, sin_ref, t_ref, p_ref, n_ref, cross_ref):
    block = v_ref[...]
    rows = h_ref.shape[0]
    both = jnp.dot(jnp.concatenate([h_ref[...], down_ref[...]], axis=0), block, preferred_element_type=F32)
    cross_ref[...] = both[rows:]
    t = both[:rows]
    wide = block.astype(F32)
    norm = jnp.sqrt(jnp.sum(wide * wide, axis=0, keepdims=True))
    n_ref[...] = norm
    t_ref[...] = t.astype(BF)
    scaled = t * (m_ref[...] / norm)

    @pl.when(pl.program_id(0) < rotated)
    def _():
        for part in range(t.shape[1] // HEAD_DIM):
            columns = slice(part * HEAD_DIM, (part + 1) * HEAD_DIM)
            p_ref[:, columns] = turned(scaled[:, columns], cos_ref[...], sin_ref[...]).astype(BF)

    @pl.when(pl.program_id(0) >= rotated)
    def _():
        p_ref[...] = scaled.astype(BF)


def qkv_forward(h, weight, downs, magnitude, cosine, sine):
    rows, depth = h.shape
    columns = magnitude.shape[1]
    width = 2 * HEAD_DIM
    rotated = columns * 2 // 3 // width
    whole = lambda j: (0, 0)
    strip = lambda j: (0, j)
    return pl.pallas_call(
        functools.partial(qkv_kernel, rotated),
        grid=(columns // width,),
        in_specs=[
            pl.BlockSpec((rows, depth), whole),
            pl.BlockSpec((depth, width), strip),
            pl.BlockSpec(downs.shape, whole),
            pl.BlockSpec((1, width), strip),
            pl.BlockSpec((rows, HEAD_DIM), whole),
            pl.BlockSpec((rows, HEAD_DIM), whole),
        ],
        out_specs=[
            pl.BlockSpec((rows, width), strip),
            pl.BlockSpec((rows, width), strip),
            pl.BlockSpec((1, width), strip),
            pl.BlockSpec((downs.shape[0], width), strip),
        ],
        out_shape=[
            jax.ShapeDtypeStruct((rows, columns), BF),
            jax.ShapeDtypeStruct((rows, columns), BF),
            jax.ShapeDtypeStruct((1, columns), F32),
            jax.ShapeDtypeStruct((downs.shape[0], columns), F32),
        ],
        compiler_params=pltpu.CompilerParams(vmem_limit_bytes=32 << 20),
        cost_estimate=pl.CostEstimate(
            flops=2 * rows * depth * columns, bytes_accessed=2 * depth * columns + 6 * rows * columns,
            transcendentals=columns,
        ),
        name="qkv_forward",
    )(h, weight, downs, magnitude, cosine, sine)


def softmax_block(q, k, bias):
    scores = nt(q, k) * HEAD_DIM ** (-0.5) + bias
    weights = jnp.exp(scores - jnp.max(scores, axis=-1, keepdims=True))
    return weights / jnp.sum(weights, axis=-1, keepdims=True)


def attend_kernel(q_ref, k_ref, v_ref, bias_ref, o_ref):
    probs = softmax_block(q_ref[...], k_ref[...], bias_ref[...])
    o_ref[...] = mm(probs.astype(BF), v_ref[...]).astype(BF)


def attend_back_kernel(q_ref, k_ref, v_ref, g_ref, bias_ref, dq_ref, dk_ref, dv_ref):
    q, k, g = q_ref[...], k_ref[...], g_ref[...]
    probs = softmax_block(q, k, bias_ref[...])
    grad = nt(g, v_ref[...])
    inner = jnp.sum(probs * grad, axis=-1, keepdims=True)
    raw = (probs * (grad - inner) * HEAD_DIM ** (-0.5)).astype(BF)
    dq_ref[...] = mm(raw, k)
    dk_ref[...] = tn(raw, q)
    dv_ref[...] = tn(probs.astype(BF), g)


def attention_call(kernel, name, heads, q, kv, offsets, extra, bias, outs):
    rows, keys = bias.shape
    head = lambda base: lambda j: (0, base + j)
    specs = [
        pl.BlockSpec((rows, HEAD_DIM), head(0)),
        pl.BlockSpec((keys, HEAD_DIM), head(offsets[0])),
        pl.BlockSpec((keys, HEAD_DIM), head(offsets[1])),
    ]
    specs += [pl.BlockSpec((rows, HEAD_DIM), head(0)) for _ in extra]
    specs.append(pl.BlockSpec((rows, keys), lambda j: (0, 0)))
    return pl.pallas_call(
        kernel,
        grid=(heads,),
        in_specs=specs,
        out_specs=[pl.BlockSpec((length, HEAD_DIM), head(0)) for length, _ in outs],
        out_shape=[jax.ShapeDtypeStruct((length, heads * HEAD_DIM), kind) for length, kind in outs],
        compiler_params=pltpu.CompilerParams(vmem_limit_bytes=48 << 20),
        cost_estimate=pl.CostEstimate(
            flops=4 * len(outs) * rows * keys * HEAD_DIM * heads,
            bytes_accessed=8 * rows * HEAD_DIM * heads, transcendentals=rows * keys * heads,
        ),
        name=name,
    )(q, kv, kv, *extra, bias)


def attend_back_turn_kernel(
    q_ref, k_ref, v_ref, g_ref, bias_ref, tq_ref, tk_ref, tv_ref, s_ref, r_ref, cos_ref, sin_ref, dt_ref, dm_ref
):
    q, k, g = q_ref[...], k_ref[...], g_ref[...]
    probs = softmax_block(q, k, bias_ref[...])
    grad = nt(g, v_ref[...])
    inner = jnp.sum(probs * grad, axis=-1, keepdims=True)
    raw = (probs * (grad - inner) * HEAD_DIM ** (-0.5)).astype(BF)
    cosine, sine = cos_ref[...], -sin_ref[...]
    plain = (turned(mm(raw, k), cosine, sine), turned(tn(raw, q), cosine, sine), tn(probs.astype(BF), g))
    for member, t_ref in enumerate((tq_ref, tk_ref, tv_ref)):
        dt_ref[member] = (plain[member] * s_ref[member]).astype(BF)
        dm_ref[member] = jnp.sum(plain[member] * t_ref[...].astype(F32), axis=0, keepdims=True) * r_ref[member]


def attend_back_turn(heads, qkv, grad, bias, t, factor, inverse, cosine, sine):
    rows = bias.shape[0]
    head = lambda base: lambda j: (0, base + j)
    whole = lambda j: (0, 0)
    block = lambda base: pl.BlockSpec((rows, HEAD_DIM), head(base))
    member = lambda j: (0, 0, j)
    return pl.pallas_call(
        attend_back_turn_kernel,
        grid=(heads,),
        in_specs=[
            block(0), block(heads), block(2 * heads), block(0),
            pl.BlockSpec((rows, rows), whole),
            block(0), block(heads), block(2 * heads),
            pl.BlockSpec((3, 1, HEAD_DIM), member),
            pl.BlockSpec((3, 1, HEAD_DIM), member),
            pl.BlockSpec((rows, HEAD_DIM), whole),
            pl.BlockSpec((rows, HEAD_DIM), whole),
        ],
        out_specs=[pl.BlockSpec((3, rows, HEAD_DIM), member), pl.BlockSpec((3, 1, HEAD_DIM), member)],
        out_shape=[
            jax.ShapeDtypeStruct((3, rows, heads * HEAD_DIM), BF),
            jax.ShapeDtypeStruct((3, 1, heads * HEAD_DIM), F32),
        ],
        compiler_params=pltpu.CompilerParams(vmem_limit_bytes=48 << 20),
        cost_estimate=pl.CostEstimate(
            flops=10 * rows * rows * HEAD_DIM * heads, bytes_accessed=20 * rows * HEAD_DIM * heads,
            transcendentals=rows * rows * heads,
        ),
        name="attend_back_turn",
    )(qkv, qkv, qkv, grad, bias, t, t, t, factor, inverse, cosine, sine)


def words_out(ref, start, value):
    rows, columns = value.shape
    for chunk in range(-(-columns // WORD)):
        left = chunk * WORD
        used = min(WORD, columns - left)
        ref[chunk, start : start + rows, :used] = value[:, left : left + used]
        if used < WORD:
            ref[chunk, start : start + rows, used:] = jnp.zeros((rows, WORD - used), F32)


def row_of(row, rows=8):
    return jnp.concatenate([row, jnp.zeros((rows - row.shape[0], row.shape[1]), F32)], axis=0)


def qkv_back_kernel(
    dt_ref, v_ref, h_ref, low_ref, up_ref, cross_ref, s_ref, n_ref, dm_ref, out_ref, shared_ref, core_ref, acc_ref
):
    member = pl.program_id(0)
    dt, weight = dt_ref[0], v_ref[...]
    rows = dt.shape[0]
    up = up_ref[0]
    pull = -s_ref[0] * dm_ref[0] / n_ref[0]
    stacked = nt(jnp.concatenate([dt, (up * pull).astype(BF)], axis=0), weight)
    update = stacked[:rows]

    @pl.when(member == 0)
    def _():
        acc_ref[...] = update

    @pl.when(member > 0)
    def _():
        acc_ref[...] += update

    @pl.when(member == pl.num_programs(0) - 1)
    def _():
        out_ref[...] = acc_ref[...].astype(BF)

    low_grad = nt(up.astype(BF), dt).astype(BF)
    words_out(shared_ref, 0, SCALE * (mm(low_grad, h_ref[...]) + stacked[rows:]))
    words_out(core_ref, 0, SCALE * (mm(low_ref[0], dt) + cross_ref[0] * pull))


def qkv_back(dt, weight, h, low, up, cross, factor, norm, dm):
    members, rows, columns = dt.shape
    width = h.shape[1]
    rank = up.shape[1]
    step = lambda j: (j, 0, 0)
    small = pl.BlockSpec((1, 1, columns), step)
    return pl.pallas_call(
        qkv_back_kernel,
        grid=(members,),
        in_specs=[
            pl.BlockSpec((1, rows, columns), step),
            pl.BlockSpec((width, columns), lambda j: (0, j)),
            pl.BlockSpec((rows, width), lambda j: (0, 0)),
            pl.BlockSpec((1, rank, rows), step),
            pl.BlockSpec((1, rank, columns), step),
            pl.BlockSpec((1, rank, columns), step),
            small, small, small,
        ],
        out_specs=[
            pl.BlockSpec((rows, width), lambda j: (0, 0)),
            pl.BlockSpec((width // WORD, rank, WORD), lambda j: (0, j, 0)),
            pl.BlockSpec((columns // WORD, rank, WORD), lambda j: (0, j, 0)),
        ],
        out_shape=[
            jax.ShapeDtypeStruct((rows, width), BF),
            jax.ShapeDtypeStruct((width // WORD, members * rank, WORD), F32),
            jax.ShapeDtypeStruct((columns // WORD, members * rank, WORD), F32),
        ],
        scratch_shapes=[pltpu.VMEM((rows, width), F32)],
        compiler_params=pltpu.CompilerParams(vmem_limit_bytes=48 << 20),
        cost_estimate=pl.CostEstimate(
            flops=2 * members * rows * columns * width, bytes_accessed=2 * members * width * columns,
            transcendentals=0,
        ),
        name="qkv_back",
    )(dt, weight, h, low, up, cross, factor, norm, dm)


def out_adapter_kernel(
    dt_ref, w_ref, u_ref, down_ref, up_ref, s_ref, n_ref, dm_ref, own_ref, shared_ref, core_ref
):
    inside = u_ref.shape[1]
    dt, u, up, down = dt_ref[...], u_ref[...], up_ref[...], down_ref[...]
    rank = up.shape[0]
    pull = -s_ref[...] * dm_ref[...] / n_ref[...]
    low_grad = nt(up.astype(BF), dt).astype(BF)
    frozen = (up * pull).astype(BF)
    sides = (slice(0, inside), slice(inside, 2 * inside))
    words_out(core_ref, 0, SCALE * (mm(low_grad, u) + sum(nt(frozen[:, part], w_ref[i]) for i, part in enumerate(sides))))
    low = nt(down, u).astype(BF)
    cross = jnp.concatenate([mm(down, w_ref[i]) for i in range(2)], axis=1)
    words_out(shared_ref, 0, SCALE * (mm(low, dt) + cross * pull))
    words_out(shared_ref, rank, row_of(own_ref[...]))


def out_adapter(dt, weight, u, down, up, factor, norm, dm_pair, dm_own):
    rank, width = up.shape
    inside = u.shape[1]
    return pl.pallas_call(
        out_adapter_kernel,
        out_shape=[
            jax.ShapeDtypeStruct((width // WORD, rank + 8, WORD), F32),
            jax.ShapeDtypeStruct((inside // WORD, rank, WORD), F32),
        ],
        compiler_params=pltpu.CompilerParams(vmem_limit_bytes=48 << 20),
        cost_estimate=pl.CostEstimate(
            flops=2 * width * inside * 256, bytes_accessed=2 * width * inside, transcendentals=0
        ),
        name="out_adapter",
    )(dt, weight, u, down, up, factor, norm, dm_pair, dm_own)


def chunks_of(columns, width):
    return [(left, min(left + width, columns)) for left in range(0, columns, width)]


def feed_prepare_kernel(
    index_ref, base_ref, cbase_ref, down_ref, up_ref, cdown_ref, cup_ref, out_ref, square_ref
):
    quarter = base_ref.shape[2]
    for member in range(2):
        merged_block = base_ref[member].astype(F32) + SCALE * mm(down_ref[member].astype(BF), up_ref[member].astype(BF))
        out_ref[0, :, member * quarter : (member + 1) * quarter] = merged_block.astype(BF)
    merged_block = cbase_ref[...].astype(F32) + SCALE * mm(cdown_ref[...].astype(BF), cup_ref[...].astype(BF))
    out_ref[0, :, 2 * quarter :] = merged_block.T.astype(BF)
    square_ref[0] = jnp.sum(merged_block * merged_block, axis=0, keepdims=True)


def feed_prepare(core, place, base, cbase, down, up, cdown, cup_columns):
    unit = base.shape[1]
    quarter = base.shape[2] // 4
    rank = up.shape[1]
    at = lambda i, index: 2 * i + index[0]
    return pl.pallas_call(
        feed_prepare_kernel,
        grid_spec=pltpu.PrefetchScalarGridSpec(
            num_scalar_prefetch=1,
            grid=(2,),
            in_specs=[
                pl.BlockSpec((2, unit, quarter), lambda i, index: (0, 0, at(i, index))),
                pl.BlockSpec((quarter, unit), lambda i, index: (at(i, index), 0)),
                pl.BlockSpec((2, unit, rank), lambda i, index: (0, index[1], 0)),
                pl.BlockSpec((2, rank, quarter), lambda i, index: (0, 0, at(i, index))),
                pl.BlockSpec((quarter, rank), lambda i, index: (at(i, index), 0)),
                pl.BlockSpec((rank, unit), lambda i, index: (0, 0)),
            ],
            out_specs=[
                pl.BlockSpec((1, unit, 3 * quarter), lambda i, index: (i, 0, 0)),
                pl.BlockSpec((1, 1, unit), lambda i, index: (i, 0, 0)),
            ],
        ),
        out_shape=[
            jax.ShapeDtypeStruct((2, unit, 3 * quarter), BF),
            jax.ShapeDtypeStruct((2, 1, unit), F32),
        ],
        cost_estimate=pl.CostEstimate(
            flops=12 * unit * quarter * rank, bytes_accessed=24 * unit * quarter, transcendentals=0
        ),
        name="feed_prepare",
    )(jnp.stack([core, place]).astype(jnp.int32), base, cbase, down, up, cdown, cup_columns)


def feed_kernel(
    known_norm, h_ref, h_pair_ref, g_ref, g_pair_ref, weight_ref, m_ref, norm_in_ref, gs_ref, down_ref, up_ref, cdown_ref,
    cup_ref, back_ref, back_pair_ref, out_ref, out_pair_ref, shared_ref, quad_ref, dm_ref, norm_ref, cross_ref,
    ccross_ref, we_ref, wc_ref, dt_ref, hid_ref, sems
):
    half, width = h_ref.shape
    block = 2 * half
    quarter = wc_ref.shape[1]
    rank = cup_ref.shape[0]
    parts = chunks_of(quarter, 512)

    def copies(index, left, right):
        target = ((we_ref, left), (we_ref, quarter + left), (wc_ref, left))
        return [
            pltpu.make_async_copy(
                weight_ref.at[:, pl.ds(kind * quarter + left, right - left)], vmem.at[:, pl.ds(start, right - left)],
                sems.at[3 * index + kind],
            )
            for kind, (vmem, start) in enumerate(target)
        ]

    for index, (left, right) in enumerate(parts):
        for copy in copies(index, left, right):
            copy.start()
    if known_norm:
        norm_ref[...] = norm_in_ref[...]
    dt_ref[block:, :] = jnp.zeros((2 * rank, 2 * quarter), BF)
    h = jnp.concatenate([h_ref[...], h_pair_ref[...]], axis=0)
    g = jnp.concatenate([g_ref[...], g_pair_ref[...]], axis=0)
    g = (g.astype(F32) * gs_ref[...]).astype(BF)
    inputs = h if known_norm else jnp.concatenate([h, down_ref[...]], axis=0)
    for index, (left, right) in enumerate(parts):
        near, far = slice(left, right), slice(quarter + left, quarter + right)

        for copy in copies(index, left, right):
            copy.wait()
        if not known_norm:
            for part in (near, far):
                wide = we_ref[:, part].astype(F32)
                norm_ref[:, part] = jnp.sqrt(jnp.sum(wide * wide, axis=0, keepdims=True))
        gate_t = mm(inputs, we_ref[:, near])
        up_t = mm(inputs, we_ref[:, far])
        if not known_norm:
            cross_ref[:, near], cross_ref[:, far] = gate_t[block:], up_t[block:]
            gate_t, up_t = gate_t[:block], up_t[:block]
        grad = mm(g, wc_ref[:, near])
        gate_s = m_ref[:, near] / norm_ref[:, near]
        up_s = m_ref[:, far] / norm_ref[:, far]
        gate = gate_t * gate_s
        up = up_t * up_s
        sigmoid = 1.0 / (1.0 + jnp.exp(-gate))
        silu = gate * sigmoid
        hid_ref[:, near] = (silu * up).astype(BF)
        up_grad = grad * silu
        gate_grad = grad * up * (sigmoid + silu * (1.0 - sigmoid))
        dm_ref[:, near] = jnp.sum(gate_grad * gate_t, axis=0, keepdims=True)
        dm_ref[:, far] = jnp.sum(up_grad * up_t, axis=0, keepdims=True)
        dt_ref[:block, near] = (gate_grad * gate_s).astype(BF)
        dt_ref[:block, far] = (up_grad * up_s).astype(BF)

    norm = norm_ref[...]
    pull = -m_ref[...] * dm_ref[...] / (norm * norm * norm)
    for member in range(2):
        part = slice(member * quarter, (member + 1) * quarter)
        dt_ref[block + member * rank : block + (member + 1) * rank, part] = (up_ref[member] * pull[:, part]).astype(BF)
    both = nt(dt_ref[...], we_ref[...])
    back_ref[...] = both[:half].astype(BF)
    back_pair_ref[...] = both[half:block].astype(BF)
    hidden = hid_ref[...]
    if known_norm:
        out = nt(hidden, wc_ref[...])
        cross_ref[...] = jnp.zeros_like(cross_ref)
        ccross_ref[...] = jnp.zeros_like(ccross_ref)
    else:
        out = nt(jnp.concatenate([hidden, cdown_ref[...]], axis=0), wc_ref[...])
        ccross_ref[...] = out[block:]
    out_ref[...] = out[:half].astype(BF)
    out_pair_ref[...] = out[half:block].astype(BF)
    low = nt(down_ref[...], h).astype(BF)
    low_grads = []
    for member in range(2):
        rows = slice(member * rank, (member + 1) * rank)
        dt = dt_ref[:block, member * quarter : (member + 1) * quarter]
        low_grads.append(nt(up_ref[member].astype(BF), dt).astype(BF))
        quad_ref[rows] = mm(low[rows], dt)
    shared_ref[: 2 * rank] = both[block:] + mm(jnp.concatenate(low_grads, axis=0), h)
    quad_ref[2 * rank :] = mm(nt(cup_ref[...], g).astype(BF), hidden)
    shared_ref[2 * rank :] = mm(nt(cdown_ref[...], hidden).astype(BF), g)


def feed_forward_back(h, h_pair, g, g_pair, weight, magnitude, norm, factor, down, up, cdown, cup):
    half, width = h.shape
    quarter = weight.shape[1] // 3
    double = 2 * quarter
    rank = cup.shape[0]
    block = 2 * half
    known = norm is not None
    vmem = pl.BlockSpec(memory_space=pltpu.VMEM)
    any_space = pl.BlockSpec(memory_space=pl.ANY)
    rows = jax.ShapeDtypeStruct((half, width), BF)
    return pl.pallas_call(
        functools.partial(feed_kernel, known),
        in_specs=[vmem] * 4 + [any_space] + [vmem] * 7,
        out_specs=[vmem] * 10,
        out_shape=[
            rows, rows, rows, rows,
            jax.ShapeDtypeStruct((3 * rank, width), F32),
            jax.ShapeDtypeStruct((3 * rank, quarter), F32),
            jax.ShapeDtypeStruct((1, double), F32),
            jax.ShapeDtypeStruct((1, double), F32),
            jax.ShapeDtypeStruct((2 * rank, double), F32),
            jax.ShapeDtypeStruct((rank, width), F32),
        ],
        scratch_shapes=[
            pltpu.VMEM((width, double), BF),
            pltpu.VMEM((width, quarter), BF),
            pltpu.VMEM((block + 2 * rank, double), BF),
            pltpu.VMEM((block, quarter), BF),
            pltpu.SemaphoreType.DMA((3 * len(chunks_of(quarter, 512)),)),
        ],
        compiler_params=pltpu.CompilerParams(vmem_limit_bytes=58 << 20),
        cost_estimate=pl.CostEstimate(
            flops=12 * block * width * quarter, bytes_accessed=6 * width * quarter + 8 * block * width,
            transcendentals=block * quarter,
        ),
        name="feed_forward_back",
    )(h, h_pair, g, g_pair, weight, magnitude, norm if known else magnitude, factor, down, up, cdown, cup)


def feed_adapter_kernel(
    shared_far_ref, shared_ref, quad_far_ref, quad_ref, cross_ref, ccross_ref, up_ref, cup_ref, contract_ref, pull_ref,
    dm_ref, cpull_ref, cdm_ref, out_ref, quad_out_ref
):
    rank = cup_ref.shape[0]
    quarter = contract_ref.shape[1]
    cpull = cpull_ref[...]
    shared = shared_far_ref[...] + shared_ref[...]
    quads = quad_far_ref[...] + quad_ref[...]
    words_out(out_ref, 0, SCALE * shared[: 2 * rank])
    words_out(out_ref, 2 * rank, SCALE * (shared[2 * rank :] + ccross_ref[...] * cpull))
    words_out(out_ref, 3 * rank, row_of(cdm_ref[...]))
    for member in range(2):
        part = slice(member * quarter, (member + 1) * quarter)
        rows = slice(member * rank, (member + 1) * rank)
        words_out(quad_out_ref, member * rank, SCALE * (quads[rows] + cross_ref[rows, part] * pull_ref[:, part]))
    frozen = mm((cup_ref[...].astype(F32) * cpull).astype(BF), contract_ref[...])
    words_out(quad_out_ref, 2 * rank, SCALE * (quads[2 * rank :] + frozen))
    both = jnp.concatenate([dm_ref[:, :quarter], dm_ref[:, quarter:]], axis=0)
    words_out(quad_out_ref, 3 * rank, row_of(both))


def feed_adapter(*operands):
    rank, width = operands[7].shape
    quarter = operands[8].shape[1] // 3
    specs = [pl.BlockSpec(memory_space=pltpu.VMEM) for _ in operands]
    specs[8] = pl.BlockSpec((width, quarter), lambda i: (0, 2))
    return pl.pallas_call(
        feed_adapter_kernel,
        grid=(1,),
        in_specs=specs,
        out_specs=[pl.BlockSpec(memory_space=pltpu.VMEM)] * 2,
        out_shape=[
            jax.ShapeDtypeStruct((width // WORD, 3 * rank + 8, WORD), F32),
            jax.ShapeDtypeStruct((-(-quarter // WORD), 3 * rank + 8, WORD), F32),
        ],
        compiler_params=pltpu.CompilerParams(vmem_limit_bytes=48 << 20),
        cost_estimate=pl.CostEstimate(
            flops=2 * 256 * width * quarter, bytes_accessed=3 * width * quarter, transcendentals=0
        ),
        name="feed_adapter",
    )(*operands)


def turn_back_kernel(rotated, g_ref, t_ref, s_ref, r_ref, cos_ref, sin_ref, dt_ref, dm_ref):
    grad = g_ref[...]

    def finish(plain):
        dt_ref[0] = (plain * s_ref[...]).astype(BF)
        dm_ref[...] = jnp.sum(plain * t_ref[...].astype(F32), axis=0, keepdims=True) * r_ref[...]

    @pl.when(pl.program_id(0) < rotated)
    def _():
        finish(turned(grad, cos_ref[...], -sin_ref[...]))

    @pl.when(pl.program_id(0) >= rotated)
    def _():
        finish(grad)


def turn_back(grads, t, factor, inverse, cosine, sine):
    rows, columns = t.shape
    whole = lambda j: (0, 0)
    strip = lambda j: (0, j)
    heads = columns // HEAD_DIM
    each = heads // 3
    return pl.pallas_call(
        functools.partial(turn_back_kernel, 2 * each),
        grid=(heads,),
        in_specs=[
            pl.BlockSpec((rows, HEAD_DIM), strip),
            pl.BlockSpec((rows, HEAD_DIM), strip),
            pl.BlockSpec((1, HEAD_DIM), strip),
            pl.BlockSpec((1, HEAD_DIM), strip),
            pl.BlockSpec((rows, HEAD_DIM), whole),
            pl.BlockSpec((rows, HEAD_DIM), whole),
        ],
        out_specs=[
            pl.BlockSpec((1, rows, HEAD_DIM), lambda j: (j // each, 0, j % each)),
            pl.BlockSpec((1, HEAD_DIM), strip),
        ],
        out_shape=[
            jax.ShapeDtypeStruct((3, rows, columns // 3), BF),
            jax.ShapeDtypeStruct((1, columns), F32),
        ],
        name="turn_back",
    )(grads, t, factor, inverse, cosine, sine)


def unpacked(words, columns):
    return jnp.concatenate([words[i] for i in range(words.shape[0])], axis=1)[:, :columns]


def pad_rows(a, multiple):
    short = -a.shape[0] % multiple
    return jnp.pad(a, ((0, short), (0, 0))) if short else a


def halve(a, name, index):
    parts = a.reshape(2, a.shape[0] // 2, a.shape[1])
    return take(parts, index, 0) + swap(take(parts, 1 - index, 0).astype(BF), name).astype(F32)


def join(a, name, index):
    return pair(a, swap(a, name), index).reshape(2 * a.shape[0], a.shape[1])


def spread(a, name):
    size, place = lax.axis_size(name), lax.axis_index(name)
    parts = a.reshape(size, a.shape[0] // size, a.shape[1])
    total = take(parts, place, 0)
    for step in range(1, size):
        total = total + shift(take(parts, (place + step) % size, 0).astype(BF), name, step).astype(F32)
    return total


def collect(a, name):
    size, place = lax.axis_size(name), lax.axis_index(name)
    buffer = jnp.zeros((size,) + a.shape, a.dtype)
    buffer = put(buffer, a, place, 0)
    for step in range(1, size):
        buffer = put(buffer, shift(a, name, step), (place - step) % size, 0)
    return buffer.reshape(size * a.shape[0], a.shape[1])


def reduce_all(shared, by_core, by_quad, first_beside, beside):
    c, x = lax.axis_index("core"), lax.axis_index("xx")
    unit = lax.axis_size("yy") * lax.axis_size("seq")
    half = halve(pad_rows(shared, 16), "core", c)
    quarter = halve(pad_rows(jnp.concatenate([half, by_core], axis=0), 16), "xx", x)
    last = pad_rows(jnp.concatenate([quarter, by_quad], axis=0), 8 * unit)
    last, first_beside = lax.optimization_barrier((last, first_beside))
    last = spread(spread(last, "yy"), "seq").astype(BF)
    last, beside = lax.optimization_barrier((last, beside))
    last = collect(collect(last, "seq"), "yy")
    joined = join(last[: quarter.shape[0]], "xx", x)
    everywhere = join(joined[: half.shape[0]], "core", c)
    mine = joined[half.shape[0] : half.shape[0] + by_core.shape[0]]
    cores = pair(mine, swap(mine, "core"), c)
    mine = last[quarter.shape[0] : quarter.shape[0] + by_quad.shape[0]]
    both = pair(mine, swap(mine, "xx"), x)
    quads = pair(both, swap(both, "core"), c, axis=1)
    return everywhere, cores, quads, first_beside, beside


def body(
    tokens,
    cotangent,
    attention_base,
    expand_base,
    contract_base,
    attention_down,
    attention_up,
    attention_magnitude,
    expand_down,
    expand_up,
    expand_magnitude,
    contract_down,
    contract_up,
    contract_magnitude,
    prompt_length,
    response_length,
):
    y, x = lax.axis_index("yy"), lax.axis_index("xx")
    c, z = lax.axis_index("core"), lax.axis_index("seq")
    ny, count = lax.axis_size("yy"), lax.axis_size("seq")
    own_rows, local, width = tokens.shape
    rows = 2 * own_rows
    split = count // rows
    piece = local // (2 * split)
    half = count * piece
    blocks = ny * 2
    rank = attention_down.shape[-1]
    unit = attention_base.shape[1]
    hidden_size = expand_base.shape[-1]
    quarter = hidden_size // 4
    place = ((y * 2 + x) * 2 + c) * count + z
    sub = z % split

    def by_core(a):
        shaped = a.reshape(a.shape[:-1] + (blocks, 2, a.shape[-1] // blocks // 2))
        axis = a.ndim
        flat = a.shape[:-1] + (a.shape[-1] // 2,)
        return take(shaped, c, axis).reshape(flat), take(shaped, 1 - c, axis).reshape(flat)

    def by_quarter(a):
        shaped = a.reshape(a.shape[:-1] + (4, quarter))
        return take(shaped, 2 * x + c, a.ndim - 1)

    down_rows = lax.dynamic_slice_in_dim(attention_down, place * unit, unit, 1)
    attention = merged(attention_base, down_rows, attention_up)
    mine, other = by_core(attention[:3])
    mine = mine.transpose(1, 0, 2).reshape(unit, -1)
    other = other.transpose(1, 0, 2).reshape(unit, -1)
    qkv_piece = pair(mine, swap(other, "core"), c)
    out_halves = jnp.stack([attention[3][:, : width // 2], attention[3][:, width // 2 :]])
    attention_piece = jnp.concatenate([qkv_piece, out_halves], axis=2)
    (
        attention_piece, tokens, cotangent, expand_base, contract_base, attention_down, attention_up,
        attention_magnitude, expand_down, expand_up, expand_magnitude, contract_down, contract_up, contract_magnitude,
        prompt_length, response_length,
    ) = lax.optimization_barrier((
        attention_piece, tokens, cotangent, expand_base, contract_base, attention_down, attention_up,
        attention_magnitude, expand_down, expand_up, expand_magnitude, contract_down, contract_up, contract_magnitude,
        prompt_length, response_length,
    ))

    def relayout_start(a):
        shaped = a.reshape(own_rows, split, 2, piece, width)
        kept, sent = take(shaped, c, 2), take(shaped, 1 - c, 2)
        return pair(kept, swap(sent, "core"), c).reshape(count, piece, width)

    contract_columns = lax.dynamic_slice_in_dim(contract_up, place * unit, unit, 1)
    prepare = lambda core: feed_prepare(
        core, place, expand_base, contract_base, expand_down, expand_up, contract_down, contract_columns
    )
    feed_other, square_other = prepare(1 - c)
    feed_mine, square_mine = prepare(c)
    feed_other = swap(feed_other, "core")
    feed_near = pair(take(feed_mine, x, 0), take(feed_other, x, 0), c)
    feed_far = pair(take(feed_mine, 1 - x, 0), take(feed_other, 1 - x, 0), c)

    boxes = {
        "a0": Box(attention_piece),
        "m0": Box(feed_near),
        "feed": Box(feed_far),
        "tokens": Box(relayout_start(tokens)),
        "cotangent": Box(relayout_start(cotangent)),
    }
    inside = width // 2

    def qkv_place(turn, column, step):
        def of(block):
            part = block[..., : 3 * inside].reshape(1, 1, 2, 1, unit, 3 * inside)
            return part, [(y - turn) % ny, column, 0, (z - step) % count, 0, 0]

        return of

    def out_place(turn, column, step):
        def of(block):
            part = block[..., 3 * inside :].reshape(2, 1, 1, 1, unit, inside)
            return part, [0, (y - turn) % ny, column, (z - step) % count, 0, 0]

        return of

    def feed_place(turn, index, step):
        def of(block):
            return block.reshape(1, 1, 2, 1, unit, 3 * quarter), [(y - turn) % ny, index, 0, (z - step) % count, 0, 0]

        return of

    qkv_places, out_places, feed_places = {}, {}, {}
    for step in range(count):
        for turn in range(ny):
            tail = f"{step}y{turn}" if turn else f"{step}"
            for name, column in (("a" + tail, x), ("a" + tail + "x", 1 - x)):
                qkv_places[name] = qkv_place(turn, column, step)
                out_places[name] = out_place(turn, column, step)
            for index, side in ((x, "m"), (1 - x, "n")):
                feed_places[side + tail] = feed_place(turn, index, step)
    buffers = {
        "qkv": Buffer((ny, 2, 2, count, unit, 3 * inside), 4, qkv_places),
        "out": Buffer((2, ny, 2, count, unit, inside), 4, out_places),
        "feed": Buffer((ny, 2, 2, count, unit, 3 * quarter), 0, feed_places),
    }
    for name in ("qkv", "out"):
        buffers[name].put("a0", attention_piece)
    buffers["feed"].put("m0", feed_near)
    links = Links(2, boxes, buffers)
    cross_x = lambda a: swap(a, "xx")
    ring = lambda a: shift(a, "seq", 1)
    exchange = lambda a: lax.all_to_all(a, "seq", 0, 0, tiled=True)
    turns = range(1, ny)

    def moves_y(kind, step):
        return [(f"{kind}{step}", f"{kind}{step}y{turn}", functools.partial(shift, name="yy", step=turn)) for turn in turns]

    sides = "mn"
    back = lambda a: shift(a, "seq", -1)
    order = []
    for step in range(1, count):
        order.append((step - 1, step, ring))
    attention_z = [(f"a{source}", f"a{step}", move) for source, step, move in order]
    feed_z = [(f"{side}{source}", f"{side}{step}", move) for source, step, move in order for side in sides]
    z_queue = attention_z[:2] + [("tokens", "tokens_moved", exchange), ("cotangent", "cotangent_moved", exchange)]
    z_queue += attention_z[2:] + feed_z
    x_queue = [("a0", "a0x", cross_x)]
    y_queue = []
    late_x = [("cotangent_moved", "cotangent_far", cross_x)]
    steps = [0] + [step for _, step, _ in order]
    feed_moves = [move for step in steps for side in sides for move in moves_y(side, step)]
    for place_of, step in enumerate(steps):
        names = [f"a{step}"] + [f"a{step}y{turn}" for turn in turns]
        x_queue += [(name, name + "x", cross_x) for name in names if name != "a0"]
        if step == 0:
            x_queue.append(("feed", "n0", cross_x))
        y_queue += moves_y("a", step)
        if place_of >= 1:
            y_queue += feed_moves[:1]
            del feed_moves[:1]
    y_queue += feed_moves

    x_queue += late_x
    links.run([z_queue, x_queue, y_queue])
    links.place(len(links.rounds) - 2)
    while qkv_places:
        links.place(links.placed + 1)
    qkv_weight = buffers["qkv"].array.reshape(width, 3 * inside)
    out_weight = buffers["out"].array.reshape(2, inside, inside)
    tokens_own = boxes["tokens_moved"].array.reshape(half, width)
    tokens_both = jnp.concatenate([tokens_own, swap(tokens_own, "core")], axis=0)
    cotangent_own = boxes["cotangent_moved"].array.reshape(half, width)
    cotangent_far = boxes["cotangent_far"].array.reshape(half, width)

    def positions_of(sub_place, core_place):
        source = jnp.arange(count, dtype=jnp.int32)[:, None] * local
        inner = sub_place * 2 * piece + core_place * piece + jnp.arange(piece, dtype=jnp.int32)[None]
        return (source + inner).reshape(half)

    query_place = jnp.concatenate([positions_of(sub, c), positions_of(sub, 1 - c)])
    key_place = jnp.concatenate(
        [positions_of((sub - step) % split, side) for step in range(split) for side in (c, 1 - c)]
    )
    totals = (prompt_length + response_length).astype(F32)
    total = take(pair(totals, swap(totals, "core"), c).reshape(rows), z // split, 0).astype(jnp.int32)
    allowed = (key_place[None] <= query_place[:, None]) & (key_place[None] < total)
    bias = jnp.where(allowed, 0.0, -1e30).astype(F32)
    frequency = 10000.0 ** (-jnp.arange(HEAD_DIM // 2).astype(F32) / (HEAD_DIM // 2))
    angles = query_place.astype(F32)[:, None] * frequency[None]
    cosine = jnp.concatenate([jnp.cos(angles)] * 2, axis=1)
    sine = jnp.concatenate([-jnp.sin(angles), jnp.sin(angles)], axis=1)

    heads = width // 2 // HEAD_DIM
    rows_both = tokens_both.astype(F32)
    first = rms(rows_both).astype(BF)
    magnitude = by_core(attention_magnitude[:3])[0].reshape(1, -1)
    downs = attention_down[:3].transpose(0, 2, 1).reshape(3 * rank, width).astype(BF)
    qkv_t, qkv_p, qkv_norm, cross = qkv_forward(first, qkv_weight, downs, magnitude, cosine, sine)

    def share(a, step):
        perm = [(i, (i // split) * split + (i % split + step) % split) for i in range(count)]
        return lax.ppermute(a, "seq", perm)

    feed_buffer = buffers["feed"]
    if split == 1:
        kv, offsets = qkv_p, (heads, 2 * heads)
    else:
        own_kv = qkv_p[:, heads * HEAD_DIM :]
        kv = jnp.concatenate([own_kv] + [share(own_kv, step) for step in range(1, split)], axis=0)
        offsets = (0, heads)
    (mixed,) = attention_call(
        attend_kernel, "attend", heads, qkv_p, kv, offsets, [], bias, [(2 * half, BF)]
    )

    def core_scatter(partial):
        return partial[:half].astype(F32) + swap(partial[half:].astype(BF), "core").astype(F32)

    def core_join(own):
        return jnp.concatenate([own, swap(own, "core")], axis=0)

    out_rows = by_core(attention_down[3].T)[0].astype(BF)
    contract_square = (square_other + square_mine).sum(axis=0)
    qkv_p, contract_square = lax.optimization_barrier((qkv_p, contract_square))
    contract_square = join(join(collect(contract_square, "seq"), "core", c), "xx", x)
    contract_square = collect(contract_square, "yy").reshape(1, width)
    mixed, cotangent_far, out_weight, feed_buffer.array = lax.optimization_barrier(
        (mixed, cotangent_far, out_weight, feed_buffer.array)
    )
    links.place(len(links.rounds))
    feed_weight = feed_buffer.array.reshape(width, 3 * quarter)
    out_square = jnp.sum(out_weight.astype(F32) ** 2, axis=1).reshape(1, width)
    out_norm = jnp.sqrt(out_square + swap(out_square, "core"))
    out_scale = attention_magnitude[3:] / out_norm
    out_sent = [mm(mixed[half:], out_weight[i]).astype(BF) for i in range(2)]
    out_sent = swap(jnp.concatenate(out_sent, axis=1), "core").astype(F32)
    out_t = jnp.concatenate([mm(mixed[:half], out_weight[i]) for i in range(2)], axis=1) + out_sent
    rows_own = tokens_own.astype(F32)
    middle = rows_own + out_t * out_scale
    second_own = rms(middle).astype(BF)
    second_far = swap(second_own, "xx")
    second_near = (second_own, swap(second_own, "core"))
    second_far = (second_far, swap(second_far, "core"))
    low = nt(downs, first).astype(BF).reshape(3, rank, 2 * half)
    cross = jnp.stack(
        [cross[i * rank : (i + 1) * rank, i * width // 2 : (i + 1) * width // 2] for i in range(3)]
    )
    second_far, cross, low = lax.optimization_barrier((second_far, cross, low))

    gate_up = jnp.stack([by_quarter(expand_up[i]) for i in range(2)])
    feed_downs = expand_down.transpose(0, 2, 1).reshape(2 * rank, width).astype(BF)
    contract_rows = take(contract_down.T.reshape(rank, 4, quarter), 2 * x + c, 1).astype(BF)
    contract_ups = contract_up.astype(BF)
    expand_magnitudes = by_quarter(expand_magnitude).reshape(1, -1)
    grad_own = cotangent_own.astype(F32)
    cotangent_near = (cotangent_own, swap(cotangent_own, "core"))
    cotangent_far = (cotangent_far, swap(cotangent_far, "core"))
    contract_norm = jnp.sqrt(contract_square)
    contract_scale = contract_magnitude[None] / contract_norm
    def total(kept, sent):
        return kept.astype(F32) + swap(sent, "core").astype(F32)

    (
        back_far, back_sent, out_far, out_sent, shared_far, quads_far, dm_far, expand_norm, expand_cross, contract_cross
    ) = feed_forward_back(
        *second_far, *cotangent_far, feed_weight, expand_magnitudes, None, contract_scale,
        feed_downs, gate_up, contract_rows, contract_ups,
    )
    back_far = total(back_far, back_sent).astype(BF)
    second_near, back_far = lax.optimization_barrier((second_near, back_far))
    back_near, back_sent, out_near, out_near_sent, shared_near, quads_near, dm_near = feed_forward_back(
        *second_near, *cotangent_near, feed_weight, expand_magnitudes, expand_norm, contract_scale,
        feed_downs, gate_up, contract_rows, contract_ups,
    )[:7]
    back_near, back_sent, back_far = lax.optimization_barrier((back_near, back_sent, swap(back_far, "xx")))
    second_grad = total(back_near, back_sent) + back_far.astype(F32)
    middle_grad = grad_own + rms_back(middle, second_grad)

    out_dm = jnp.sum(middle_grad * out_t, axis=0, keepdims=True) / out_norm
    out_dt = core_join((middle_grad * out_scale).astype(BF))
    mixed_grad = sum(nt(out_dt[:, i * inside : (i + 1) * inside], out_weight[i]) for i in range(2)).astype(BF)
    out_far, back_far = lax.optimization_barrier((total(out_far, out_sent).astype(BF), back_far))
    out_far = swap(out_far, "xx")
    keys = 2 * half * split
    members = lambda a: a.reshape(3, 1, width // 2)
    qkv_scale = magnitude / qkv_norm

    def reunite(a):
        parts = a.reshape(split, 2 * half, -1)
        total = parts[0]
        for step in range(1, split):
            total = total + share(parts[step].astype(BF), -step).astype(F32)
        return total

    if split > 1:
        dq, dk, dv = attention_call(
            attend_back_kernel, "attend_back", heads, qkv_p, kv, offsets, [mixed_grad], bias,
            [(2 * half, F32), (keys, F32), (keys, F32)],
        )
        grads = jnp.concatenate([dq, reunite(dk), reunite(dv)], axis=1)
        qkv_dt, qkv_dm = turn_back(grads, qkv_t, qkv_scale, 1.0 / qkv_norm, cosine, sine)
        qkv_dm = members(qkv_dm)
    else:
        qkv_dt, qkv_dm = attend_back_turn(
            heads, qkv_p, mixed_grad, bias, qkv_t, members(qkv_scale), members(1.0 / qkv_norm), cosine, sine
        )
    core_up = by_core(attention_up[:3])[0]
    def restore_start(own):
        return lax.all_to_all(own.reshape(count, piece, width), "seq", 0, 0, tiled=True)

    qkv_dt, out_far, out_near, out_near_sent = lax.optimization_barrier((qkv_dt, out_far, out_near, out_near_sent))
    contract_t = total(out_near, out_near_sent) + out_far.astype(F32)
    output_own = (middle + contract_t * contract_scale).astype(BF)
    layer_moved = restore_start(output_own)
    first_part, qkv_shared, qkv_core = qkv_back(
        qkv_dt, qkv_weight, first, low, core_up, cross, members(qkv_scale), members(qkv_norm), qkv_dm
    )
    first_grad = core_scatter(first_part)
    tokens_grad_own = middle_grad + rms_back(rows_own, first_grad)

    def restore_end(moved):
        shaped = moved.reshape(2, own_rows, split, piece, width)
        kept, sent = take(shaped, c, 0), take(shaped, 1 - c, 0)
        return pair(kept, swap(sent, "core"), c, axis=2).reshape(own_rows, local, width)

    expand_sum = dm_near + dm_far
    expand_pull = -expand_magnitudes * expand_sum / (expand_norm * expand_norm * expand_norm)
    contract_dm = jnp.sum(grad_own * contract_t, axis=0, keepdims=True) / contract_norm
    contract_sum = contract_dm + swap(contract_dm, "core")
    contract_sum = contract_sum + swap(contract_sum, "xx")
    contract_pull = -contract_scale * contract_sum / contract_norm
    feed_words, feed_quad_words = feed_adapter(
        shared_far, shared_near, quads_far, quads_near, expand_cross, contract_cross, gate_up, contract_ups,
        feed_weight, expand_pull, expand_sum / expand_norm, contract_pull, contract_dm,
    )
    flat = lambda a: a.reshape(-1, WORD)

    out_words, out_core_words = out_adapter(
        out_dt, out_weight, mixed, out_rows, attention_up[3], out_scale, out_norm,
        out_dm + swap(out_dm, "core"), out_dm,
    )
    dm_words = jnp.pad(qkv_dm[:, 0], ((0, 5), (0, 0)))
    dm_words = jnp.stack([dm_words[:, i : i + WORD] for i in range(0, width // 2, WORD)])
    shared = jnp.concatenate([flat(qkv_shared), flat(out_words), flat(feed_words)])
    cores = jnp.concatenate([flat(qkv_core), flat(dm_words), flat(out_core_words)])
    attention_shared, attention_cores, feed_quads, layer_moved, tokens_moved = reduce_all(
        shared, cores, flat(feed_quad_words), layer_moved, restore_start(tokens_grad_own.astype(BF))
    )
    used = flat(qkv_shared).shape[0] + flat(out_words).shape[0]
    feed_shared = attention_shared[used:]

    def interleave(parts):
        shaped = [p.reshape(p.shape[0], blocks, 1, -1) for p in parts]
        return jnp.concatenate(shaped, axis=2).reshape(parts[0].shape[0], -1)

    used = flat(qkv_shared).shape[0]
    qkv_down_all = unpacked(attention_shared[:used].reshape(qkv_shared.shape), width)
    out_all = unpacked(attention_shared[used : used + flat(out_words).shape[0]].reshape(out_words.shape), width)
    core_parts = []
    for side in range(2):
        start, parts = 0, []
        for words in (qkv_core, dm_words, out_core_words):
            used = flat(words).shape[0]
            parts.append(unpacked(attention_cores[side, start : start + used].reshape(words.shape), width // 2))
            start += used
        core_parts.append(parts)
    qkv_up_all, qkv_dm_all, out_down_all = (interleave([core_parts[0][i], core_parts[1][i]]) for i in range(3))
    attention_down_grad = (
        jnp.concatenate([qkv_down_all, out_down_all]).reshape(4, rank, width).transpose(0, 2, 1)
    )
    attention_up_grad = jnp.concatenate([qkv_up_all, out_all[:rank]]).reshape(4, rank, width)
    attention_magnitude_grad = jnp.concatenate([qkv_dm_all[:3], out_all[rank : rank + 1]])

    feed_all = unpacked(feed_shared[: flat(feed_words).shape[0]].reshape(feed_words.shape), width)
    quad_all = jnp.concatenate(
        [unpacked(feed_quads[i, j].reshape(feed_quad_words.shape), quarter) for i in range(2) for j in range(2)],
        axis=1,
    )

    layer_output = restore_end(layer_moved)
    tokens_grad = restore_end(tokens_moved).astype(F32)
    return (
        layer_output,
        tokens_grad,
        attention_down_grad.astype(F32),
        attention_up_grad.astype(F32),
        attention_magnitude_grad.astype(F32),
        feed_all[: 2 * rank].reshape(2, rank, width).transpose(0, 2, 1).astype(F32),
        quad_all[: 2 * rank].reshape(2, rank, hidden_size).astype(F32),
        quad_all[3 * rank : 3 * rank + 2].astype(F32),
        quad_all[2 * rank : 3 * rank].T.astype(F32),
        feed_all[2 * rank : 3 * rank].astype(F32),
        feed_all[3 * rank].astype(F32),
    )


def solution(mesh):
    devices = mesh.devices
    chips = devices.shape[0] // 2
    fine = Mesh(devices.reshape(chips // 2, 2, 2, devices.shape[1]), ALL)
    dp = ("yy", "xx", "core")
    every = ("yy", "xx", "core", "seq")
    placed = (
        P(dp, "seq", None),
        P(dp, "seq", None),
        P(None, every, None),
        P(None, every, None),
        P(None, every),
        P(),
        P(),
        P(),
        P(),
        P(),
        P(),
        P(),
        P(),
        P(),
        P(dp),
        P(dp),
    )
    return jax.shard_map(
        body,
        mesh=fine,
        in_specs=placed,
        out_specs=(P(dp, "seq", None), P(dp, "seq", None)) + (P(),) * 9,
        check_vma=False,
    )
```

```python
import functools

import jax
import jax.numpy as jnp
from jax import lax
from jax.experimental import pallas as pl
from jax.experimental.pallas import tpu as pltpu
from jax.sharding import Mesh
from jax.sharding import PartitionSpec as P

HEAD_DIM = 128
SCALE = 2.0
BF = jnp.bfloat16
F32 = jnp.float32
ALL = ("yy", "xx", "core", "seq")
WORD = 512


def mm(a, b, dims=((1,), (0,))):
    return lax.dot_general(a, b, (dims, ((), ())), preferred_element_type=F32)


def nt(a, b):
    return mm(a, b, ((1,), (1,)))


def tn(a, b):
    return mm(a, b, ((0,), (0,)))


def take(a, index, axis):
    return lax.dynamic_index_in_dim(a, index, axis, keepdims=False)


def swap(a, name):
    return lax.ppermute(a, name, [(0, 1), (1, 0)])


def shift(a, name, step):
    size = lax.axis_size(name)
    return lax.ppermute(a, name, [(i, (i + step) % size) for i in range(size)])


def pair(mine, other, index, axis=0):
    first = jnp.where(index == 0, mine, other)
    second = jnp.where(index == 0, other, mine)
    return jnp.stack([first, second], axis=axis)


def put(buffer, block, index, axis):
    return lax.dynamic_update_slice_in_dim(buffer, jnp.expand_dims(block, axis), index, axis)


def rms(v):
    return v * lax.rsqrt(jnp.mean(v * v, axis=-1, keepdims=True) + 1e-05)


def rms_back(v, grad):
    inverse = lax.rsqrt(jnp.mean(v * v, axis=-1, keepdims=True) + 1e-05)
    inner = jnp.mean(v * grad, axis=-1, keepdims=True)
    return grad * inverse - v * (inner * inverse * inverse * inverse)


def merged(base, down, up):
    product = lax.dot_general(
        down.astype(BF), up.astype(BF), (((down.ndim - 1,), (up.ndim - 2,)), (tuple(range(down.ndim - 2)),) * 2),
        preferred_element_type=F32,
    )
    return (base.astype(F32) + SCALE * product).astype(BF)


class Box:
    def __init__(self, array):
        self.array = self.raw = array


class Links:
    def __init__(self, depth, boxes, buffers):
        self.depth = depth
        self.boxes = boxes
        self.buffers = buffers
        self.rounds = []
        self.placed = 0
        self.derived = []

    def run(self, queues):
        boxes = self.boxes
        while any(queues):
            for name, sources, join_of in [e for e in self.derived if all(n in boxes for n in e[1])]:
                boxes[name] = Box(join_of(*[boxes[n].array for n in sources]))
            self.derived = [e for e in self.derived if e[0] not in boxes]
            ready = set(boxes)
            self.rounds.append([])
            for queue in queues:
                for place, (source, result, move) in enumerate(queue):
                    if source in ready:
                        queue.pop(place)
                        self.send(boxes, source, result, move)
                        break
            self.place(len(self.rounds) - self.depth)

    def place(self, until):
        while self.placed < until:
            for name, box in self.rounds[self.placed]:
                for buffer in self.buffers.values():
                    buffer.put(name, box.raw)
            self.placed += 1

    def send(self, boxes, source, result, move):
        box = boxes[source]
        if len(self.rounds) > self.depth:
            old = [b for name, b in self.rounds[-1 - self.depth] if b is not box and "_" not in name]
            if len(self.rounds) > 4:
                old += [b for name, b in self.rounds[-5] if b is not box and "_" in name]
            held = [b for b in self.buffers.values() if b.pending()]
            both = lax.optimization_barrier((box.array, [b.array for b in old], [b.array for b in held]))
            box.array = both[0]
            for b, array in zip(old + held, both[1] + both[2]):
                b.array = array
        boxes[result] = Box(move(box.array))
        self.rounds[-1].append((result, boxes[result]))


class Buffer:
    def __init__(self, shape, free, blocks):
        self.array = unwritten(shape, BF)
        self.free = free
        self.blocks = blocks

    def pending(self):
        return len(self.blocks) > self.free

    def put(self, name, block):
        if name in self.blocks:
            part, start = self.blocks.pop(name)(block)
            self.array = lax.dynamic_update_slice(self.array, part, [jnp.int32(v) for v in start])


def unwritten(shape, kind):
    return pl.pallas_call(
        lambda ref: None, out_shape=jax.ShapeDtypeStruct(shape, kind),
        out_specs=pl.BlockSpec(memory_space=pl.ANY), name="unwritten",
    )()


def turned(v, cosine, sine):
    return v * cosine + pltpu.roll(v, HEAD_DIM // 2, 1) * sine


def qkv_kernel(rotated, h_ref, v_ref, down_ref, m_ref, cos_ref, sin_ref, t_ref, p_ref, n_ref, cross_ref):
    block = v_ref[...]
    rows = h_ref.shape[0]
    both = jnp.dot(jnp.concatenate([h_ref[...], down_ref[...]], axis=0), block, preferred_element_type=F32)
    cross_ref[...] = both[rows:]
    t = both[:rows]
    wide = block.astype(F32)
    norm = jnp.sqrt(jnp.sum(wide * wide, axis=0, keepdims=True))
    n_ref[...] = norm
    t_ref[...] = t.astype(BF)
    scaled = t * (m_ref[...] / norm)

    @pl.when(pl.program_id(0) < rotated)
    def _():
        for part in range(t.shape[1] // HEAD_DIM):
            columns = slice(part * HEAD_DIM, (part + 1) * HEAD_DIM)
            p_ref[:, columns] = turned(scaled[:, columns], cos_ref[...], sin_ref[...]).astype(BF)

    @pl.when(pl.program_id(0) >= rotated)
    def _():
        p_ref[...] = scaled.astype(BF)


def qkv_forward(h, weight, downs, magnitude, cosine, sine):
    rows, depth = h.shape
    columns = magnitude.shape[1]
    width = 2 * HEAD_DIM
    rotated = columns * 2 // 3 // width
    whole = lambda j: (0, 0)
    strip = lambda j: (0, j)
    return pl.pallas_call(
        functools.partial(qkv_kernel, rotated),
        grid=(columns // width,),
        in_specs=[
            pl.BlockSpec((rows, depth), whole),
            pl.BlockSpec((depth, width), strip),
            pl.BlockSpec(downs.shape, whole),
            pl.BlockSpec((1, width), strip),
            pl.BlockSpec((rows, HEAD_DIM), whole),
            pl.BlockSpec((rows, HEAD_DIM), whole),
        ],
        out_specs=[
            pl.BlockSpec((rows, width), strip),
            pl.BlockSpec((rows, width), strip),
            pl.BlockSpec((1, width), strip),
            pl.BlockSpec((downs.shape[0], width), strip),
        ],
        out_shape=[
            jax.ShapeDtypeStruct((rows, columns), BF),
            jax.ShapeDtypeStruct((rows, columns), BF),
            jax.ShapeDtypeStruct((1, columns), F32),
            jax.ShapeDtypeStruct((downs.shape[0], columns), F32),
        ],
        compiler_params=pltpu.CompilerParams(vmem_limit_bytes=32 << 20),
        cost_estimate=pl.CostEstimate(
            flops=2 * rows * depth * columns, bytes_accessed=2 * depth * columns + 6 * rows * columns,
            transcendentals=columns,
        ),
        name="qkv_forward",
    )(h, weight, downs, magnitude, cosine, sine)


def softmax_block(q, k, bias):
    scores = nt(q, k) * HEAD_DIM ** (-0.5) + bias
    weights = jnp.exp(scores - jnp.max(scores, axis=-1, keepdims=True))
    return weights / jnp.sum(weights, axis=-1, keepdims=True)


def attend_kernel(q_ref, k_ref, v_ref, bias_ref, o_ref):
    probs = softmax_block(q_ref[...], k_ref[...], bias_ref[...])
    o_ref[...] = mm(probs.astype(BF), v_ref[...]).astype(BF)


def attend_back_kernel(q_ref, k_ref, v_ref, g_ref, bias_ref, dq_ref, dk_ref, dv_ref):
    q, k, g = q_ref[...], k_ref[...], g_ref[...]
    probs = softmax_block(q, k, bias_ref[...])
    grad = nt(g, v_ref[...])
    inner = jnp.sum(probs * grad, axis=-1, keepdims=True)
    raw = (probs * (grad - inner) * HEAD_DIM ** (-0.5)).astype(BF)
    dq_ref[...] = mm(raw, k)
    dk_ref[...] = tn(raw, q)
    dv_ref[...] = tn(probs.astype(BF), g)


def attention_call(kernel, name, heads, q, kv, offsets, extra, bias, outs):
    rows, keys = bias.shape
    head = lambda base: lambda j: (0, base + j)
    specs = [
        pl.BlockSpec((rows, HEAD_DIM), head(0)),
        pl.BlockSpec((keys, HEAD_DIM), head(offsets[0])),
        pl.BlockSpec((keys, HEAD_DIM), head(offsets[1])),
    ]
    specs += [pl.BlockSpec((rows, HEAD_DIM), head(0)) for _ in extra]
    specs.append(pl.BlockSpec((rows, keys), lambda j: (0, 0)))
    return pl.pallas_call(
        kernel,
        grid=(heads,),
        in_specs=specs,
        out_specs=[pl.BlockSpec((length, HEAD_DIM), head(0)) for length, _ in outs],
        out_shape=[jax.ShapeDtypeStruct((length, heads * HEAD_DIM), kind) for length, kind in outs],
        compiler_params=pltpu.CompilerParams(vmem_limit_bytes=48 << 20),
        cost_estimate=pl.CostEstimate(
            flops=4 * len(outs) * rows * keys * HEAD_DIM * heads,
            bytes_accessed=8 * rows * HEAD_DIM * heads, transcendentals=rows * keys * heads,
        ),
        name=name,
    )(q, kv, kv, *extra, bias)


def middle_back_kernel(
    near_ref, pair_ref, far_ref, g_ref, middle_ref, t_ref, s_ref, n_ref, grad_ref, dt_ref, dm_ref
):
    second = near_ref[...].astype(F32) + pair_ref[...].astype(F32) + far_ref[...].astype(F32)
    grad = g_ref[...].astype(F32) + rms_back(middle_ref[...], second)
    grad_ref[...] = grad
    dt_ref[...] = (grad * s_ref[...]).astype(BF)
    part = jnp.sum(grad * t_ref[...], axis=0, keepdims=True) / n_ref[...]

    @pl.when(pl.program_id(0) == 0)
    def _():
        dm_ref[...] = part

    @pl.when(pl.program_id(0) > 0)
    def _():
        dm_ref[...] += part


def middle_back(near, pair_part, far, g, middle, t, factor, norm):
    rows, width = middle.shape
    block = rows // 4
    row = pl.BlockSpec((block, width), lambda i: (i, 0))
    one = pl.BlockSpec((1, width), lambda i: (0, 0))
    return pl.pallas_call(
        middle_back_kernel,
        grid=(rows // block,),
        in_specs=[row] * 6 + [one] * 2,
        out_specs=[row, row, one],
        out_shape=[
            jax.ShapeDtypeStruct((rows, width), F32),
            jax.ShapeDtypeStruct((rows, width), BF),
            jax.ShapeDtypeStruct((1, width), F32),
        ],
        cost_estimate=pl.CostEstimate(flops=20 * rows * width, bytes_accessed=24 * rows * width, transcendentals=rows),
        name="middle_back",
    )(near, pair_part, far, g, middle, t, factor, norm)


def attend_back_turn_kernel(
    q_ref, k_ref, v_ref, g_ref, bias_ref, tq_ref, tk_ref, tv_ref, s_ref, r_ref, cos_ref, sin_ref, dt_ref, dm_ref
):
    q, k, g = q_ref[...], k_ref[...], g_ref[...]
    probs = softmax_block(q, k, bias_ref[...])
    grad = nt(g, v_ref[...])
    inner = jnp.sum(probs * grad, axis=-1, keepdims=True)
    raw = (probs * (grad - inner) * HEAD_DIM ** (-0.5)).astype(BF)
    cosine, sine = cos_ref[...], -sin_ref[...]
    plain = (turned(mm(raw, k), cosine, sine), turned(tn(raw, q), cosine, sine), tn(probs.astype(BF), g))
    for member, t_ref in enumerate((tq_ref, tk_ref, tv_ref)):
        dt_ref[member] = (plain[member] * s_ref[member]).astype(BF)
        dm_ref[member] = jnp.sum(plain[member] * t_ref[...].astype(F32), axis=0, keepdims=True) * r_ref[member]


def attend_back_turn(heads, qkv, grad, bias, t, factor, inverse, cosine, sine):
    rows = bias.shape[0]
    head = lambda base: lambda j: (0, base + j)
    whole = lambda j: (0, 0)
    block = lambda base: pl.BlockSpec((rows, HEAD_DIM), head(base))
    member = lambda j: (0, 0, j)
    return pl.pallas_call(
        attend_back_turn_kernel,
        grid=(heads,),
        in_specs=[
            block(0), block(heads), block(2 * heads), block(0),
            pl.BlockSpec((rows, rows), whole),
            block(0), block(heads), block(2 * heads),
            pl.BlockSpec((3, 1, HEAD_DIM), member),
            pl.BlockSpec((3, 1, HEAD_DIM), member),
            pl.BlockSpec((rows, HEAD_DIM), whole),
            pl.BlockSpec((rows, HEAD_DIM), whole),
        ],
        out_specs=[pl.BlockSpec((3, rows, HEAD_DIM), member), pl.BlockSpec((3, 1, HEAD_DIM), member)],
        out_shape=[
            jax.ShapeDtypeStruct((3, rows, heads * HEAD_DIM), BF),
            jax.ShapeDtypeStruct((3, 1, heads * HEAD_DIM), F32),
        ],
        compiler_params=pltpu.CompilerParams(vmem_limit_bytes=48 << 20),
        cost_estimate=pl.CostEstimate(
            flops=10 * rows * rows * HEAD_DIM * heads, bytes_accessed=20 * rows * HEAD_DIM * heads,
            transcendentals=rows * rows * heads,
        ),
        name="attend_back_turn",
    )(qkv, qkv, qkv, grad, bias, t, t, t, factor, inverse, cosine, sine)


def words_out(ref, start, value):
    rows, columns = value.shape
    for chunk in range(-(-columns // WORD)):
        left = chunk * WORD
        used = min(WORD, columns - left)
        ref[chunk, start : start + rows, :used] = value[:, left : left + used]
        if used < WORD:
            ref[chunk, start : start + rows, used:] = jnp.zeros((rows, WORD - used), F32)


def row_of(row, rows=8):
    return jnp.concatenate([row, jnp.zeros((rows - row.shape[0], row.shape[1]), F32)], axis=0)


def qkv_back_kernel(
    dt_ref, v_ref, h_ref, low_ref, up_ref, cross_ref, s_ref, n_ref, dm_ref, out_ref, shared_ref, core_ref, acc_ref
):
    member = pl.program_id(0)
    dt, weight = dt_ref[0], v_ref[...]
    rows = dt.shape[0]
    up = up_ref[0]
    pull = -s_ref[0] * dm_ref[0] / n_ref[0]
    stacked = nt(jnp.concatenate([dt, (up * pull).astype(BF)], axis=0), weight)
    update = stacked[:rows]

    @pl.when(member == 0)
    def _():
        acc_ref[...] = update

    @pl.when(member > 0)
    def _():
        acc_ref[...] += update

    @pl.when(member == pl.num_programs(0) - 1)
    def _():
        out_ref[...] = acc_ref[...].astype(BF)

    low_grad = nt(up.astype(BF), dt).astype(BF)
    words_out(shared_ref, 0, SCALE * (mm(low_grad, h_ref[...]) + stacked[rows:]))
    words_out(core_ref, 0, SCALE * (mm(low_ref[0], dt) + cross_ref[0] * pull))


def qkv_back(dt, weight, h, low, up, cross, factor, norm, dm):
    members, rows, columns = dt.shape
    width = h.shape[1]
    rank = up.shape[1]
    step = lambda j: (j, 0, 0)
    small = pl.BlockSpec((1, 1, columns), step)
    return pl.pallas_call(
        qkv_back_kernel,
        grid=(members,),
        in_specs=[
            pl.BlockSpec((1, rows, columns), step),
            pl.BlockSpec((width, columns), lambda j: (0, j)),
            pl.BlockSpec((rows, width), lambda j: (0, 0)),
            pl.BlockSpec((1, rank, rows), step),
            pl.BlockSpec((1, rank, columns), step),
            pl.BlockSpec((1, rank, columns), step),
            small, small, small,
        ],
        out_specs=[
            pl.BlockSpec((rows, width), lambda j: (0, 0)),
            pl.BlockSpec((width // WORD, rank, WORD), lambda j: (0, j, 0)),
            pl.BlockSpec((columns // WORD, rank, WORD), lambda j: (0, j, 0)),
        ],
        out_shape=[
            jax.ShapeDtypeStruct((rows, width), BF),
            jax.ShapeDtypeStruct((width // WORD, members * rank, WORD), F32),
            jax.ShapeDtypeStruct((columns // WORD, members * rank, WORD), F32),
        ],
        scratch_shapes=[pltpu.VMEM((rows, width), F32)],
        compiler_params=pltpu.CompilerParams(vmem_limit_bytes=48 << 20),
        cost_estimate=pl.CostEstimate(
            flops=2 * members * rows * columns * width, bytes_accessed=2 * members * width * columns,
            transcendentals=0,
        ),
        name="qkv_back",
    )(dt, weight, h, low, up, cross, factor, norm, dm)


def out_adapter_kernel(
    dt_ref, w_ref, u_ref, down_ref, up_ref, s_ref, n_ref, dm_ref, own_ref, shared_ref, core_ref
):
    inside = u_ref.shape[1]
    dt, u, up, down = dt_ref[...], u_ref[...], up_ref[...], down_ref[...]
    rank = up.shape[0]
    pull = -s_ref[...] * dm_ref[...] / n_ref[...]
    low_grad = nt(up.astype(BF), dt).astype(BF)
    frozen = (up * pull).astype(BF)
    sides = (slice(0, inside), slice(inside, 2 * inside))
    words_out(core_ref, 0, SCALE * (mm(low_grad, u) + sum(nt(frozen[:, part], w_ref[i]) for i, part in enumerate(sides))))
    low = nt(down, u).astype(BF)
    cross = jnp.concatenate([mm(down, w_ref[i]) for i in range(2)], axis=1)
    words_out(shared_ref, 0, SCALE * (mm(low, dt) + cross * pull))
    words_out(shared_ref, rank, row_of(own_ref[...]))


def out_adapter(dt, weight, u, down, up, factor, norm, dm_pair, dm_own):
    rank, width = up.shape
    inside = u.shape[1]
    return pl.pallas_call(
        out_adapter_kernel,
        out_shape=[
            jax.ShapeDtypeStruct((width // WORD, rank + 8, WORD), F32),
            jax.ShapeDtypeStruct((inside // WORD, rank, WORD), F32),
        ],
        compiler_params=pltpu.CompilerParams(vmem_limit_bytes=48 << 20),
        cost_estimate=pl.CostEstimate(
            flops=2 * width * inside * 256, bytes_accessed=2 * width * inside, transcendentals=0
        ),
        name="out_adapter",
    )(dt, weight, u, down, up, factor, norm, dm_pair, dm_own)


def chunks_of(columns, width):
    return [(left, min(left + width, columns)) for left in range(0, columns, width)]


def feed_prepare_kernel(
    index_ref, base_ref, cbase_ref, down_ref, up_ref, cdown_ref, cup_ref, out_ref, square_ref
):
    quarter = base_ref.shape[2]
    for member in range(2):
        merged_block = base_ref[member].astype(F32) + SCALE * mm(down_ref[member].astype(BF), up_ref[member].astype(BF))
        out_ref[0, :, member * quarter : (member + 1) * quarter] = merged_block.astype(BF)
    merged_block = cbase_ref[...].astype(F32) + SCALE * mm(cdown_ref[...].astype(BF), cup_ref[...].astype(BF))
    out_ref[0, :, 2 * quarter :] = merged_block.T.astype(BF)
    square_ref[0] = jnp.sum(merged_block * merged_block, axis=0, keepdims=True)


def feed_prepare(core, place, base, cbase, down, up, cdown, cup_columns):
    unit = base.shape[1]
    quarter = base.shape[2] // 4
    rank = up.shape[1]
    at = lambda i, index: 2 * i + index[0]
    return pl.pallas_call(
        feed_prepare_kernel,
        grid_spec=pltpu.PrefetchScalarGridSpec(
            num_scalar_prefetch=1,
            grid=(2,),
            in_specs=[
                pl.BlockSpec((2, unit, quarter), lambda i, index: (0, 0, at(i, index))),
                pl.BlockSpec((quarter, unit), lambda i, index: (at(i, index), 0)),
                pl.BlockSpec((2, unit, rank), lambda i, index: (0, index[1], 0)),
                pl.BlockSpec((2, rank, quarter), lambda i, index: (0, 0, at(i, index))),
                pl.BlockSpec((quarter, rank), lambda i, index: (at(i, index), 0)),
                pl.BlockSpec((rank, unit), lambda i, index: (0, 0)),
            ],
            out_specs=[
                pl.BlockSpec((1, unit, 3 * quarter), lambda i, index: (i, 0, 0)),
                pl.BlockSpec((1, 1, unit), lambda i, index: (i, 0, 0)),
            ],
        ),
        out_shape=[
            jax.ShapeDtypeStruct((2, unit, 3 * quarter), BF),
            jax.ShapeDtypeStruct((2, 1, unit), F32),
        ],
        cost_estimate=pl.CostEstimate(
            flops=12 * unit * quarter * rank, bytes_accessed=24 * unit * quarter, transcendentals=0
        ),
        name="feed_prepare",
    )(jnp.stack([core, place]).astype(jnp.int32), base, cbase, down, up, cdown, cup_columns)


def feed_kernel(
    known_norm, h_ref, h_pair_ref, g_ref, g_pair_ref, weight_ref, m_ref, norm_in_ref, gs_ref, down_ref, up_ref, cdown_ref,
    cup_ref, back_ref, back_pair_ref, out_ref, out_pair_ref, shared_ref, quad_ref, dm_ref, norm_ref, cross_ref,
    ccross_ref, we_ref, wc_ref, dt_ref, hid_ref, sems
):
    half, width = h_ref.shape
    block = 2 * half
    quarter = wc_ref.shape[1]
    rank = cup_ref.shape[0]
    parts = chunks_of(quarter, 512)

    def copies(index, left, right):
        target = ((we_ref, left), (we_ref, quarter + left), (wc_ref, left))
        return [
            pltpu.make_async_copy(
                weight_ref.at[:, pl.ds(kind * quarter + left, right - left)], vmem.at[:, pl.ds(start, right - left)],
                sems.at[3 * index + kind],
            )
            for kind, (vmem, start) in enumerate(target)
        ]

    for index, (left, right) in enumerate(parts):
        for copy in copies(index, left, right):
            copy.start()
    if known_norm:
        norm_ref[...] = norm_in_ref[...]
    dt_ref[block:, :] = jnp.zeros((2 * rank, 2 * quarter), BF)
    h = jnp.concatenate([h_ref[...], h_pair_ref[...]], axis=0)
    g = jnp.concatenate([g_ref[...], g_pair_ref[...]], axis=0)
    g = (g.astype(F32) * gs_ref[...]).astype(BF)
    inputs = h if known_norm else jnp.concatenate([h, down_ref[...]], axis=0)
    for index, (left, right) in enumerate(parts):
        near, far = slice(left, right), slice(quarter + left, quarter + right)

        for copy in copies(index, left, right):
            copy.wait()
        if not known_norm:
            for part in (near, far):
                wide = we_ref[:, part].astype(F32)
                norm_ref[:, part] = jnp.sqrt(jnp.sum(wide * wide, axis=0, keepdims=True))
        gate_t = mm(inputs, we_ref[:, near])
        up_t = mm(inputs, we_ref[:, far])
        if not known_norm:
            cross_ref[:, near], cross_ref[:, far] = gate_t[block:], up_t[block:]
            gate_t, up_t = gate_t[:block], up_t[:block]
        grad = mm(g, wc_ref[:, near])
        gate_s = m_ref[:, near] / norm_ref[:, near]
        up_s = m_ref[:, far] / norm_ref[:, far]
        gate = gate_t * gate_s
        up = up_t * up_s
        sigmoid = 1.0 / (1.0 + jnp.exp(-gate))
        silu = gate * sigmoid
        hid_ref[:, near] = (silu * up).astype(BF)
        up_grad = grad * silu
        gate_grad = grad * up * (sigmoid + silu * (1.0 - sigmoid))
        dm_ref[:, near] = jnp.sum(gate_grad * gate_t, axis=0, keepdims=True)
        dm_ref[:, far] = jnp.sum(up_grad * up_t, axis=0, keepdims=True)
        dt_ref[:block, near] = (gate_grad * gate_s).astype(BF)
        dt_ref[:block, far] = (up_grad * up_s).astype(BF)

    norm = norm_ref[...]
    pull = -m_ref[...] * dm_ref[...] / (norm * norm * norm)
    for member in range(2):
        part = slice(member * quarter, (member + 1) * quarter)
        dt_ref[block + member * rank : block + (member + 1) * rank, part] = (up_ref[member] * pull[:, part]).astype(BF)
    both = nt(dt_ref[...], we_ref[...])
    back_ref[...] = both[:half].astype(BF)
    back_pair_ref[...] = both[half:block].astype(BF)
    hidden = hid_ref[...]
    if known_norm:
        out = nt(hidden, wc_ref[...])
        cross_ref[...] = jnp.zeros_like(cross_ref)
        ccross_ref[...] = jnp.zeros_like(ccross_ref)
    else:
        out = nt(jnp.concatenate([hidden, cdown_ref[...]], axis=0), wc_ref[...])
        ccross_ref[...] = out[block:]
    out_ref[...] = out[:half].astype(BF)
    out_pair_ref[...] = out[half:block].astype(BF)
    low = nt(down_ref[...], h).astype(BF)
    low_grads = []
    for member in range(2):
        rows = slice(member * rank, (member + 1) * rank)
        dt = dt_ref[:block, member * quarter : (member + 1) * quarter]
        low_grads.append(nt(up_ref[member].astype(BF), dt).astype(BF))
        quad_ref[rows] = mm(low[rows], dt)
    shared_ref[: 2 * rank] = both[block:] + mm(jnp.concatenate(low_grads, axis=0), h)
    quad_ref[2 * rank :] = mm(nt(cup_ref[...], g).astype(BF), hidden)
    shared_ref[2 * rank :] = mm(nt(cdown_ref[...], hidden).astype(BF), g)


def feed_forward_back(h, h_pair, g, g_pair, weight, magnitude, norm, factor, down, up, cdown, cup):
    half, width = h.shape
    quarter = weight.shape[1] // 3
    double = 2 * quarter
    rank = cup.shape[0]
    block = 2 * half
    known = norm is not None
    vmem = pl.BlockSpec(memory_space=pltpu.VMEM)
    any_space = pl.BlockSpec(memory_space=pl.ANY)
    rows = jax.ShapeDtypeStruct((half, width), BF)
    return pl.pallas_call(
        functools.partial(feed_kernel, known),
        in_specs=[vmem] * 4 + [any_space] + [vmem] * 7,
        out_specs=[vmem] * 10,
        out_shape=[
            rows, rows, rows, rows,
            jax.ShapeDtypeStruct((3 * rank, width), F32),
            jax.ShapeDtypeStruct((3 * rank, quarter), F32),
            jax.ShapeDtypeStruct((1, double), F32),
            jax.ShapeDtypeStruct((1, double), F32),
            jax.ShapeDtypeStruct((2 * rank, double), F32),
            jax.ShapeDtypeStruct((rank, width), F32),
        ],
        scratch_shapes=[
            pltpu.VMEM((width, double), BF),
            pltpu.VMEM((width, quarter), BF),
            pltpu.VMEM((block + 2 * rank, double), BF),
            pltpu.VMEM((block, quarter), BF),
            pltpu.SemaphoreType.DMA((3 * len(chunks_of(quarter, 512)),)),
        ],
        compiler_params=pltpu.CompilerParams(vmem_limit_bytes=58 << 20),
        cost_estimate=pl.CostEstimate(
            flops=12 * block * width * quarter, bytes_accessed=6 * width * quarter + 8 * block * width,
            transcendentals=block * quarter,
        ),
        name="feed_forward_back",
    )(h, h_pair, g, g_pair, weight, magnitude, norm if known else magnitude, factor, down, up, cdown, cup)


def feed_adapter_kernel(
    shared_far_ref, shared_ref, quad_far_ref, quad_ref, cross_ref, ccross_ref, up_ref, cup_ref, contract_ref, pull_ref,
    dm_ref, cpull_ref, cdm_ref, out_ref, quad_out_ref
):
    rank = cup_ref.shape[0]
    quarter = contract_ref.shape[1]
    cpull = cpull_ref[...]
    shared = shared_far_ref[...] + shared_ref[...]
    quads = quad_far_ref[...] + quad_ref[...]
    words_out(out_ref, 0, SCALE * shared[: 2 * rank])
    words_out(out_ref, 2 * rank, SCALE * (shared[2 * rank :] + ccross_ref[...] * cpull))
    words_out(out_ref, 3 * rank, row_of(cdm_ref[...]))
    for member in range(2):
        part = slice(member * quarter, (member + 1) * quarter)
        rows = slice(member * rank, (member + 1) * rank)
        words_out(quad_out_ref, member * rank, SCALE * (quads[rows] + cross_ref[rows, part] * pull_ref[:, part]))
    frozen = mm((cup_ref[...].astype(F32) * cpull).astype(BF), contract_ref[...])
    words_out(quad_out_ref, 2 * rank, SCALE * (quads[2 * rank :] + frozen))
    both = jnp.concatenate([dm_ref[:, :quarter], dm_ref[:, quarter:]], axis=0)
    words_out(quad_out_ref, 3 * rank, row_of(both))


def feed_adapter(*operands):
    rank, width = operands[7].shape
    quarter = operands[8].shape[1] // 3
    specs = [pl.BlockSpec(memory_space=pltpu.VMEM) for _ in operands]
    specs[8] = pl.BlockSpec((width, quarter), lambda i: (0, 2))
    return pl.pallas_call(
        feed_adapter_kernel,
        grid=(1,),
        in_specs=specs,
        out_specs=[pl.BlockSpec(memory_space=pltpu.VMEM)] * 2,
        out_shape=[
            jax.ShapeDtypeStruct((width // WORD, 3 * rank + 8, WORD), F32),
            jax.ShapeDtypeStruct((-(-quarter // WORD), 3 * rank + 8, WORD), F32),
        ],
        compiler_params=pltpu.CompilerParams(vmem_limit_bytes=48 << 20),
        cost_estimate=pl.CostEstimate(
            flops=2 * 256 * width * quarter, bytes_accessed=3 * width * quarter, transcendentals=0
        ),
        name="feed_adapter",
    )(*operands)


def turn_back_kernel(rotated, g_ref, t_ref, s_ref, r_ref, cos_ref, sin_ref, dt_ref, dm_ref):
    grad = g_ref[...]

    def finish(plain):
        dt_ref[0] = (plain * s_ref[...]).astype(BF)
        dm_ref[...] = jnp.sum(plain * t_ref[...].astype(F32), axis=0, keepdims=True) * r_ref[...]

    @pl.when(pl.program_id(0) < rotated)
    def _():
        finish(turned(grad, cos_ref[...], -sin_ref[...]))

    @pl.when(pl.program_id(0) >= rotated)
    def _():
        finish(grad)


def turn_back(grads, t, factor, inverse, cosine, sine):
    rows, columns = t.shape
    whole = lambda j: (0, 0)
    strip = lambda j: (0, j)
    heads = columns // HEAD_DIM
    each = heads // 3
    return pl.pallas_call(
        functools.partial(turn_back_kernel, 2 * each),
        grid=(heads,),
        in_specs=[
            pl.BlockSpec((rows, HEAD_DIM), strip),
            pl.BlockSpec((rows, HEAD_DIM), strip),
            pl.BlockSpec((1, HEAD_DIM), strip),
            pl.BlockSpec((1, HEAD_DIM), strip),
            pl.BlockSpec((rows, HEAD_DIM), whole),
            pl.BlockSpec((rows, HEAD_DIM), whole),
        ],
        out_specs=[
            pl.BlockSpec((1, rows, HEAD_DIM), lambda j: (j // each, 0, j % each)),
            pl.BlockSpec((1, HEAD_DIM), strip),
        ],
        out_shape=[
            jax.ShapeDtypeStruct((3, rows, columns // 3), BF),
            jax.ShapeDtypeStruct((1, columns), F32),
        ],
        name="turn_back",
    )(grads, t, factor, inverse, cosine, sine)


def unpacked(words, columns):
    return jnp.concatenate([words[i] for i in range(words.shape[0])], axis=1)[:, :columns]


def pad_rows(a, multiple):
    short = -a.shape[0] % multiple
    return jnp.pad(a, ((0, short), (0, 0))) if short else a


def halve(a, name, index):
    parts = a.reshape(2, a.shape[0] // 2, a.shape[1])
    return take(parts, index, 0) + swap(take(parts, 1 - index, 0).astype(BF), name).astype(F32)


def join(a, name, index):
    return pair(a, swap(a, name), index).reshape(2 * a.shape[0], a.shape[1])


def spread(a, name):
    size, place = lax.axis_size(name), lax.axis_index(name)
    parts = a.reshape(size, a.shape[0] // size, a.shape[1])
    total = take(parts, place, 0)
    for step in range(1, size):
        total = total + shift(take(parts, (place + step) % size, 0).astype(BF), name, step).astype(F32)
    return total


def collect(a, name):
    size, place = lax.axis_size(name), lax.axis_index(name)
    buffer = jnp.zeros((size,) + a.shape, a.dtype)
    buffer = put(buffer, a, place, 0)
    for step in range(1, size):
        buffer = put(buffer, shift(a, name, step), (place - step) % size, 0)
    return buffer.reshape(size * a.shape[0], a.shape[1])


def reduce_all(shared, by_core, by_quad, first_beside, beside):
    c, x = lax.axis_index("core"), lax.axis_index("xx")
    unit = lax.axis_size("yy") * lax.axis_size("seq")
    half = halve(pad_rows(shared, 16), "core", c)
    quarter = halve(pad_rows(jnp.concatenate([half, by_core], axis=0), 16), "xx", x)
    last = pad_rows(jnp.concatenate([quarter, by_quad], axis=0), 8 * unit)
    last = spread(spread(last, "yy"), "seq").astype(BF)
    last, first_beside = lax.optimization_barrier((last, first_beside))
    last, beside = lax.optimization_barrier((collect(last, "seq"), beside))
    last = collect(last, "yy")
    joined = join(last[: quarter.shape[0]], "xx", x)
    everywhere = join(joined[: half.shape[0]], "core", c)
    mine = joined[half.shape[0] : half.shape[0] + by_core.shape[0]]
    cores = pair(mine, swap(mine, "core"), c)
    mine = last[quarter.shape[0] : quarter.shape[0] + by_quad.shape[0]]
    both = pair(mine, swap(mine, "xx"), x)
    quads = pair(both, swap(both, "core"), c, axis=1)
    return everywhere, cores, quads, first_beside, beside


def body(
    tokens,
    cotangent,
    attention_base,
    expand_base,
    contract_base,
    attention_down,
    attention_up,
    attention_magnitude,
    expand_down,
    expand_up,
    expand_magnitude,
    contract_down,
    contract_up,
    contract_magnitude,
    prompt_length,
    response_length,
):
    y, x = lax.axis_index("yy"), lax.axis_index("xx")
    c, z = lax.axis_index("core"), lax.axis_index("seq")
    ny, count = lax.axis_size("yy"), lax.axis_size("seq")
    own_rows, local, width = tokens.shape
    rows = 2 * own_rows
    split = count // rows
    piece = local // (2 * split)
    half = count * piece
    blocks = ny * 2
    rank = attention_down.shape[-1]
    unit = attention_base.shape[1]
    hidden_size = expand_base.shape[-1]
    quarter = hidden_size // 4
    place = ((y * 2 + x) * 2 + c) * count + z
    sub = z % split

    def by_core(a):
        shaped = a.reshape(a.shape[:-1] + (blocks, 2, a.shape[-1] // blocks // 2))
        axis = a.ndim
        flat = a.shape[:-1] + (a.shape[-1] // 2,)
        return take(shaped, c, axis).reshape(flat), take(shaped, 1 - c, axis).reshape(flat)

    def by_quarter(a):
        shaped = a.reshape(a.shape[:-1] + (4, quarter))
        return take(shaped, 2 * x + c, a.ndim - 1)

    down_rows = lax.dynamic_slice_in_dim(attention_down, place * unit, unit, 1)
    attention = merged(attention_base, down_rows, attention_up)
    mine, other = by_core(attention[:3])
    mine = mine.transpose(1, 0, 2).reshape(unit, -1)
    other = other.transpose(1, 0, 2).reshape(unit, -1)
    qkv_piece = pair(mine, swap(other, "core"), c)
    out_halves = jnp.stack([attention[3][:, : width // 2], attention[3][:, width // 2 :]])
    attention_piece = jnp.concatenate([qkv_piece, out_halves], axis=2)
    (
        attention_piece, tokens, cotangent, expand_base, contract_base, attention_down, attention_up,
        attention_magnitude, expand_down, expand_up, expand_magnitude, contract_down, contract_up, contract_magnitude,
        prompt_length, response_length,
    ) = lax.optimization_barrier((
        attention_piece, tokens, cotangent, expand_base, contract_base, attention_down, attention_up,
        attention_magnitude, expand_down, expand_up, expand_magnitude, contract_down, contract_up, contract_magnitude,
        prompt_length, response_length,
    ))

    def relayout_start(a):
        shaped = a.reshape(own_rows, split, 2, piece, width)
        kept, sent = take(shaped, c, 2), take(shaped, 1 - c, 2)
        return pair(kept, swap(sent, "core"), c).reshape(count, piece, width)

    contract_columns = lax.dynamic_slice_in_dim(contract_up, place * unit, unit, 1)
    prepare = lambda core: feed_prepare(
        core, place, expand_base, contract_base, expand_down, expand_up, contract_down, contract_columns
    )
    feed_other, square_other = prepare(1 - c)
    feed_mine, square_mine = prepare(c)
    feed_other = swap(feed_other, "core")
    feed_near = pair(take(feed_mine, x, 0), take(feed_other, x, 0), c)
    feed_far = pair(take(feed_mine, 1 - x, 0), take(feed_other, 1 - x, 0), c)

    boxes = {
        "a0": Box(attention_piece),
        "m0": Box(feed_near),
        "feed": Box(feed_far),
        "tokens": Box(relayout_start(tokens)),
        "cotangent": Box(relayout_start(cotangent)),
    }
    inside = width // 2

    def qkv_place(turn, column, step):
        def of(block):
            part = block[..., : 3 * inside].reshape(1, 1, 2, 1, unit, 3 * inside)
            return part, [(y - turn) % ny, column, 0, (z - step) % count, 0, 0]

        return of

    def out_place(turn, column, step):
        def of(block):
            part = block[..., 3 * inside :].reshape(2, 1, 1, 1, unit, inside)
            return part, [0, (y - turn) % ny, column, (z - step) % count, 0, 0]

        return of

    def feed_place(turn, index, step):
        def of(block):
            return block.reshape(1, 1, 2, 1, unit, 3 * quarter), [(y - turn) % ny, index, 0, (z - step) % count, 0, 0]

        return of

    qkv_places, out_places, feed_places = {}, {}, {}
    for step in range(count):
        for turn in range(ny):
            tail = f"{step}y{turn}" if turn else f"{step}"
            for name, column in (("a" + tail, x), ("a" + tail + "x", 1 - x)):
                qkv_places[name] = qkv_place(turn, column, step)
                out_places[name] = out_place(turn, column, step)
            for index, side in ((x, "m"), (1 - x, "n")):
                feed_places[side + tail] = feed_place(turn, index, step)
    buffers = {
        "qkv": Buffer((ny, 2, 2, count, unit, 3 * inside), 4, qkv_places),
        "out": Buffer((2, ny, 2, count, unit, inside), 4, out_places),
        "feed": Buffer((ny, 2, 2, count, unit, 3 * quarter), 0, feed_places),
    }
    for name in ("qkv", "out"):
        buffers[name].put("a0", attention_piece)
    buffers["feed"].put("m0", feed_near)
    links = Links(2, boxes, buffers)
    cross_x = lambda a: swap(a, "xx")
    ring = lambda a: shift(a, "seq", 1)
    exchange = lambda a: lax.all_to_all(a, "seq", 0, 0, tiled=True)
    turns = range(1, ny)

    def moves_y(kind, step):
        return [(f"{kind}{step}", f"{kind}{step}y{turn}", functools.partial(shift, name="yy", step=turn)) for turn in turns]

    sides = "mn"
    back = lambda a: shift(a, "seq", -1)
    order = []
    for step in range(1, count):
        order.append((step - 1, step, ring))
    attention_z = [(f"a{source}", f"a{step}", move) for source, step, move in order]
    feed_z = [(f"{side}{source}", f"{side}{step}", move) for source, step, move in order for side in sides]
    z_queue = attention_z[:2] + [("tokens", "tokens_moved", exchange), ("cotangent", "cotangent_moved", exchange)]
    z_queue += attention_z[2:] + feed_z
    boxes["s0"] = Box((square_other + square_mine).sum(axis=0))
    small_queue = [(f"s{step - 1}", f"s{step}", ring) for step in range(1, count)]

    def by_seq(*pieces):
        buffer = jnp.zeros((count, unit), F32)
        for step, one in enumerate(pieces):
            buffer = lax.dynamic_update_slice_in_dim(buffer, one, (z - step) % count, 0)
        return buffer

    def in_order(index):
        return lambda mine, other: pair(mine, other, index).reshape(2 * mine.shape[0], unit)

    def by_yy(*pieces):
        buffer = jnp.zeros((ny,) + pieces[0].shape, F32)
        for step, one in enumerate(pieces):
            buffer = put(buffer, one, (y - step) % ny, 0)
        return buffer

    links.derived.append(("sz", [f"s{step}" for step in range(count)], by_seq))
    small_queue.append(("sz", "szc", lambda a: swap(a, "core")))
    links.derived.append(("sc", ["sz", "szc"], in_order(c)))
    small_queue.append(("sc", "scx", cross_x))
    links.derived.append(("sx", ["sc", "scx"], in_order(x)))
    small_queue += moves_y("s", "x")
    links.derived.append(("square", ["sx"] + [f"sxy{turn}" for turn in turns], by_yy))
    x_queue = [("a0", "a0x", cross_x)]
    y_queue = []
    steps = [0] + [step for _, step, _ in order]
    feed_moves = [move for step in steps for side in sides for move in moves_y(side, step)]
    for place_of, step in enumerate(steps):
        names = [f"a{step}"] + [f"a{step}y{turn}" for turn in turns]
        x_queue += [(name, name + "x", cross_x) for name in names if name != "a0"]
        if step == 0:
            x_queue.append(("feed", "n0", cross_x))
        y_queue += moves_y("a", step)
        if place_of >= 1:
            y_queue += feed_moves[:1]
            del feed_moves[:1]
    y_queue += feed_moves

    links.run([z_queue, x_queue, y_queue, small_queue])
    links.place(len(links.rounds) - 2)
    while qkv_places:
        links.place(links.placed + 1)
    qkv_weight = buffers["qkv"].array.reshape(width, 3 * inside)
    out_weight = buffers["out"].array.reshape(2, inside, inside)
    tokens_own = boxes["tokens_moved"].array.reshape(half, width)
    tokens_both = jnp.concatenate([tokens_own, swap(tokens_own, "core")], axis=0)
    def positions_of(sub_place, core_place):
        source = jnp.arange(count, dtype=jnp.int32)[:, None] * local
        inner = sub_place * 2 * piece + core_place * piece + jnp.arange(piece, dtype=jnp.int32)[None]
        return (source + inner).reshape(half)

    query_place = jnp.concatenate([positions_of(sub, c), positions_of(sub, 1 - c)])
    key_place = jnp.concatenate(
        [positions_of((sub - step) % split, side) for step in range(split) for side in (c, 1 - c)]
    )
    totals = (prompt_length + response_length).astype(F32)
    total = take(pair(totals, swap(totals, "core"), c).reshape(rows), z // split, 0).astype(jnp.int32)
    allowed = (key_place[None] <= query_place[:, None]) & (key_place[None] < total)
    bias = jnp.where(allowed, 0.0, -1e30).astype(F32)
    frequency = 10000.0 ** (-jnp.arange(HEAD_DIM // 2).astype(F32) / (HEAD_DIM // 2))
    angles = query_place.astype(F32)[:, None] * frequency[None]
    cosine = jnp.concatenate([jnp.cos(angles)] * 2, axis=1)
    sine = jnp.concatenate([-jnp.sin(angles), jnp.sin(angles)], axis=1)

    heads = width // 2 // HEAD_DIM
    rows_both = tokens_both.astype(F32)
    first = rms(rows_both).astype(BF)
    magnitude = by_core(attention_magnitude[:3])[0].reshape(1, -1)
    downs = attention_down[:3].transpose(0, 2, 1).reshape(3 * rank, width).astype(BF)
    qkv_t, qkv_p, qkv_norm, cross = qkv_forward(first, qkv_weight, downs, magnitude, cosine, sine)

    def share(a, step):
        perm = [(i, (i // split) * split + (i % split + step) % split) for i in range(count)]
        return lax.ppermute(a, "seq", perm)

    feed_buffer = buffers["feed"]
    if split == 1:
        kv, offsets = qkv_p, (heads, 2 * heads)
    else:
        own_kv = qkv_p[:, heads * HEAD_DIM :]
        kv = jnp.concatenate([own_kv] + [share(own_kv, step) for step in range(1, split)], axis=0)
        offsets = (0, heads)
    (mixed,) = attention_call(
        attend_kernel, "attend", heads, qkv_p, kv, offsets, [], bias, [(2 * half, BF)]
    )

    def core_scatter(partial):
        return partial[:half].astype(F32) + swap(partial[half:].astype(BF), "core").astype(F32)

    def core_join(own):
        return jnp.concatenate([own, swap(own, "core")], axis=0)

    out_rows = by_core(attention_down[3].T)[0].astype(BF)
    contract_square = boxes["square"].array.reshape(1, width)
    qkv_p, cotangent_own = lax.optimization_barrier((qkv_p, boxes["cotangent_moved"].array))
    cotangent_own = cotangent_own.reshape(half, width)
    cotangent_far = swap(cotangent_own, "xx")
    mixed, cotangent_far, out_weight = lax.optimization_barrier((mixed, cotangent_far, out_weight))
    links.place(len(links.rounds))
    feed_weight = feed_buffer.array.reshape(width, 3 * quarter)
    out_square = jnp.sum(out_weight.astype(F32) ** 2, axis=1).reshape(1, width)
    out_norm = jnp.sqrt(out_square + swap(out_square, "core"))
    out_scale = attention_magnitude[3:] / out_norm
    out_sent = [mm(mixed[half:], out_weight[i]).astype(BF) for i in range(2)]
    out_sent = swap(jnp.concatenate(out_sent, axis=1), "core").astype(F32)
    out_t = jnp.concatenate([mm(mixed[:half], out_weight[i]) for i in range(2)], axis=1) + out_sent
    rows_own = tokens_own.astype(F32)
    middle = rows_own + out_t * out_scale
    second_own = rms(middle).astype(BF)
    second_far = swap(second_own, "xx")
    second_near = (second_own, swap(second_own, "core"))
    second_far = (second_far, swap(second_far, "core"))
    low = nt(downs, first).astype(BF).reshape(3, rank, 2 * half)
    cross = jnp.stack(
        [cross[i * rank : (i + 1) * rank, i * width // 2 : (i + 1) * width // 2] for i in range(3)]
    )
    core_up = by_core(attention_up[:3])[0]
    second_far, cross, low, core_up = lax.optimization_barrier((second_far, cross, low, core_up))

    gate_up = jnp.stack([by_quarter(expand_up[i]) for i in range(2)])
    feed_downs = expand_down.transpose(0, 2, 1).reshape(2 * rank, width).astype(BF)
    contract_rows = take(contract_down.T.reshape(rank, 4, quarter), 2 * x + c, 1).astype(BF)
    contract_ups = contract_up.astype(BF)
    expand_magnitudes = by_quarter(expand_magnitude).reshape(1, -1)
    grad_own = cotangent_own.astype(F32)
    cotangent_near = (cotangent_own, swap(cotangent_own, "core"))
    cotangent_far = (cotangent_far, swap(cotangent_far, "core"))
    contract_norm = jnp.sqrt(contract_square)
    contract_scale = contract_magnitude[None] / contract_norm
    def total(kept, sent):
        return kept.astype(F32) + swap(sent, "core").astype(F32)

    (
        back_far, back_sent, out_far, out_sent, shared_far, quads_far, dm_far, expand_norm, expand_cross, contract_cross
    ) = feed_forward_back(
        *second_far, *cotangent_far, feed_weight, expand_magnitudes, None, contract_scale,
        feed_downs, gate_up, contract_rows, contract_ups,
    )
    back_far = total(back_far, back_sent).astype(BF)
    second_near, back_far = lax.optimization_barrier((second_near, back_far))
    back_near, back_sent, out_near, out_near_sent, shared_near, quads_near, dm_near = feed_forward_back(
        *second_near, *cotangent_near, feed_weight, expand_magnitudes, expand_norm, contract_scale,
        feed_downs, gate_up, contract_rows, contract_ups,
    )[:7]
    back_near, back_sent, back_far = lax.optimization_barrier((back_near, back_sent, swap(back_far, "xx")))
    middle_grad, out_dt_own, out_dm = middle_back(
        back_near, swap(back_sent, "core"), back_far, cotangent_own, middle, out_t, out_scale, out_norm
    )

    out_dt = core_join(out_dt_own)
    mixed_grad = sum(nt(out_dt[:, i * inside : (i + 1) * inside], out_weight[i]) for i in range(2)).astype(BF)
    out_far, back_far = lax.optimization_barrier((total(out_far, out_sent).astype(BF), back_far))
    out_far = swap(out_far, "xx")
    keys = 2 * half * split
    members = lambda a: a.reshape(3, 1, width // 2)
    qkv_scale = magnitude / qkv_norm

    def reunite(a):
        parts = a.reshape(split, 2 * half, -1)
        total = parts[0]
        for step in range(1, split):
            total = total + share(parts[step].astype(BF), -step).astype(F32)
        return total

    if split > 1:
        dq, dk, dv = attention_call(
            attend_back_kernel, "attend_back", heads, qkv_p, kv, offsets, [mixed_grad], bias,
            [(2 * half, F32), (keys, F32), (keys, F32)],
        )
        grads = jnp.concatenate([dq, reunite(dk), reunite(dv)], axis=1)
        qkv_dt, qkv_dm = turn_back(grads, qkv_t, qkv_scale, 1.0 / qkv_norm, cosine, sine)
        qkv_dm = members(qkv_dm)
    else:
        qkv_dt, qkv_dm = attend_back_turn(
            heads, qkv_p, mixed_grad, bias, qkv_t, members(qkv_scale), members(1.0 / qkv_norm), cosine, sine
        )
    def restore_start(own):
        return lax.all_to_all(own.reshape(count, piece, width), "seq", 0, 0, tiled=True)

    qkv_dt, out_far, out_near, out_near_sent = lax.optimization_barrier((qkv_dt, out_far, out_near, out_near_sent))
    contract_t = total(out_near, out_near_sent) + out_far.astype(F32)
    output_own = (middle + contract_t * contract_scale).astype(BF)
    layer_moved = restore_start(output_own)
    first_part, qkv_shared, qkv_core = qkv_back(
        qkv_dt, qkv_weight, first, low, core_up, cross, members(qkv_scale), members(qkv_norm), qkv_dm
    )
    first_grad = core_scatter(first_part)
    tokens_grad_own = middle_grad + rms_back(rows_own, first_grad)

    def restore_end(moved):
        shaped = moved.reshape(2, own_rows, split, piece, width)
        kept, sent = take(shaped, c, 0), take(shaped, 1 - c, 0)
        return pair(kept, swap(sent, "core"), c, axis=2).reshape(own_rows, local, width)

    expand_sum = dm_near + dm_far
    expand_pull = -expand_magnitudes * expand_sum / (expand_norm * expand_norm * expand_norm)
    contract_dm = jnp.sum(grad_own * contract_t, axis=0, keepdims=True) / contract_norm
    contract_sum = contract_dm + swap(contract_dm, "core")
    contract_sum = contract_sum + swap(contract_sum, "xx")
    contract_pull = -contract_scale * contract_sum / contract_norm
    feed_words, feed_quad_words = feed_adapter(
        shared_far, shared_near, quads_far, quads_near, expand_cross, contract_cross, gate_up, contract_ups,
        feed_weight, expand_pull, expand_sum / expand_norm, contract_pull, contract_dm,
    )
    flat = lambda a: a.reshape(-1, WORD)

    out_words, out_core_words = out_adapter(
        out_dt, out_weight, mixed, out_rows, attention_up[3], out_scale, out_norm,
        out_dm + swap(out_dm, "core"), out_dm,
    )
    dm_words = jnp.pad(qkv_dm[:, 0], ((0, 5), (0, 0)))
    dm_words = jnp.stack([dm_words[:, i : i + WORD] for i in range(0, width // 2, WORD)])
    shared = jnp.concatenate([flat(qkv_shared), flat(out_words), flat(feed_words)])
    cores = jnp.concatenate([flat(qkv_core), flat(dm_words), flat(out_core_words)])
    attention_shared, attention_cores, feed_quads, layer_moved, tokens_moved = reduce_all(
        shared, cores, flat(feed_quad_words), layer_moved, tokens_grad_own.astype(BF)
    )
    tokens_moved = restore_start(tokens_moved)
    used = flat(qkv_shared).shape[0] + flat(out_words).shape[0]
    feed_shared = attention_shared[used:]

    def interleave(parts):
        shaped = [p.reshape(p.shape[0], blocks, 1, -1) for p in parts]
        return jnp.concatenate(shaped, axis=2).reshape(parts[0].shape[0], -1)

    used = flat(qkv_shared).shape[0]
    qkv_down_all = unpacked(attention_shared[:used].reshape(qkv_shared.shape), width)
    out_all = unpacked(attention_shared[used : used + flat(out_words).shape[0]].reshape(out_words.shape), width)
    core_parts = []
    for side in range(2):
        start, parts = 0, []
        for words in (qkv_core, dm_words, out_core_words):
            used = flat(words).shape[0]
            parts.append(unpacked(attention_cores[side, start : start + used].reshape(words.shape), width // 2))
            start += used
        core_parts.append(parts)
    qkv_up_all, qkv_dm_all, out_down_all = (interleave([core_parts[0][i], core_parts[1][i]]) for i in range(3))
    attention_down_grad = (
        jnp.concatenate([qkv_down_all, out_down_all]).reshape(4, rank, width).transpose(0, 2, 1)
    )
    attention_up_grad = jnp.concatenate([qkv_up_all, out_all[:rank]]).reshape(4, rank, width)
    attention_magnitude_grad = jnp.concatenate([qkv_dm_all[:3], out_all[rank : rank + 1]])

    feed_all = unpacked(feed_shared[: flat(feed_words).shape[0]].reshape(feed_words.shape), width)
    quad_all = jnp.concatenate(
        [unpacked(feed_quads[i, j].reshape(feed_quad_words.shape), quarter) for i in range(2) for j in range(2)],
        axis=1,
    )

    layer_output = restore_end(layer_moved)
    tokens_grad = restore_end(tokens_moved).astype(F32)
    return (
        layer_output,
        tokens_grad,
        attention_down_grad.astype(F32),
        attention_up_grad.astype(F32),
        attention_magnitude_grad.astype(F32),
        feed_all[: 2 * rank].reshape(2, rank, width).transpose(0, 2, 1).astype(F32),
        quad_all[: 2 * rank].reshape(2, rank, hidden_size).astype(F32),
        quad_all[3 * rank : 3 * rank + 2].astype(F32),
        quad_all[2 * rank : 3 * rank].T.astype(F32),
        feed_all[2 * rank : 3 * rank].astype(F32),
        feed_all[3 * rank].astype(F32),
    )


def solution(mesh):
    devices = mesh.devices
    chips = devices.shape[0] // 2
    fine = Mesh(devices.reshape(chips // 2, 2, 2, devices.shape[1]), ALL)
    dp = ("yy", "xx", "core")
    every = ("yy", "xx", "core", "seq")
    placed = (
        P(dp, "seq", None),
        P(dp, "seq", None),
        P(None, every, None),
        P(None, every, None),
        P(None, every),
        P(),
        P(),
        P(),
        P(),
        P(),
        P(),
        P(),
        P(),
        P(),
        P(dp),
        P(dp),
    )
    return jax.shard_map(
        body,
        mesh=fine,
        in_specs=placed,
        out_specs=(P(dp, "seq", None), P(dp, "seq", None)) + (P(),) * 9,
        check_vma=False,
    )
```

```python
import functools

import jax
import jax.numpy as jnp
from jax import lax
from jax.experimental import pallas as pl
from jax.experimental.pallas import tpu as pltpu
from jax.sharding import Mesh
from jax.sharding import PartitionSpec as P

HEAD_DIM = 128
SCALE = 2.0
BF = jnp.bfloat16
F32 = jnp.float32
ALL = ("yy", "xx", "core", "seq")
WORD = 512


def mm(a, b, dims=((1,), (0,))):
    return lax.dot_general(a, b, (dims, ((), ())), preferred_element_type=F32)


def nt(a, b):
    return mm(a, b, ((1,), (1,)))


def tn(a, b):
    return mm(a, b, ((0,), (0,)))


def take(a, index, axis):
    return lax.dynamic_index_in_dim(a, index, axis, keepdims=False)


def swap(a, name):
    return lax.ppermute(a, name, [(0, 1), (1, 0)])


def shift(a, name, step):
    size = lax.axis_size(name)
    return lax.ppermute(a, name, [(i, (i + step) % size) for i in range(size)])


def pair(mine, other, index, axis=0):
    first = jnp.where(index == 0, mine, other)
    second = jnp.where(index == 0, other, mine)
    return jnp.stack([first, second], axis=axis)


def put(buffer, block, index, axis):
    return lax.dynamic_update_slice_in_dim(buffer, jnp.expand_dims(block, axis), index, axis)


def rms(v):
    return v * lax.rsqrt(jnp.mean(v * v, axis=-1, keepdims=True) + 1e-05)


def rms_back(v, grad):
    inverse = lax.rsqrt(jnp.mean(v * v, axis=-1, keepdims=True) + 1e-05)
    inner = jnp.mean(v * grad, axis=-1, keepdims=True)
    return grad * inverse - v * (inner * inverse * inverse * inverse)


def merged(base, down, up):
    product = lax.dot_general(
        down.astype(BF), up.astype(BF), (((down.ndim - 1,), (up.ndim - 2,)), (tuple(range(down.ndim - 2)),) * 2),
        preferred_element_type=F32,
    )
    return (base.astype(F32) + SCALE * product).astype(BF)


class Box:
    def __init__(self, array):
        self.array = self.raw = array


class Links:
    def __init__(self, depth, boxes, buffers):
        self.depth = depth
        self.boxes = boxes
        self.buffers = buffers
        self.rounds = []
        self.placed = 0
        self.derived = []

    def run(self, queues):
        boxes = self.boxes
        while any(queues):
            for name, sources, join_of in [e for e in self.derived if all(n in boxes for n in e[1])]:
                boxes[name] = Box(join_of(*[boxes[n].array for n in sources]))
            self.derived = [e for e in self.derived if e[0] not in boxes]
            ready = set(boxes)
            self.rounds.append([])
            for queue in queues:
                for place, (source, result, move) in enumerate(queue):
                    if source in ready:
                        queue.pop(place)
                        self.send(boxes, source, result, move)
                        break
            self.place(len(self.rounds) - self.depth)

    def place(self, until):
        while self.placed < until:
            for name, box in self.rounds[self.placed]:
                for buffer in self.buffers.values():
                    buffer.put(name, box.raw)
            self.placed += 1

    def send(self, boxes, source, result, move):
        box = boxes[source]
        if len(self.rounds) > self.depth:
            old = [b for name, b in self.rounds[-1 - self.depth] if b is not box and "_" not in name]
            if len(self.rounds) > 6:
                old += [b for name, b in self.rounds[-7] if b is not box and "_" in name]
            held = [b for b in self.buffers.values() if b.pending()]
            both = lax.optimization_barrier((box.array, [b.array for b in old], [b.array for b in held]))
            box.array = both[0]
            for b, array in zip(old + held, both[1] + both[2]):
                b.array = array
        boxes[result] = Box(move(box.array))
        self.rounds[-1].append((result, boxes[result]))


class Buffer:
    def __init__(self, shape, free, blocks):
        self.array = unwritten(shape, BF)
        self.free = free
        self.blocks = blocks

    def pending(self):
        return len(self.blocks) > self.free

    def put(self, name, block):
        if name in self.blocks:
            part, start = self.blocks.pop(name)(block)
            self.array = lax.dynamic_update_slice(self.array, part, [jnp.int32(v) for v in start])


def unwritten(shape, kind):
    return pl.pallas_call(
        lambda ref: None, out_shape=jax.ShapeDtypeStruct(shape, kind),
        out_specs=pl.BlockSpec(memory_space=pl.ANY), name="unwritten",
    )()


def turned(v, cosine, sine):
    return v * cosine + pltpu.roll(v, HEAD_DIM // 2, 1) * sine


def qkv_kernel(rotated, h_ref, v_ref, down_ref, m_ref, cos_ref, sin_ref, t_ref, p_ref, n_ref, cross_ref):
    block = v_ref[...]
    rows = h_ref.shape[0]
    both = jnp.dot(jnp.concatenate([h_ref[...], down_ref[...]], axis=0), block, preferred_element_type=F32)
    cross_ref[...] = both[rows:]
    t = both[:rows]
    wide = block.astype(F32)
    norm = jnp.sqrt(jnp.sum(wide * wide, axis=0, keepdims=True))
    n_ref[...] = norm
    t_ref[...] = t.astype(BF)
    scaled = t * (m_ref[...] / norm)

    @pl.when(pl.program_id(0) < rotated)
    def _():
        for part in range(t.shape[1] // HEAD_DIM):
            columns = slice(part * HEAD_DIM, (part + 1) * HEAD_DIM)
            p_ref[:, columns] = turned(scaled[:, columns], cos_ref[...], sin_ref[...]).astype(BF)

    @pl.when(pl.program_id(0) >= rotated)
    def _():
        p_ref[...] = scaled.astype(BF)


def qkv_forward(h, weight, downs, magnitude, cosine, sine):
    rows, depth = h.shape
    columns = magnitude.shape[1]
    width = 2 * HEAD_DIM
    rotated = columns * 2 // 3 // width
    whole = lambda j: (0, 0)
    strip = lambda j: (0, j)
    return pl.pallas_call(
        functools.partial(qkv_kernel, rotated),
        grid=(columns // width,),
        in_specs=[
            pl.BlockSpec((rows, depth), whole),
            pl.BlockSpec((depth, width), strip),
            pl.BlockSpec(downs.shape, whole),
            pl.BlockSpec((1, width), strip),
            pl.BlockSpec((rows, HEAD_DIM), whole),
            pl.BlockSpec((rows, HEAD_DIM), whole),
        ],
        out_specs=[
            pl.BlockSpec((rows, width), strip),
            pl.BlockSpec((rows, width), strip),
            pl.BlockSpec((1, width), strip),
            pl.BlockSpec((downs.shape[0], width), strip),
        ],
        out_shape=[
            jax.ShapeDtypeStruct((rows, columns), BF),
            jax.ShapeDtypeStruct((rows, columns), BF),
            jax.ShapeDtypeStruct((1, columns), F32),
            jax.ShapeDtypeStruct((downs.shape[0], columns), F32),
        ],
        compiler_params=pltpu.CompilerParams(vmem_limit_bytes=32 << 20),
        cost_estimate=pl.CostEstimate(
            flops=2 * rows * depth * columns, bytes_accessed=2 * depth * columns + 6 * rows * columns,
            transcendentals=columns,
        ),
        name="qkv_forward",
    )(h, weight, downs, magnitude, cosine, sine)


def softmax_block(q, k, bias):
    scores = nt(q, k) * HEAD_DIM ** (-0.5) + bias
    weights = jnp.exp(scores - jnp.max(scores, axis=-1, keepdims=True))
    return weights / jnp.sum(weights, axis=-1, keepdims=True)


def attend_kernel(q_ref, k_ref, v_ref, bias_ref, o_ref):
    probs = softmax_block(q_ref[...], k_ref[...], bias_ref[...])
    o_ref[...] = mm(probs.astype(BF), v_ref[...]).astype(BF)


def attend_back_kernel(q_ref, k_ref, v_ref, g_ref, bias_ref, dq_ref, dk_ref, dv_ref):
    q, k, g = q_ref[...], k_ref[...], g_ref[...]
    probs = softmax_block(q, k, bias_ref[...])
    grad = nt(g, v_ref[...])
    inner = jnp.sum(probs * grad, axis=-1, keepdims=True)
    raw = (probs * (grad - inner) * HEAD_DIM ** (-0.5)).astype(BF)
    dq_ref[...] = mm(raw, k)
    dk_ref[...] = tn(raw, q)
    dv_ref[...] = tn(probs.astype(BF), g)


def attention_call(kernel, name, heads, q, kv, offsets, extra, bias, outs):
    rows, keys = bias.shape
    head = lambda base: lambda j: (0, base + j)
    specs = [
        pl.BlockSpec((rows, HEAD_DIM), head(0)),
        pl.BlockSpec((keys, HEAD_DIM), head(offsets[0])),
        pl.BlockSpec((keys, HEAD_DIM), head(offsets[1])),
    ]
    specs += [pl.BlockSpec((rows, HEAD_DIM), head(0)) for _ in extra]
    specs.append(pl.BlockSpec((rows, keys), lambda j: (0, 0)))
    return pl.pallas_call(
        kernel,
        grid=(heads,),
        in_specs=specs,
        out_specs=[pl.BlockSpec((length, HEAD_DIM), head(0)) for length, _ in outs],
        out_shape=[jax.ShapeDtypeStruct((length, heads * HEAD_DIM), kind) for length, kind in outs],
        compiler_params=pltpu.CompilerParams(vmem_limit_bytes=48 << 20),
        cost_estimate=pl.CostEstimate(
            flops=4 * len(outs) * rows * keys * HEAD_DIM * heads,
            bytes_accessed=8 * rows * HEAD_DIM * heads, transcendentals=rows * keys * heads,
        ),
        name=name,
    )(q, kv, kv, *extra, bias)


def middle_back_kernel(
    near_ref, pair_ref, far_ref, g_ref, middle_ref, t_ref, s_ref, n_ref, grad_ref, dt_ref, dm_ref
):
    second = near_ref[...].astype(F32) + pair_ref[...].astype(F32) + far_ref[...].astype(F32)
    grad = g_ref[...].astype(F32) + rms_back(middle_ref[...], second)
    grad_ref[...] = grad
    dt_ref[...] = (grad * s_ref[...]).astype(BF)
    part = jnp.sum(grad * t_ref[...], axis=0, keepdims=True) / n_ref[...]

    @pl.when(pl.program_id(0) == 0)
    def _():
        dm_ref[...] = part

    @pl.when(pl.program_id(0) > 0)
    def _():
        dm_ref[...] += part


def middle_back(near, pair_part, far, g, middle, t, factor, norm):
    rows, width = middle.shape
    block = rows // 4
    row = pl.BlockSpec((block, width), lambda i: (i, 0))
    one = pl.BlockSpec((1, width), lambda i: (0, 0))
    return pl.pallas_call(
        middle_back_kernel,
        grid=(rows // block,),
        in_specs=[row] * 6 + [one] * 2,
        out_specs=[row, row, one],
        out_shape=[
            jax.ShapeDtypeStruct((rows, width), F32),
            jax.ShapeDtypeStruct((rows, width), BF),
            jax.ShapeDtypeStruct((1, width), F32),
        ],
        cost_estimate=pl.CostEstimate(flops=20 * rows * width, bytes_accessed=24 * rows * width, transcendentals=rows),
        name="middle_back",
    )(near, pair_part, far, g, middle, t, factor, norm)


def attend_back_turn_kernel(
    q_ref, k_ref, v_ref, g_ref, bias_ref, tq_ref, tk_ref, tv_ref, s_ref, r_ref, cos_ref, sin_ref, dt_ref, dm_ref
):
    q, k, g = q_ref[...], k_ref[...], g_ref[...]
    probs = softmax_block(q, k, bias_ref[...])
    grad = nt(g, v_ref[...])
    inner = jnp.sum(probs * grad, axis=-1, keepdims=True)
    raw = (probs * (grad - inner) * HEAD_DIM ** (-0.5)).astype(BF)
    cosine, sine = cos_ref[...], -sin_ref[...]
    plain = (turned(mm(raw, k), cosine, sine), turned(tn(raw, q), cosine, sine), tn(probs.astype(BF), g))
    for member, t_ref in enumerate((tq_ref, tk_ref, tv_ref)):
        dt_ref[member] = (plain[member] * s_ref[member]).astype(BF)
        dm_ref[member] = jnp.sum(plain[member] * t_ref[...].astype(F32), axis=0, keepdims=True) * r_ref[member]


def attend_back_turn(heads, qkv, grad, bias, t, factor, inverse, cosine, sine):
    rows = bias.shape[0]
    head = lambda base: lambda j: (0, base + j)
    whole = lambda j: (0, 0)
    block = lambda base: pl.BlockSpec((rows, HEAD_DIM), head(base))
    member = lambda j: (0, 0, j)
    return pl.pallas_call(
        attend_back_turn_kernel,
        grid=(heads,),
        in_specs=[
            block(0), block(heads), block(2 * heads), block(0),
            pl.BlockSpec((rows, rows), whole),
            block(0), block(heads), block(2 * heads),
            pl.BlockSpec((3, 1, HEAD_DIM), member),
            pl.BlockSpec((3, 1, HEAD_DIM), member),
            pl.BlockSpec((rows, HEAD_DIM), whole),
            pl.BlockSpec((rows, HEAD_DIM), whole),
        ],
        out_specs=[pl.BlockSpec((3, rows, HEAD_DIM), member), pl.BlockSpec((3, 1, HEAD_DIM), member)],
        out_shape=[
            jax.ShapeDtypeStruct((3, rows, heads * HEAD_DIM), BF),
            jax.ShapeDtypeStruct((3, 1, heads * HEAD_DIM), F32),
        ],
        compiler_params=pltpu.CompilerParams(vmem_limit_bytes=48 << 20),
        cost_estimate=pl.CostEstimate(
            flops=10 * rows * rows * HEAD_DIM * heads, bytes_accessed=20 * rows * HEAD_DIM * heads,
            transcendentals=rows * rows * heads,
        ),
        name="attend_back_turn",
    )(qkv, qkv, qkv, grad, bias, t, t, t, factor, inverse, cosine, sine)


def words_out(ref, start, value):
    rows, columns = value.shape
    for chunk in range(-(-columns // WORD)):
        left = chunk * WORD
        used = min(WORD, columns - left)
        ref[chunk, start : start + rows, :used] = value[:, left : left + used]
        if used < WORD:
            ref[chunk, start : start + rows, used:] = jnp.zeros((rows, WORD - used), F32)


def row_of(row, rows=8):
    return jnp.concatenate([row, jnp.zeros((rows - row.shape[0], row.shape[1]), F32)], axis=0)


def qkv_back_kernel(
    dt_ref, v_ref, h_ref, low_ref, up_ref, cross_ref, s_ref, n_ref, dm_ref, out_ref, shared_ref, core_ref, acc_ref
):
    member = pl.program_id(0)
    dt, weight = dt_ref[0], v_ref[...]
    rows = dt.shape[0]
    up = up_ref[0]
    pull = -s_ref[0] * dm_ref[0] / n_ref[0]
    stacked = nt(jnp.concatenate([dt, (up * pull).astype(BF)], axis=0), weight)
    update = stacked[:rows]

    @pl.when(member == 0)
    def _():
        acc_ref[...] = update

    @pl.when(member > 0)
    def _():
        acc_ref[...] += update

    @pl.when(member == pl.num_programs(0) - 1)
    def _():
        out_ref[...] = acc_ref[...].astype(BF)

    low_grad = nt(up.astype(BF), dt).astype(BF)
    words_out(shared_ref, 0, SCALE * (mm(low_grad, h_ref[...]) + stacked[rows:]))
    words_out(core_ref, 0, SCALE * (mm(low_ref[0], dt) + cross_ref[0] * pull))


def qkv_back(dt, weight, h, low, up, cross, factor, norm, dm):
    members, rows, columns = dt.shape
    width = h.shape[1]
    rank = up.shape[1]
    step = lambda j: (j, 0, 0)
    small = pl.BlockSpec((1, 1, columns), step)
    return pl.pallas_call(
        qkv_back_kernel,
        grid=(members,),
        in_specs=[
            pl.BlockSpec((1, rows, columns), step),
            pl.BlockSpec((width, columns), lambda j: (0, j)),
            pl.BlockSpec((rows, width), lambda j: (0, 0)),
            pl.BlockSpec((1, rank, rows), step),
            pl.BlockSpec((1, rank, columns), step),
            pl.BlockSpec((1, rank, columns), step),
            small, small, small,
        ],
        out_specs=[
            pl.BlockSpec((rows, width), lambda j: (0, 0)),
            pl.BlockSpec((width // WORD, rank, WORD), lambda j: (0, j, 0)),
            pl.BlockSpec((columns // WORD, rank, WORD), lambda j: (0, j, 0)),
        ],
        out_shape=[
            jax.ShapeDtypeStruct((rows, width), BF),
            jax.ShapeDtypeStruct((width // WORD, members * rank, WORD), F32),
            jax.ShapeDtypeStruct((columns // WORD, members * rank, WORD), F32),
        ],
        scratch_shapes=[pltpu.VMEM((rows, width), F32)],
        compiler_params=pltpu.CompilerParams(vmem_limit_bytes=48 << 20),
        cost_estimate=pl.CostEstimate(
            flops=2 * members * rows * columns * width, bytes_accessed=2 * members * width * columns,
            transcendentals=0,
        ),
        name="qkv_back",
    )(dt, weight, h, low, up, cross, factor, norm, dm)


def out_adapter_kernel(
    dt_ref, w_ref, u_ref, down_ref, up_ref, s_ref, n_ref, dm_ref, own_ref, shared_ref, core_ref
):
    inside = u_ref.shape[1]
    dt, u, up, down = dt_ref[...], u_ref[...], up_ref[...], down_ref[...]
    rank = up.shape[0]
    pull = -s_ref[...] * dm_ref[...] / n_ref[...]
    low_grad = nt(up.astype(BF), dt).astype(BF)
    frozen = (up * pull).astype(BF)
    sides = (slice(0, inside), slice(inside, 2 * inside))
    words_out(core_ref, 0, SCALE * (mm(low_grad, u) + sum(nt(frozen[:, part], w_ref[i]) for i, part in enumerate(sides))))
    low = nt(down, u).astype(BF)
    cross = jnp.concatenate([mm(down, w_ref[i]) for i in range(2)], axis=1)
    words_out(shared_ref, 0, SCALE * (mm(low, dt) + cross * pull))
    words_out(shared_ref, rank, row_of(own_ref[...]))


def out_adapter(dt, weight, u, down, up, factor, norm, dm_pair, dm_own):
    rank, width = up.shape
    inside = u.shape[1]
    return pl.pallas_call(
        out_adapter_kernel,
        out_shape=[
            jax.ShapeDtypeStruct((width // WORD, rank + 8, WORD), F32),
            jax.ShapeDtypeStruct((inside // WORD, rank, WORD), F32),
        ],
        compiler_params=pltpu.CompilerParams(vmem_limit_bytes=48 << 20),
        cost_estimate=pl.CostEstimate(
            flops=2 * width * inside * 256, bytes_accessed=2 * width * inside, transcendentals=0
        ),
        name="out_adapter",
    )(dt, weight, u, down, up, factor, norm, dm_pair, dm_own)


def chunks_of(columns, width):
    return [(left, min(left + width, columns)) for left in range(0, columns, width)]


def feed_prepare_kernel(
    index_ref, base_ref, cbase_ref, down_ref, up_ref, cdown_ref, cup_ref, out_ref, square_ref
):
    quarter = base_ref.shape[2]
    for member in range(2):
        merged_block = base_ref[member].astype(F32) + SCALE * mm(down_ref[member].astype(BF), up_ref[member].astype(BF))
        out_ref[0, :, member * quarter : (member + 1) * quarter] = merged_block.astype(BF)
    merged_block = cbase_ref[...].astype(F32) + SCALE * mm(cdown_ref[...].astype(BF), cup_ref[...].astype(BF))
    out_ref[0, :, 2 * quarter :] = merged_block.T.astype(BF)
    square_ref[0] = jnp.sum(merged_block * merged_block, axis=0, keepdims=True)


def feed_prepare(core, place, base, cbase, down, up, cdown, cup_columns):
    unit = base.shape[1]
    quarter = base.shape[2] // 4
    rank = up.shape[1]
    at = lambda i, index: 2 * i + index[0]
    return pl.pallas_call(
        feed_prepare_kernel,
        grid_spec=pltpu.PrefetchScalarGridSpec(
            num_scalar_prefetch=1,
            grid=(2,),
            in_specs=[
                pl.BlockSpec((2, unit, quarter), lambda i, index: (0, 0, at(i, index))),
                pl.BlockSpec((quarter, unit), lambda i, index: (at(i, index), 0)),
                pl.BlockSpec((2, unit, rank), lambda i, index: (0, index[1], 0)),
                pl.BlockSpec((2, rank, quarter), lambda i, index: (0, 0, at(i, index))),
                pl.BlockSpec((quarter, rank), lambda i, index: (at(i, index), 0)),
                pl.BlockSpec((rank, unit), lambda i, index: (0, 0)),
            ],
            out_specs=[
                pl.BlockSpec((1, unit, 3 * quarter), lambda i, index: (i, 0, 0)),
                pl.BlockSpec((1, 1, unit), lambda i, index: (i, 0, 0)),
            ],
        ),
        out_shape=[
            jax.ShapeDtypeStruct((2, unit, 3 * quarter), BF),
            jax.ShapeDtypeStruct((2, 1, unit), F32),
        ],
        cost_estimate=pl.CostEstimate(
            flops=12 * unit * quarter * rank, bytes_accessed=24 * unit * quarter, transcendentals=0
        ),
        name="feed_prepare",
    )(jnp.stack([core, place]).astype(jnp.int32), base, cbase, down, up, cdown, cup_columns)


def feed_kernel(
    known_norm, h_ref, h_pair_ref, g_ref, g_pair_ref, weight_ref, m_ref, norm_in_ref, gs_ref, down_ref, up_ref, cdown_ref,
    cup_ref, back_ref, back_pair_ref, out_ref, out_pair_ref, shared_ref, quad_ref, dm_ref, norm_ref, cross_ref,
    ccross_ref, we_ref, wc_ref, dt_ref, hid_ref, sems
):
    half, width = h_ref.shape
    block = 2 * half
    quarter = wc_ref.shape[1]
    rank = cup_ref.shape[0]
    parts = chunks_of(quarter, 512)

    def copies(index, left, right):
        target = ((we_ref, left), (we_ref, quarter + left), (wc_ref, left))
        return [
            pltpu.make_async_copy(
                weight_ref.at[:, pl.ds(kind * quarter + left, right - left)], vmem.at[:, pl.ds(start, right - left)],
                sems.at[3 * index + kind],
            )
            for kind, (vmem, start) in enumerate(target)
        ]

    for index, (left, right) in enumerate(parts):
        for copy in copies(index, left, right):
            copy.start()
    if known_norm:
        norm_ref[...] = norm_in_ref[...]
    dt_ref[block:, :] = jnp.zeros((2 * rank, 2 * quarter), BF)
    h = jnp.concatenate([h_ref[...], h_pair_ref[...]], axis=0)
    g = jnp.concatenate([g_ref[...], g_pair_ref[...]], axis=0)
    g = (g.astype(F32) * gs_ref[...]).astype(BF)
    inputs = h if known_norm else jnp.concatenate([h, down_ref[...]], axis=0)
    for index, (left, right) in enumerate(parts):
        near, far = slice(left, right), slice(quarter + left, quarter + right)

        for copy in copies(index, left, right):
            copy.wait()
        if not known_norm:
            for part in (near, far):
                wide = we_ref[:, part].astype(F32)
                norm_ref[:, part] = jnp.sqrt(jnp.sum(wide * wide, axis=0, keepdims=True))
        gate_t = mm(inputs, we_ref[:, near])
        up_t = mm(inputs, we_ref[:, far])
        if not known_norm:
            cross_ref[:, near], cross_ref[:, far] = gate_t[block:], up_t[block:]
            gate_t, up_t = gate_t[:block], up_t[:block]
        grad = mm(g, wc_ref[:, near])
        gate_s = m_ref[:, near] / norm_ref[:, near]
        up_s = m_ref[:, far] / norm_ref[:, far]
        gate = gate_t * gate_s
        up = up_t * up_s
        sigmoid = 1.0 / (1.0 + jnp.exp(-gate))
        silu = gate * sigmoid
        hid_ref[:, near] = (silu * up).astype(BF)
        up_grad = grad * silu
        gate_grad = grad * up * (sigmoid + silu * (1.0 - sigmoid))
        dm_ref[:, near] = jnp.sum(gate_grad * gate_t, axis=0, keepdims=True)
        dm_ref[:, far] = jnp.sum(up_grad * up_t, axis=0, keepdims=True)
        dt_ref[:block, near] = (gate_grad * gate_s).astype(BF)
        dt_ref[:block, far] = (up_grad * up_s).astype(BF)

    norm = norm_ref[...]
    pull = -m_ref[...] * dm_ref[...] / (norm * norm * norm)
    for member in range(2):
        part = slice(member * quarter, (member + 1) * quarter)
        dt_ref[block + member * rank : block + (member + 1) * rank, part] = (up_ref[member] * pull[:, part]).astype(BF)
    both = nt(dt_ref[...], we_ref[...])
    back_ref[...] = both[:half].astype(BF)
    back_pair_ref[...] = both[half:block].astype(BF)
    hidden = hid_ref[...]
    if known_norm:
        out = nt(hidden, wc_ref[...])
        cross_ref[...] = jnp.zeros_like(cross_ref)
        ccross_ref[...] = jnp.zeros_like(ccross_ref)
    else:
        out = nt(jnp.concatenate([hidden, cdown_ref[...]], axis=0), wc_ref[...])
        ccross_ref[...] = out[block:]
    out_ref[...] = out[:half].astype(BF)
    out_pair_ref[...] = out[half:block].astype(BF)
    low = nt(down_ref[...], h).astype(BF)
    low_grads = []
    for member in range(2):
        rows = slice(member * rank, (member + 1) * rank)
        dt = dt_ref[:block, member * quarter : (member + 1) * quarter]
        low_grads.append(nt(up_ref[member].astype(BF), dt).astype(BF))
        quad_ref[rows] = mm(low[rows], dt)
    shared_ref[: 2 * rank] = both[block:] + mm(jnp.concatenate(low_grads, axis=0), h)
    quad_ref[2 * rank :] = mm(nt(cup_ref[...], g).astype(BF), hidden)
    shared_ref[2 * rank :] = mm(nt(cdown_ref[...], hidden).astype(BF), g)


def feed_forward_back(h, h_pair, g, g_pair, weight, magnitude, norm, factor, down, up, cdown, cup):
    half, width = h.shape
    quarter = weight.shape[1] // 3
    double = 2 * quarter
    rank = cup.shape[0]
    block = 2 * half
    known = norm is not None
    vmem = pl.BlockSpec(memory_space=pltpu.VMEM)
    any_space = pl.BlockSpec(memory_space=pl.ANY)
    rows = jax.ShapeDtypeStruct((half, width), BF)
    return pl.pallas_call(
        functools.partial(feed_kernel, known),
        in_specs=[vmem] * 4 + [any_space] + [vmem] * 7,
        out_specs=[vmem] * 10,
        out_shape=[
            rows, rows, rows, rows,
            jax.ShapeDtypeStruct((3 * rank, width), F32),
            jax.ShapeDtypeStruct((3 * rank, quarter), F32),
            jax.ShapeDtypeStruct((1, double), F32),
            jax.ShapeDtypeStruct((1, double), F32),
            jax.ShapeDtypeStruct((2 * rank, double), F32),
            jax.ShapeDtypeStruct((rank, width), F32),
        ],
        scratch_shapes=[
            pltpu.VMEM((width, double), BF),
            pltpu.VMEM((width, quarter), BF),
            pltpu.VMEM((block + 2 * rank, double), BF),
            pltpu.VMEM((block, quarter), BF),
            pltpu.SemaphoreType.DMA((3 * len(chunks_of(quarter, 512)),)),
        ],
        compiler_params=pltpu.CompilerParams(vmem_limit_bytes=58 << 20),
        cost_estimate=pl.CostEstimate(
            flops=12 * block * width * quarter, bytes_accessed=6 * width * quarter + 8 * block * width,
            transcendentals=block * quarter,
        ),
        name="feed_forward_back",
    )(h, h_pair, g, g_pair, weight, magnitude, norm if known else magnitude, factor, down, up, cdown, cup)


def feed_adapter_kernel(
    shared_far_ref, shared_ref, quad_far_ref, quad_ref, cross_ref, ccross_ref, up_ref, cup_ref, contract_ref, pull_ref,
    dm_ref, cpull_ref, cdm_ref, out_ref, quad_out_ref
):
    rank = cup_ref.shape[0]
    quarter = contract_ref.shape[1]
    cpull = cpull_ref[...]
    shared = shared_far_ref[...] + shared_ref[...]
    quads = quad_far_ref[...] + quad_ref[...]
    words_out(out_ref, 0, SCALE * shared[: 2 * rank])
    words_out(out_ref, 2 * rank, SCALE * (shared[2 * rank :] + ccross_ref[...] * cpull))
    words_out(out_ref, 3 * rank, row_of(cdm_ref[...]))
    for member in range(2):
        part = slice(member * quarter, (member + 1) * quarter)
        rows = slice(member * rank, (member + 1) * rank)
        words_out(quad_out_ref, member * rank, SCALE * (quads[rows] + cross_ref[rows, part] * pull_ref[:, part]))
    frozen = mm((cup_ref[...].astype(F32) * cpull).astype(BF), contract_ref[...])
    words_out(quad_out_ref, 2 * rank, SCALE * (quads[2 * rank :] + frozen))
    both = jnp.concatenate([dm_ref[:, :quarter], dm_ref[:, quarter:]], axis=0)
    words_out(quad_out_ref, 3 * rank, row_of(both))


def feed_adapter(*operands):
    rank, width = operands[7].shape
    quarter = operands[8].shape[1] // 3
    specs = [pl.BlockSpec(memory_space=pltpu.VMEM) for _ in operands]
    specs[8] = pl.BlockSpec((width, quarter), lambda i: (0, 2))
    return pl.pallas_call(
        feed_adapter_kernel,
        grid=(1,),
        in_specs=specs,
        out_specs=[pl.BlockSpec(memory_space=pltpu.VMEM)] * 2,
        out_shape=[
            jax.ShapeDtypeStruct((width // WORD, 3 * rank + 8, WORD), F32),
            jax.ShapeDtypeStruct((-(-quarter // WORD), 3 * rank + 8, WORD), F32),
        ],
        compiler_params=pltpu.CompilerParams(vmem_limit_bytes=48 << 20),
        cost_estimate=pl.CostEstimate(
            flops=2 * 256 * width * quarter, bytes_accessed=3 * width * quarter, transcendentals=0
        ),
        name="feed_adapter",
    )(*operands)


def turn_back_kernel(rotated, g_ref, t_ref, s_ref, r_ref, cos_ref, sin_ref, dt_ref, dm_ref):
    grad = g_ref[...]

    def finish(plain):
        dt_ref[0] = (plain * s_ref[...]).astype(BF)
        dm_ref[...] = jnp.sum(plain * t_ref[...].astype(F32), axis=0, keepdims=True) * r_ref[...]

    @pl.when(pl.program_id(0) < rotated)
    def _():
        finish(turned(grad, cos_ref[...], -sin_ref[...]))

    @pl.when(pl.program_id(0) >= rotated)
    def _():
        finish(grad)


def turn_back(grads, t, factor, inverse, cosine, sine):
    rows, columns = t.shape
    whole = lambda j: (0, 0)
    strip = lambda j: (0, j)
    heads = columns // HEAD_DIM
    each = heads // 3
    return pl.pallas_call(
        functools.partial(turn_back_kernel, 2 * each),
        grid=(heads,),
        in_specs=[
            pl.BlockSpec((rows, HEAD_DIM), strip),
            pl.BlockSpec((rows, HEAD_DIM), strip),
            pl.BlockSpec((1, HEAD_DIM), strip),
            pl.BlockSpec((1, HEAD_DIM), strip),
            pl.BlockSpec((rows, HEAD_DIM), whole),
            pl.BlockSpec((rows, HEAD_DIM), whole),
        ],
        out_specs=[
            pl.BlockSpec((1, rows, HEAD_DIM), lambda j: (j // each, 0, j % each)),
            pl.BlockSpec((1, HEAD_DIM), strip),
        ],
        out_shape=[
            jax.ShapeDtypeStruct((3, rows, columns // 3), BF),
            jax.ShapeDtypeStruct((1, columns), F32),
        ],
        name="turn_back",
    )(grads, t, factor, inverse, cosine, sine)


def unpacked(words, columns):
    return jnp.concatenate([words[i] for i in range(words.shape[0])], axis=1)[:, :columns]


def pad_rows(a, multiple):
    short = -a.shape[0] % multiple
    return jnp.pad(a, ((0, short), (0, 0))) if short else a


def halve(a, name, index):
    parts = a.reshape(2, a.shape[0] // 2, a.shape[1])
    return take(parts, index, 0) + swap(take(parts, 1 - index, 0).astype(BF), name).astype(F32)


def join(a, name, index):
    return pair(a, swap(a, name), index).reshape(2 * a.shape[0], a.shape[1])


def spread(a, name):
    size, place = lax.axis_size(name), lax.axis_index(name)
    parts = a.reshape(size, a.shape[0] // size, a.shape[1])
    total = take(parts, place, 0)
    for step in range(1, size):
        total = total + shift(take(parts, (place + step) % size, 0).astype(BF), name, step).astype(F32)
    return total


def collect(a, name):
    size, place = lax.axis_size(name), lax.axis_index(name)
    buffer = jnp.zeros((size,) + a.shape, a.dtype)
    buffer = put(buffer, a, place, 0)
    for step in range(1, size):
        buffer = put(buffer, shift(a, name, step), (place - step) % size, 0)
    return buffer.reshape(size * a.shape[0], a.shape[1])


def reduce_all(shared, by_core, by_quad, first_beside, beside):
    c, x = lax.axis_index("core"), lax.axis_index("xx")
    unit = lax.axis_size("yy") * lax.axis_size("seq")
    half = halve(pad_rows(shared, 16), "core", c)
    quarter = halve(pad_rows(jnp.concatenate([half, by_core], axis=0), 16), "xx", x)
    last = pad_rows(jnp.concatenate([quarter, by_quad], axis=0), 8 * unit)
    last = spread(spread(last, "yy"), "seq").astype(BF)
    last, first_beside = lax.optimization_barrier((last, first_beside))
    last, beside = lax.optimization_barrier((collect(last, "seq"), beside))
    last = collect(last, "yy")
    joined = join(last[: quarter.shape[0]], "xx", x)
    everywhere = join(joined[: half.shape[0]], "core", c)
    mine = joined[half.shape[0] : half.shape[0] + by_core.shape[0]]
    cores = pair(mine, swap(mine, "core"), c)
    mine = last[quarter.shape[0] : quarter.shape[0] + by_quad.shape[0]]
    both = pair(mine, swap(mine, "xx"), x)
    quads = pair(both, swap(both, "core"), c, axis=1)
    return everywhere, cores, quads, first_beside, beside


def body(
    tokens,
    cotangent,
    attention_base,
    expand_base,
    contract_base,
    attention_down,
    attention_up,
    attention_magnitude,
    expand_down,
    expand_up,
    expand_magnitude,
    contract_down,
    contract_up,
    contract_magnitude,
    prompt_length,
    response_length,
):
    y, x = lax.axis_index("yy"), lax.axis_index("xx")
    c, z = lax.axis_index("core"), lax.axis_index("seq")
    ny, count = lax.axis_size("yy"), lax.axis_size("seq")
    own_rows, local, width = tokens.shape
    rows = 2 * own_rows
    split = count // rows
    piece = local // (2 * split)
    half = count * piece
    blocks = ny * 2
    rank = attention_down.shape[-1]
    unit = attention_base.shape[1]
    hidden_size = expand_base.shape[-1]
    quarter = hidden_size // 4
    place = ((y * 2 + x) * 2 + c) * count + z
    sub = z % split

    def by_core(a):
        shaped = a.reshape(a.shape[:-1] + (blocks, 2, a.shape[-1] // blocks // 2))
        axis = a.ndim
        flat = a.shape[:-1] + (a.shape[-1] // 2,)
        return take(shaped, c, axis).reshape(flat), take(shaped, 1 - c, axis).reshape(flat)

    def by_quarter(a):
        shaped = a.reshape(a.shape[:-1] + (4, quarter))
        return take(shaped, 2 * x + c, a.ndim - 1)

    down_rows = lax.dynamic_slice_in_dim(attention_down, place * unit, unit, 1)
    attention = merged(attention_base, down_rows, attention_up)
    mine, other = by_core(attention[:3])
    mine = mine.transpose(1, 0, 2).reshape(unit, -1)
    other = other.transpose(1, 0, 2).reshape(unit, -1)
    qkv_piece = pair(mine, swap(other, "core"), c)
    out_halves = jnp.stack([attention[3][:, : width // 2], attention[3][:, width // 2 :]])
    attention_piece = jnp.concatenate([qkv_piece, out_halves], axis=2)
    (
        attention_piece, tokens, cotangent, expand_base, contract_base, attention_down, attention_up,
        attention_magnitude, expand_down, expand_up, expand_magnitude, contract_down, contract_up, contract_magnitude,
        prompt_length, response_length,
    ) = lax.optimization_barrier((
        attention_piece, tokens, cotangent, expand_base, contract_base, attention_down, attention_up,
        attention_magnitude, expand_down, expand_up, expand_magnitude, contract_down, contract_up, contract_magnitude,
        prompt_length, response_length,
    ))

    def relayout_start(a):
        shaped = a.reshape(own_rows, split, 2, piece, width)
        kept, sent = take(shaped, c, 2), take(shaped, 1 - c, 2)
        return pair(kept, swap(sent, "core"), c).reshape(count, piece, width)

    contract_columns = lax.dynamic_slice_in_dim(contract_up, place * unit, unit, 1)
    prepare = lambda core: feed_prepare(
        core, place, expand_base, contract_base, expand_down, expand_up, contract_down, contract_columns
    )
    feed_other, square_other = prepare(1 - c)
    feed_mine, square_mine = prepare(c)
    feed_other = swap(feed_other, "core")
    feed_near = pair(take(feed_mine, x, 0), take(feed_other, x, 0), c)
    feed_far = pair(take(feed_mine, 1 - x, 0), take(feed_other, 1 - x, 0), c)

    boxes = {
        "a0": Box(attention_piece),
        "m0": Box(feed_near),
        "feed": Box(feed_far),
        "rows": Box(jnp.concatenate([relayout_start(tokens), relayout_start(cotangent)], axis=1)),
    }
    inside = width // 2

    def qkv_place(turn, column, step):
        def of(block):
            part = block[..., : 3 * inside].reshape(1, 1, 2, 1, unit, 3 * inside)
            return part, [(y - turn) % ny, column, 0, (z - step) % count, 0, 0]

        return of

    def out_place(turn, column, step):
        def of(block):
            part = block[..., 3 * inside :].reshape(2, 1, 1, 1, unit, inside)
            return part, [0, (y - turn) % ny, column, (z - step) % count, 0, 0]

        return of

    def feed_place(turn, index, step):
        def of(block):
            return block.reshape(1, 1, 2, 1, unit, 3 * quarter), [(y - turn) % ny, index, 0, (z - step) % count, 0, 0]

        return of

    qkv_places, out_places, feed_places = {}, {}, {}
    for step in range(count):
        for turn in range(ny):
            tail = f"{step}y{turn}" if turn else f"{step}"
            for name, column in (("a" + tail, x), ("a" + tail + "x", 1 - x)):
                qkv_places[name] = qkv_place(turn, column, step)
                out_places[name] = out_place(turn, column, step)
            for index, side in ((x, "m"), (1 - x, "n")):
                feed_places[side + tail] = feed_place(turn, index, step)
    buffers = {
        "qkv": Buffer((ny, 2, 2, count, unit, 3 * inside), 4, qkv_places),
        "out": Buffer((2, ny, 2, count, unit, inside), 4, out_places),
        "feed": Buffer((ny, 2, 2, count, unit, 3 * quarter), 0, feed_places),
    }
    for name in ("qkv", "out"):
        buffers[name].put("a0", attention_piece)
    buffers["feed"].put("m0", feed_near)
    links = Links(2, boxes, buffers)
    cross_x = lambda a: swap(a, "xx")
    ring = lambda a: shift(a, "seq", 1)
    exchange = lambda a: lax.all_to_all(a, "seq", 0, 0, tiled=True)
    turns = range(1, ny)

    def moves_y(kind, step):
        return [(f"{kind}{step}", f"{kind}{step}y{turn}", functools.partial(shift, name="yy", step=turn)) for turn in turns]

    sides = "mn"
    back = lambda a: shift(a, "seq", -1)
    order = []
    for step in range(1, count):
        order.append((step - 1, step, ring))
    attention_z = [(f"a{source}", f"a{step}", move) for source, step, move in order]
    feed_z = [(f"{side}{source}", f"{side}{step}", move) for source, step, move in order for side in sides]
    z_queue = attention_z[:2] + [("rows", "rows_moved", exchange)] + attention_z[2:] + feed_z
    boxes["s0"] = Box((square_other + square_mine).sum(axis=0))
    small_queue = [(f"s{step - 1}", f"s{step}", ring) for step in range(1, count)]

    def by_seq(*pieces):
        buffer = jnp.zeros((count, unit), F32)
        for step, one in enumerate(pieces):
            buffer = lax.dynamic_update_slice_in_dim(buffer, one, (z - step) % count, 0)
        return buffer

    def in_order(index):
        return lambda mine, other: pair(mine, other, index).reshape(2 * mine.shape[0], unit)

    def by_yy(*pieces):
        buffer = jnp.zeros((ny,) + pieces[0].shape, F32)
        for step, one in enumerate(pieces):
            buffer = put(buffer, one, (y - step) % ny, 0)
        return buffer

    links.derived.append(("sz", [f"s{step}" for step in range(count)], by_seq))
    small_queue.append(("sz", "szc", lambda a: swap(a, "core")))
    links.derived.append(("sc", ["sz", "szc"], in_order(c)))
    small_queue.append(("sc", "scx", cross_x))
    links.derived.append(("sx", ["sc", "scx"], in_order(x)))
    small_queue += moves_y("s", "x")
    links.derived.append(("square", ["sx"] + [f"sxy{turn}" for turn in turns], by_yy))
    x_queue = [("a0", "a0x", cross_x)]
    y_queue = []
    steps = [0] + [step for _, step, _ in order]
    feed_moves = [move for step in steps for side in sides for move in moves_y(side, step)]
    for place_of, step in enumerate(steps):
        names = [f"a{step}"] + [f"a{step}y{turn}" for turn in turns]
        x_queue += [(name, name + "x", cross_x) for name in names if name != "a0"]
        if step == 0:
            x_queue.append(("feed", "n0", cross_x))
        y_queue += moves_y("a", step)
        if place_of >= 1:
            y_queue += feed_moves[:1]
            del feed_moves[:1]
    y_queue += feed_moves

    links.run([z_queue, x_queue, y_queue, small_queue])
    links.place(len(links.rounds) - 2)
    while qkv_places:
        links.place(links.placed + 1)
    qkv_weight = buffers["qkv"].array.reshape(width, 3 * inside)
    out_weight = buffers["out"].array.reshape(2, inside, inside)
    rows_moved = boxes["rows_moved"].array
    tokens_own = rows_moved[:, :piece].reshape(half, width)
    tokens_both = jnp.concatenate([tokens_own, swap(tokens_own, "core")], axis=0)
    def positions_of(sub_place, core_place):
        source = jnp.arange(count, dtype=jnp.int32)[:, None] * local
        inner = sub_place * 2 * piece + core_place * piece + jnp.arange(piece, dtype=jnp.int32)[None]
        return (source + inner).reshape(half)

    query_place = jnp.concatenate([positions_of(sub, c), positions_of(sub, 1 - c)])
    key_place = jnp.concatenate(
        [positions_of((sub - step) % split, side) for step in range(split) for side in (c, 1 - c)]
    )
    totals = (prompt_length + response_length).astype(F32)
    total = take(pair(totals, swap(totals, "core"), c).reshape(rows), z // split, 0).astype(jnp.int32)
    allowed = (key_place[None] <= query_place[:, None]) & (key_place[None] < total)
    bias = jnp.where(allowed, 0.0, -1e30).astype(F32)
    frequency = 10000.0 ** (-jnp.arange(HEAD_DIM // 2).astype(F32) / (HEAD_DIM // 2))
    angles = query_place.astype(F32)[:, None] * frequency[None]
    cosine = jnp.concatenate([jnp.cos(angles)] * 2, axis=1)
    sine = jnp.concatenate([-jnp.sin(angles), jnp.sin(angles)], axis=1)

    heads = width // 2 // HEAD_DIM
    rows_both = tokens_both.astype(F32)
    first = rms(rows_both).astype(BF)
    magnitude = by_core(attention_magnitude[:3])[0].reshape(1, -1)
    downs = attention_down[:3].transpose(0, 2, 1).reshape(3 * rank, width).astype(BF)
    qkv_t, qkv_p, qkv_norm, cross = qkv_forward(first, qkv_weight, downs, magnitude, cosine, sine)

    def share(a, step):
        perm = [(i, (i // split) * split + (i % split + step) % split) for i in range(count)]
        return lax.ppermute(a, "seq", perm)

    feed_buffer = buffers["feed"]
    if split == 1:
        kv, offsets = qkv_p, (heads, 2 * heads)
    else:
        own_kv = qkv_p[:, heads * HEAD_DIM :]
        kv = jnp.concatenate([own_kv] + [share(own_kv, step) for step in range(1, split)], axis=0)
        offsets = (0, heads)
    (mixed,) = attention_call(
        attend_kernel, "attend", heads, qkv_p, kv, offsets, [], bias, [(2 * half, BF)]
    )

    def core_scatter(partial):
        return partial[:half].astype(F32) + swap(partial[half:].astype(BF), "core").astype(F32)

    def core_join(own):
        return jnp.concatenate([own, swap(own, "core")], axis=0)

    out_rows = by_core(attention_down[3].T)[0].astype(BF)
    contract_square = boxes["square"].array.reshape(1, width)
    qkv_p, cotangent_own = lax.optimization_barrier((qkv_p, rows_moved[:, piece:]))
    cotangent_own = cotangent_own.reshape(half, width)
    cotangent_far = swap(cotangent_own, "xx")
    mixed, cotangent_far, out_weight = lax.optimization_barrier((mixed, cotangent_far, out_weight))
    links.place(len(links.rounds))
    feed_weight = feed_buffer.array.reshape(width, 3 * quarter)
    out_square = jnp.sum(out_weight.astype(F32) ** 2, axis=1).reshape(1, width)
    out_norm = jnp.sqrt(out_square + swap(out_square, "core"))
    out_scale = attention_magnitude[3:] / out_norm
    out_sent = [mm(mixed[half:], out_weight[i]).astype(BF) for i in range(2)]
    out_sent = swap(jnp.concatenate(out_sent, axis=1), "core").astype(F32)
    out_t = jnp.concatenate([mm(mixed[:half], out_weight[i]) for i in range(2)], axis=1) + out_sent
    rows_own = tokens_own.astype(F32)
    middle = rows_own + out_t * out_scale
    second_own = rms(middle).astype(BF)
    second_far = swap(second_own, "xx")
    second_near = (second_own, swap(second_own, "core"))
    second_far = (second_far, swap(second_far, "core"))
    low = nt(downs, first).astype(BF).reshape(3, rank, 2 * half)
    cross = jnp.stack(
        [cross[i * rank : (i + 1) * rank, i * width // 2 : (i + 1) * width // 2] for i in range(3)]
    )
    core_up = by_core(attention_up[:3])[0]
    second_far, cross, low, core_up = lax.optimization_barrier((second_far, cross, low, core_up))

    gate_up = jnp.stack([by_quarter(expand_up[i]) for i in range(2)])
    feed_downs = expand_down.transpose(0, 2, 1).reshape(2 * rank, width).astype(BF)
    contract_rows = take(contract_down.T.reshape(rank, 4, quarter), 2 * x + c, 1).astype(BF)
    contract_ups = contract_up.astype(BF)
    expand_magnitudes = by_quarter(expand_magnitude).reshape(1, -1)
    grad_own = cotangent_own.astype(F32)
    cotangent_near = (cotangent_own, swap(cotangent_own, "core"))
    cotangent_far = (cotangent_far, swap(cotangent_far, "core"))
    contract_norm = jnp.sqrt(contract_square)
    contract_scale = contract_magnitude[None] / contract_norm
    def total(kept, sent):
        return kept.astype(F32) + swap(sent, "core").astype(F32)

    (
        back_far, back_sent, out_far, out_sent, shared_far, quads_far, dm_far, expand_norm, expand_cross, contract_cross
    ) = feed_forward_back(
        *second_far, *cotangent_far, feed_weight, expand_magnitudes, None, contract_scale,
        feed_downs, gate_up, contract_rows, contract_ups,
    )
    back_far = total(back_far, back_sent).astype(BF)
    second_near, back_far = lax.optimization_barrier((second_near, back_far))
    back_near, back_sent, out_near, out_near_sent, shared_near, quads_near, dm_near = feed_forward_back(
        *second_near, *cotangent_near, feed_weight, expand_magnitudes, expand_norm, contract_scale,
        feed_downs, gate_up, contract_rows, contract_ups,
    )[:7]
    back_near, back_sent, back_far = lax.optimization_barrier((back_near, back_sent, swap(back_far, "xx")))
    middle_grad, out_dt_own, out_dm = middle_back(
        back_near, swap(back_sent, "core"), back_far, cotangent_own, middle, out_t, out_scale, out_norm
    )

    out_dt = core_join(out_dt_own)
    mixed_grad = sum(nt(out_dt[:, i * inside : (i + 1) * inside], out_weight[i]) for i in range(2)).astype(BF)
    out_far, back_far = lax.optimization_barrier((total(out_far, out_sent).astype(BF), back_far))
    out_far = swap(out_far, "xx")
    keys = 2 * half * split
    members = lambda a: a.reshape(3, 1, width // 2)
    qkv_scale = magnitude / qkv_norm

    def reunite(a):
        parts = a.reshape(split, 2 * half, -1)
        total = parts[0]
        for step in range(1, split):
            total = total + share(parts[step].astype(BF), -step).astype(F32)
        return total

    if split > 1:
        dq, dk, dv = attention_call(
            attend_back_kernel, "attend_back", heads, qkv_p, kv, offsets, [mixed_grad], bias,
            [(2 * half, F32), (keys, F32), (keys, F32)],
        )
        grads = jnp.concatenate([dq, reunite(dk), reunite(dv)], axis=1)
        qkv_dt, qkv_dm = turn_back(grads, qkv_t, qkv_scale, 1.0 / qkv_norm, cosine, sine)
        qkv_dm = members(qkv_dm)
    else:
        qkv_dt, qkv_dm = attend_back_turn(
            heads, qkv_p, mixed_grad, bias, qkv_t, members(qkv_scale), members(1.0 / qkv_norm), cosine, sine
        )
    def restore_start(own):
        return lax.all_to_all(own.reshape(count, piece, width), "seq", 0, 0, tiled=True)

    qkv_dt, out_far, out_near, out_near_sent = lax.optimization_barrier((qkv_dt, out_far, out_near, out_near_sent))
    contract_t = total(out_near, out_near_sent) + out_far.astype(F32)
    output_own = (middle + contract_t * contract_scale).astype(BF)
    layer_moved = restore_start(output_own)
    first_part, qkv_shared, qkv_core = qkv_back(
        qkv_dt, qkv_weight, first, low, core_up, cross, members(qkv_scale), members(qkv_norm), qkv_dm
    )
    first_grad = core_scatter(first_part)
    tokens_grad_own = middle_grad + rms_back(rows_own, first_grad)

    def restore_end(moved):
        shaped = moved.reshape(2, own_rows, split, piece, width)
        kept, sent = take(shaped, c, 0), take(shaped, 1 - c, 0)
        return pair(kept, swap(sent, "core"), c, axis=2).reshape(own_rows, local, width)

    expand_sum = dm_near + dm_far
    expand_pull = -expand_magnitudes * expand_sum / (expand_norm * expand_norm * expand_norm)
    contract_dm = jnp.sum(grad_own * contract_t, axis=0, keepdims=True) / contract_norm
    contract_sum = contract_dm + swap(contract_dm, "core")
    contract_sum = contract_sum + swap(contract_sum, "xx")
    contract_pull = -contract_scale * contract_sum / contract_norm
    feed_words, feed_quad_words = feed_adapter(
        shared_far, shared_near, quads_far, quads_near, expand_cross, contract_cross, gate_up, contract_ups,
        feed_weight, expand_pull, expand_sum / expand_norm, contract_pull, contract_dm,
    )
    flat = lambda a: a.reshape(-1, WORD)

    out_words, out_core_words = out_adapter(
        out_dt, out_weight, mixed, out_rows, attention_up[3], out_scale, out_norm,
        out_dm + swap(out_dm, "core"), out_dm,
    )
    dm_words = jnp.pad(qkv_dm[:, 0], ((0, 5), (0, 0)))
    dm_words = jnp.stack([dm_words[:, i : i + WORD] for i in range(0, width // 2, WORD)])
    shared = jnp.concatenate([flat(qkv_shared), flat(out_words), flat(feed_words)])
    cores = jnp.concatenate([flat(qkv_core), flat(dm_words), flat(out_core_words)])
    attention_shared, attention_cores, feed_quads, layer_moved, tokens_moved = reduce_all(
        shared, cores, flat(feed_quad_words), layer_moved, tokens_grad_own.astype(BF)
    )
    tokens_moved = restore_start(tokens_moved)
    used = flat(qkv_shared).shape[0] + flat(out_words).shape[0]
    feed_shared = attention_shared[used:]

    def interleave(parts):
        shaped = [p.reshape(p.shape[0], blocks, 1, -1) for p in parts]
        return jnp.concatenate(shaped, axis=2).reshape(parts[0].shape[0], -1)

    used = flat(qkv_shared).shape[0]
    qkv_down_all = unpacked(attention_shared[:used].reshape(qkv_shared.shape), width)
    out_all = unpacked(attention_shared[used : used + flat(out_words).shape[0]].reshape(out_words.shape), width)
    core_parts = []
    for side in range(2):
        start, parts = 0, []
        for words in (qkv_core, dm_words, out_core_words):
            used = flat(words).shape[0]
            parts.append(unpacked(attention_cores[side, start : start + used].reshape(words.shape), width // 2))
            start += used
        core_parts.append(parts)
    qkv_up_all, qkv_dm_all, out_down_all = (interleave([core_parts[0][i], core_parts[1][i]]) for i in range(3))
    attention_down_grad = (
        jnp.concatenate([qkv_down_all, out_down_all]).reshape(4, rank, width).transpose(0, 2, 1)
    )
    attention_up_grad = jnp.concatenate([qkv_up_all, out_all[:rank]]).reshape(4, rank, width)
    attention_magnitude_grad = jnp.concatenate([qkv_dm_all[:3], out_all[rank : rank + 1]])

    feed_all = unpacked(feed_shared[: flat(feed_words).shape[0]].reshape(feed_words.shape), width)
    quad_all = jnp.concatenate(
        [unpacked(feed_quads[i, j].reshape(feed_quad_words.shape), quarter) for i in range(2) for j in range(2)],
        axis=1,
    )

    layer_output = restore_end(layer_moved)
    tokens_grad = restore_end(tokens_moved).astype(F32)
    return (
        layer_output,
        tokens_grad,
        attention_down_grad.astype(F32),
        attention_up_grad.astype(F32),
        attention_magnitude_grad.astype(F32),
        feed_all[: 2 * rank].reshape(2, rank, width).transpose(0, 2, 1).astype(F32),
        quad_all[: 2 * rank].reshape(2, rank, hidden_size).astype(F32),
        quad_all[3 * rank : 3 * rank + 2].astype(F32),
        quad_all[2 * rank : 3 * rank].T.astype(F32),
        feed_all[2 * rank : 3 * rank].astype(F32),
        feed_all[3 * rank].astype(F32),
    )


def solution(mesh):
    devices = mesh.devices
    chips = devices.shape[0] // 2
    fine = Mesh(devices.reshape(chips // 2, 2, 2, devices.shape[1]), ALL)
    dp = ("yy", "xx", "core")
    every = ("yy", "xx", "core", "seq")
    placed = (
        P(dp, "seq", None),
        P(dp, "seq", None),
        P(None, every, None),
        P(None, every, None),
        P(None, every),
        P(),
        P(),
        P(),
        P(),
        P(),
        P(),
        P(),
        P(),
        P(),
        P(dp),
        P(dp),
    )
    return jax.shard_map(
        body,
        mesh=fine,
        in_specs=placed,
        out_specs=(P(dp, "seq", None), P(dp, "seq", None)) + (P(),) * 9,
        check_vma=False,
    )
```
